1024 devices in a mesh: gx: 16 (over x, core), gy: 64 (over y, z).
Axes of the slice: x: 8, y: 8, z: 8, core: 2. Of those that a mesh axis runs over, the one named last changes fastest.
Arguments:
- solution: float32 [128, 512, 512], P('gx', 'gy'), may hold values from -6 to 6
- right_side: float32 [128, 512, 512], P('gx', 'gy'), may hold values from -6 to 6
- alpha: bfloat16 [128, 512, 512], P('gx', 'gy'), may hold values from 0.5 to 2
- beta_x: bfloat16 [128, 512, 512], P('gx', 'gy'), may hold values from 0.25 to 2.5
- beta_y: bfloat16 [128, 512, 512], P('gx', 'gy'), may hold values from 0.25 to 2.5
- beta_z: bfloat16 [128, 512, 512], P('gx', 'gy'), may hold values from 0.25 to 2.5
Outputs:
- fine_iterate: float32 [128, 512, 512], P('gx', 'gy')
- middle_iterate: float32 [64, 256, 256], P('gx', 'gy')
- coarse_iterate: float32 [32, 128, 128], P('gx', 'gy')
The draws below stay inside these ranges and needn't reach their ends.
All inputs are finite; a program needn't handle non-finite values.
Results may differ from the reference program's by a relative error of at most 0.0003.
Values sent between devices are 32-bit elements; how exact they have to be, the bound alone decides.
No kernel may reach another device: no remote copies, remote signals or barrier semaphores. Data moves between devices by JAX's collectives and lax.ppermute only.
A program may use at most 64 MiB of HBM per device.

```python
import math
import jax
import jax.numpy as jnp
from jax import lax

LEVELS = 3
SWEEPS = 2
NX = 128
NY = 512
NZ = 512


def shard_levels(own_key, dims, pieces, least, top_value):
    factor_of, own = 1.0, jax.random.fold_in(own_key, 6)
    for dim, blocks in pieces:
        draws = jnp.exp(jax.random.uniform(jax.random.fold_in(own, dim), (blocks,), jnp.float32, least / len(pieces), top_value / len(pieces)))
        factor_of = factor_of * jnp.repeat(draws, dims[dim] // blocks).reshape([-1 if axis == dim else 1 for axis in range(len(dims))])
    return factor_of


def bell_draw(stream_key, dims, deviation, reach, split=(), held_as=jnp.bfloat16):
    entries = jax.random.normal(stream_key, dims, jnp.float32) * deviation
    if len(split) > 0:
        entries = shard_levels(stream_key, dims, split, -0.22, 0.18) * entries
    return jnp.clip(entries, min=-reach, max=reach).astype(held_as)


def setup_inputs(seed: int = 0) -> dict:
    key_of = jax.random.split(jax.random.key(seed), 7)
    return {
        "solution": bell_draw(key_of[0], (NX, NY, NZ), 1.0, 6.0, ((0, 16), (1, 64)), jnp.float32),
        "right_side": bell_draw(key_of[1], (NX, NY, NZ), 1.0, 6.0, ((0, 16), (1, 64)), jnp.float32),
        "alpha": jnp.clip(0.5 + 1.5 * jax.random.uniform(key_of[2], (NX, NY, NZ), jnp.float32) ** shard_levels(key_of[2], (NX, NY, NZ), ((0, 16), (1, 64)), -0.2, 0.2), 0.5, 2.0).astype(jnp.bfloat16),
        "beta_x": jnp.clip(jnp.exp(math.log(2.5) - 2.3025851 * jax.random.uniform(key_of[3], (NX, NY, NZ), jnp.float32) ** shard_levels(key_of[3], (NX, NY, NZ), ((0, 16), (1, 64)), -0.2, 0.2)), 0.25, 2.5).astype(jnp.bfloat16),
        "beta_y": jnp.clip(jnp.exp(math.log(2.5) - 2.3025851 * jax.random.uniform(key_of[4], (NX, NY, NZ), jnp.float32) ** shard_levels(key_of[4], (NX, NY, NZ), ((0, 16), (1, 64)), -0.2, 0.2)), 0.25, 2.5).astype(jnp.bfloat16),
        "beta_z": jnp.clip(jnp.exp(math.log(2.5) - 2.3025851 * jax.random.uniform(key_of[5], (NX, NY, NZ), jnp.float32) ** shard_levels(key_of[5], (NX, NY, NZ), ((0, 16), (1, 64)), -0.2, 0.2)), 0.25, 2.5).astype(jnp.bfloat16),
    }


def shift_up(field, axis):
    size = field.shape[axis]
    rest = lax.slice_in_dim(field, 1, size, axis=axis)
    edge = jnp.zeros_like(lax.slice_in_dim(field, 0, 1, axis=axis))
    return jnp.concatenate([rest, edge], axis=axis)


def shift_down(field, axis):
    size = field.shape[axis]
    rest = lax.slice_in_dim(field, 0, size - 1, axis=axis)
    edge = jnp.zeros_like(lax.slice_in_dim(field, 0, 1, axis=axis))
    return jnp.concatenate([edge, rest], axis=axis)


def stencil(field, beside, coefs, scale):
    out = coefs[0] * field
    for direc in range(3):
        upper_face = coefs[1 + 2 * direc]
        lower_face = coefs[2 + 2 * direc]
        out = out + scale * (upper_face * (field - beside[2 * direc]) + lower_face * (field - beside[2 * direc + 1]))
    return out


def diagonal_of(coefs, scale):
    return coefs[0] + scale * ((coefs[1] + coefs[2]) + (coefs[3] + coefs[4]) + (coefs[5] + coefs[6]))


def parity_of(shape):
    total = lax.broadcasted_iota(jnp.int32, shape, 0) + lax.broadcasted_iota(jnp.int32, shape, 1) + lax.broadcasted_iota(jnp.int32, shape, 2)
    return total % 2


def all_beside(field):
    return (shift_up(field, 0), shift_down(field, 0), shift_up(field, 1), shift_down(field, 1), shift_up(field, 2), shift_down(field, 2))


def coarsen_cells(field):
    nx, ny, nz = field.shape
    return field.reshape(nx // 2, 2, ny // 2, 2, nz // 2, 2).mean(axis=(1, 3, 5))


def coarsen_faces(bx, by, bz):
    nx, ny, nz = bx.shape
    cx = bx[1::2].reshape(nx // 2, ny // 2, 2, nz // 2, 2).mean(axis=(2, 4))
    cy = by[:, 1::2].reshape(nx // 2, 2, ny // 2, nz // 2, 2).mean(axis=(1, 4))
    cz = bz[:, :, 1::2].reshape(nx // 2, 2, ny // 2, 2, nz // 2).mean(axis=(1, 3))
    return cx, cy, cz


def reference(solution, right_side, alpha, beta_x, beta_y, beta_z):
    iterate = solution
    source = right_side
    cell_coef = alpha.astype(jnp.float32)
    face_x = beta_x.astype(jnp.float32)
    face_y = beta_y.astype(jnp.float32)
    face_z = beta_z.astype(jnp.float32)
    results = []
    for level in range(LEVELS):
        scale = 0.25 ** level
        coefs = (cell_coef, face_x, shift_down(face_x, 0), face_y, shift_down(face_y, 1), face_z, shift_down(face_z, 2))
        diag = diagonal_of(coefs, scale)
        parity = parity_of(iterate.shape)
        for sweep in range(SWEEPS):
            for colour in (0, 1):
                resid = source - stencil(iterate, all_beside(iterate), coefs, scale)
                iterate = jnp.where(parity == colour, iterate + resid / diag, iterate)
        results.append(iterate)
        if level + 1 < LEVELS:
            resid = source - stencil(iterate, all_beside(iterate), coefs, scale)
            source = coarsen_cells(resid)
            cell_coef = coarsen_cells(cell_coef)
            face_x, face_y, face_z = coarsen_faces(face_x, face_y, face_z)
            iterate = jnp.zeros_like(source)
    return (results[0], results[1], results[2])
```

```python
import jax
import jax.numpy as jnp
from jax import lax
from jax.experimental import pallas as pl
from jax.experimental.pallas import tpu as pltpu
from jax.sharding import PartitionSpec as P

F32 = jnp.float32
BF16 = jnp.bfloat16

U, F, A, BX, BY, BZ = range(6)
PAIRS = ((U, F), (A, BY), (BX, BZ))
H = 4


def iota(shape, dim):
    return lax.broadcasted_iota(jnp.int32, shape, dim)


def call(body, outs, args, scratch=(), flops=1_000_000, nbytes=2_000_000):
    vmem = pl.BlockSpec(memory_space=pltpu.VMEM)
    return pl.pallas_call(
        body,
        out_shape=outs,
        in_specs=[vmem] * len(args),
        out_specs=jax.tree.map(lambda _: vmem, outs),
        scratch_shapes=list(scratch),
        compiler_params=pltpu.CompilerParams(vmem_limit_bytes=48 << 20),
        cost_estimate=pl.CostEstimate(flops=flops, bytes_accessed=nbytes, transcendentals=0),
    )(*args)


def pair_low(first, second):
    return jnp.where(iota(first.shape, 0) < 4, first, pltpu.roll(second, 4, 0))


def pair_high(first, second):
    return jnp.where(iota(first.shape, 0) >= 4, first, pltpu.roll(second, 4, 0))


def pack_body(u, f, a, bx, by, bz, xl, xh, yl, yh):
    fields = (u, f, a, bx, by, bz)
    cut = bx[3].astype(F32)
    for k, ref in enumerate(fields):
        for j in range(H):
            low, high = ref[j].astype(F32), ref[4 + j].astype(F32)
            if j == 3:
                if k == F:
                    low = low + cut * u[4]
                elif k == A:
                    low = low + cut
                elif k == BX:
                    low = jnp.zeros_like(low)
            if j == 0:
                if k == F:
                    high = high + cut * u[3]
                elif k == A:
                    high = high + cut
            xl[k * H + j] = low
            xh[k * H + j] = high
    row = iota(u.shape[1:], 0)
    for p in range(u.shape[0]):
        v = [ref[p].astype(F32) for ref in fields]
        face = v[BY]
        low = list(v)
        low[F] = v[F] + jnp.where(row == 3, face * pltpu.roll(v[U], 7, 0), 0.0)
        low[A] = v[A] + jnp.where(row == 3, face, 0.0)
        low[BY] = jnp.where(row == 3, 0.0, face)
        high = list(v)
        below = pltpu.roll(face, 1, 0)
        high[F] = v[F] + jnp.where(row == 4, below * pltpu.roll(v[U], 1, 0), 0.0)
        high[A] = v[A] + jnp.where(row == 4, below, 0.0)
        for n, (i, j) in enumerate(PAIRS):
            yl[n * 8 + p] = pair_low(low[i], low[j])
            yh[n * 8 + p] = pair_high(high[i], high[j])


def corner_body(xlr, xhr, ycl, ych):
    for p in range(8):
        v = [xhr[k * H + p] if p < 4 else xlr[k * H + p - 4] for k in range(6)]
        for n, (i, j) in enumerate(PAIRS):
            ycl[n * 8 + p] = pair_low(v[i], v[j])
            ych[n * 8 + p] = pair_high(v[i], v[j])


def halves(n):
    row, col = iota((n, n // 2), 0), iota((n, n // 2), 1)
    both = jnp.where(row // 2 == col, 1.0, 0.0).astype(BF16)
    odd = jnp.where(row == 2 * col + 1, 1.0, 0.0).astype(BF16)
    return both, odd


def exact_dot(x, m):
    n = x.shape[0]
    one = x.astype(BF16)
    rest = x - one.astype(F32)
    two = rest.astype(BF16)
    three = (rest - two.astype(F32)).astype(BF16)
    y = jnp.dot(
        jnp.concatenate([one.astype(F32), two.astype(F32), three.astype(F32)], axis=0).astype(BF16),
        m,
        preferred_element_type=F32,
    )
    return (y[2 * n :] + y[n : 2 * n]) + y[:n]


def put(ref, at, x):
    for g in range(x.shape[1] // 128):
        ref[g, at : at + x.shape[0]] = x[:, 128 * g : 128 * g + 128]


def every_other(ref, first, n, width):
    return jnp.concatenate([ref[g, pl.ds(first, n, 2)] for g in range(width // 128)], axis=1)


def below_z(face):
    return jnp.where(iota(face.shape, face.ndim - 1) == 0, 0.0, pltpu.roll(face, 1, face.ndim - 1))


def coarse_body(a, bx, by, bz, xhr, yhr, c1, c2, rows, edge, fine, small):
    nz = a.shape[2]
    both, odd = halves(nz)
    both2, odd2 = halves(nz // 2)

    def even_odd(n):
        return every_other(rows, 0, n, nz), every_other(rows, 1, n, nz)

    def pairs(ref):
        for i in range(4):
            put(rows, 8 * i, ref[2 * i].astype(F32) + ref[2 * i + 1].astype(F32))
        return even_odd(16)

    e, o = pairs(a)
    a_in = e + o
    e, o = pairs(bz)
    bz_in = e + o
    e, o = pairs(by)
    by_in = o
    for i in range(4):
        put(rows, 8 * i, bx[2 * i + 1].astype(F32))
    e, o = even_odd(16)
    bx_in = e + o
    put(rows, 0, xhr[BX * H + 3])
    e, o = even_odd(4)
    edge[0:4] = e + o
    for i in range(4):
        edge[4 + i : 5 + i] = yhr[8 + 2 * i, 3:4] + yhr[8 + 2 * i + 1, 3:4]
    out = exact_dot(jnp.concatenate([a_in, bx_in, by_in, edge[...]], axis=0), both)
    a1, bx1, by1, edges = out[0:16] * 0.125, out[16:32] * 0.25, out[32:48] * 0.25, out[48:56] * 0.25
    bz1 = exact_dot(bz_in, odd) * 0.25
    c1[1] = bx1
    c1[2] = by1
    c1[3] = bz1
    fine[0, 0:8] = edges
    fine[1, 0:4] = edges[0:4]
    fine[1, 4:20] = bx1
    lower_x = fine[1, 0:16]
    fine[2, 1:17] = by1
    lower_y = fine[2, 0:16]
    for i in range(4):
        fine[3, 4 * i : 4 * i + 4] = jnp.broadcast_to(fine[0, 4 + i : 5 + i], (4, nz // 2))
    lower_y = jnp.where(iota(lower_y.shape, 0) % 4 == 0, fine[3, 0:16], lower_y)
    c1[0] = a1 + 0.25 * ((bx1 + lower_x) + (by1 + lower_y) + (bz1 + below_z(bz1)))

    def split(x):
        put(rows, 0, x)
        n = x.shape[0] // 2
        return every_other(rows, 0, n, nz // 2), every_other(rows, 1, n, nz // 2)

    def layers(t):
        small[0:8] = t
        top = small[0:2] + small[2:4]
        bottom = small[4:6] + small[6:8]
        return top, bottom

    e, o = split(a1)
    a_t = layers(e + o)
    e, o = split(bz1)
    bz_t = layers(e + o)
    e, o = split(by1)
    by_t = layers(o)
    e, o = split(bx1)
    small[0:8] = e + o
    bx_t = (small[2:4], small[6:8])
    e, o = split(edges)
    small[0:4] = e + o
    small[8:10] = a_t[0]
    small[10:12] = a_t[1]
    small[12:14] = by_t[0]
    small[14:16] = by_t[1]
    small[16:18] = bx_t[0]
    small[18:20] = bx_t[1]
    small[20:24] = small[0:4]
    small[24:26] = bz_t[0]
    small[26:28] = bz_t[1]
    small[28:32] = small[0:4]
    out = exact_dot(small[8:24], both2)
    out_z = exact_dot(small[24:32], odd2)[0:4] * 0.25
    a2, by2, bx2, edges = out[0:4] * 0.125, out[4:8] * 0.25, out[8:12] * 0.25, out[12:16] * 0.25
    w = nz // 4
    c2[4:8] = bx2
    c2[8:12] = by2
    c2[12:16] = out_z
    small[0:2, 0:w] = edges[0:2]
    small[2:6, 0:w] = bx2
    lower_x = small[0:4, 0:w]
    small[8:12, 0:w] = by2
    small[16:20, 0:w] = edges
    small[24:25, 0:w] = small[18:19, 0:w]
    small[25:26, 0:w] = small[8:9, 0:w]
    small[26:27, 0:w] = small[19:20, 0:w]
    small[27:28, 0:w] = small[10:11, 0:w]
    lower_y = small[24:28, 0:w]
    c2[0:4] = a2 + 0.0625 * ((bx2 + lower_x) + (by2 + lower_y) + (out_z + below_z(out_z)))


def set_weights(weights, w, inverse, source, up_x, low_x, up_y, up_z):
    lane = iota(inverse.shape, 1)
    nz = inverse.shape[1]
    weights[0, w] = source * inverse
    weights[1, w] = up_x * inverse
    weights[2, w] = low_x * inverse
    weights[3, w] = up_y * inverse
    weights[4, w] = pltpu.roll(up_y, 1, 0) * inverse
    weights[5, w] = jnp.where(lane == nz - 1, 0.0, up_z) * inverse
    weights[6, w] = jnp.where(lane == 0, 0.0, pltpu.roll(up_z, 1, 1)) * inverse


def relaxed(weights, held, w):
    here = held[w + 1]
    ny, nz = here.shape
    x = weights[1, w] * held[w + 2] + weights[2, w] * held[w]
    y = weights[3, w] * pltpu.roll(here, ny - 1, 0) + weights[4, w] * pltpu.roll(here, 1, 0)
    z = weights[5, w] * pltpu.roll(here, nz - 1, 1) + weights[6, w] * pltpu.roll(here, 1, 1)
    return ((weights[0, w] + x) + (y + z)), here


def smooth(weights, held, reach):
    count = weights.shape[1]
    spare = (weights.shape[2], weights.shape[3])
    parity = (iota(spare, 0) + iota(spare, 1)) % 2
    for step in range(4):

        def one(w, carry, step=step):
            new, here = relaxed(weights, held, w)
            held[w + 1] = jnp.where((parity + w + step) % 2 == 0, new, here)
            return carry

        first = step
        lax.fori_loop(first, count - first, one, 0)


def fine_body(u, f, a, bx, by, bz, xlr, xhr, ylr, yhr, yclr, ychr, c1, out, p1, win, weights, held, diag, rows):
    own = (u, f, a, bx, by, bz)
    nz = u.shape[2]
    upper = iota((8, nz), 0) >= 4

    for w in range(16):
        for n, pair in enumerate(PAIRS):
            if w < 4:
                below, above = ychr[n * 8 + w], yclr[n * 8 + w]
            elif w < 12:
                below, above = yhr[n * 8 + w - 4], ylr[n * 8 + w - 4]
            else:
                below, above = ychr[n * 8 + w - 8], yclr[n * 8 + w - 8]
            for side, k in enumerate(pair):
                if side:
                    below, above = pltpu.roll(below, 4, 0), pltpu.roll(above, 4, 0)
                if w < 4:
                    mid = xhr[k * H + w]
                elif w < 12:
                    mid = own[k][w - 4].astype(F32)
                else:
                    mid = xlr[k * H + w - 12]
                low = jnp.where(upper, below, 0.0)
                high = jnp.where(upper, 0.0, above)
                if k == U:
                    held[w + 1, 0:8] = low
                    held[w + 1, 8:16] = mid
                    held[w + 1, 16:24] = high
                else:
                    win[k - 1, w + 1, 0:8] = low
                    win[k - 1, w + 1, 8:16] = mid
                    win[k - 1, w + 1, 16:24] = high
    zero = jnp.zeros((24, nz), F32)
    held[0] = zero
    held[17] = zero
    win[BX - 1, 0] = zero

    def prepare(w, carry):
        av, bxv, byv, bzv = win[A - 1, w + 1], win[BX - 1, w + 1], win[BY - 1, w + 1], win[BZ - 1, w + 1]
        low_x = win[BX - 1, w]
        total = av + ((bxv + low_x) + (byv + pltpu.roll(byv, 1, 0)) + (bzv + below_z(bzv)))
        inside = av > 0.0
        inverse = jnp.where(inside, 1.0 / jnp.where(inside, total, 1.0), 0.0)
        set_weights(weights, w, inverse, win[F - 1, w + 1], bxv, low_x, byv, bzv)
        diag[w] = total[8:16]
        return carry

    lax.fori_loop(0, 16, prepare, 0)
    smooth(weights, held, H)
    for i in range(4):
        total = None
        for j in range(2):
            w = 4 + 2 * i + j
            new, here = relaxed(weights, held, w)
            out[w - 4] = here[8:16]
            res = diag[w] * (new[8:16] - here[8:16])
            total = res if total is None else total + res
        put(rows, 8 * i, total)
    both, _ = halves(nz)
    p1[0] = exact_dot(every_other(rows, 0, 16, nz) + every_other(rows, 1, 16, nz), both) * 0.125
    for k in range(4):
        p1[1 + k] = c1[k]


def middle_body(below, here, above, c2, out, p2, win, weights, held, rows):
    nz = below.shape[2]
    zero = jnp.zeros((16, nz), F32)
    for k in range(5):
        for w in range(12):
            win[k, w + 1, 0:4] = jnp.zeros((4, nz), F32)
            win[k, w + 1, 4:8] = below[k, 4 * w : 4 * w + 4]
            win[k, w + 1, 8:12] = here[k, 4 * w : 4 * w + 4]
            win[k, w + 1, 12:16] = above[k, 4 * w : 4 * w + 4]
    win[2, 0] = zero

    def prepare(w, carry):
        total = win[1, w + 1]
        inside = total > 0.0
        inverse = jnp.where(inside, 0.25 / jnp.where(inside, total, 1.0), 0.0)
        set_weights(weights, w, inverse, 4.0 * win[0, w + 1], win[2, w + 1], win[2, w], win[3, w + 1], win[4, w + 1])
        held[w + 1] = zero
        return carry

    lax.fori_loop(0, 12, prepare, 0)
    held[0] = zero
    held[13] = zero
    smooth(weights, held, H)
    for i in range(2):
        total = None
        for j in range(2):
            w = 4 + 2 * i + j
            new, now = relaxed(weights, held, w)
            out[w - 4] = now[8:12]
            res = win[1, w + 1, 8:16] * (new[8:16] - now[8:16])
            total = res if total is None else total + res
        put(rows, 8 * i, total)
    both, _ = halves(nz)
    coarse = exact_dot(every_other(rows, 0, 8, nz) + every_other(rows, 1, 8, nz), both) * 0.125
    p2[0:2] = coarse[0:2]
    p2[2:4] = coarse[4:6]
    p2[4:20] = c2[...]


def coarse_level_body(left, right, down, up, below, here, above, out, win, weights, held):
    nz = left.shape[1]
    win[...] = jnp.zeros(win.shape, F32)
    for k in range(5):
        win[k, 1, 3:5] = left[4 * k + 2 : 4 * k + 4]
        win[k, 8, 3:5] = right[4 * k : 4 * k + 2]
        for i in range(2):
            at = 4 * k + 2 * i
            win[k, 4 + i, 0:1] = down[at + 1 : at + 2]
            win[k, 4 + i, 7:8] = up[at : at + 1]
            for b in range(3):
                win[k, 2 + 2 * b + i, 1:3] = below[b, at : at + 2]
                win[k, 2 + 2 * b + i, 3:5] = here[b, at : at + 2]
                win[k, 2 + 2 * b + i, 5:7] = above[b, at : at + 2]
    held[...] = jnp.zeros(held.shape, F32)
    for w in range(8):
        total = win[1, w + 1]
        inside = total > 0.0
        inverse = jnp.where(inside, 0.0625 / jnp.where(inside, total, 1.0), 0.0)
        set_weights(weights, w, inverse, 16.0 * win[0, w + 1], win[2, w + 1], win[2, w], win[3, w + 1], win[4, w + 1])
    smooth(weights, held, 3)
    for i in range(2):
        out[i] = held[4 + i, 3:5]


def moved(block, axis, by):
    count = lax.axis_size(axis)
    return lax.ppermute(block, axis, [(i, i + by) for i in range(count) if 0 <= i + by < count])


def shape(*dims):
    return jax.ShapeDtypeStruct(dims, F32)


def shards(solution, right_side, alpha, beta_x, beta_y, beta_z):
    own = (solution, right_side, alpha, beta_x, beta_y, beta_z)
    nz = solution.shape[2]
    sent = shape(24, 8, nz)
    xl, xh, yl, yh = call(pack_body, (sent,) * 4, own)
    xlr, xhr = moved(xl, "gx", -1), moved(xh, "gx", 1)
    ylr, yhr = moved(yl, "gy", -1), moved(yh, "gy", 1)
    ycl, ych = call(corner_body, (sent,) * 2, (xlr, xhr))
    yclr, ychr = moved(ycl, "gy", -1), moved(ych, "gy", 1)
    c1, c2 = call(
        coarse_body,
        (shape(4, 16, nz // 2), shape(16, nz // 4)),
        (alpha, beta_x, beta_y, beta_z, xhr, yhr),
        [
            pltpu.VMEM((nz // 128, 32, 128), F32),
            pltpu.VMEM((8, nz), F32),
            pltpu.VMEM((4, 24, nz // 2), F32),
            pltpu.VMEM((32, nz // 2), F32),
        ],
    )
    fine, p1 = call(
        fine_body,
        (shape(8, 8, nz), shape(5, 16, nz // 2)),
        (*own, xlr, xhr, ylr, yhr, yclr, ychr, c1),
        [
            pltpu.VMEM((5, 17, 24, nz), F32),
            pltpu.VMEM((7, 16, 24, nz), F32),
            pltpu.VMEM((18, 24, nz), F32),
            pltpu.VMEM((16, 8, nz), F32),
            pltpu.VMEM((nz // 128, 32, 128), F32),
        ],
        flops=20_000_000,
        nbytes=20_000_000,
    )
    here = jnp.concatenate([moved(p1, "gx", 1), p1, moved(p1, "gx", -1)], axis=1)
    below, above = moved(here, "gy", 1), moved(here, "gy", -1)
    middle, p2 = call(
        middle_body,
        (shape(4, 4, nz // 2), shape(20, nz // 4)),
        (below, here, above, c2),
        [
            pltpu.VMEM((5, 13, 16, nz // 2), F32),
            pltpu.VMEM((7, 12, 16, nz // 2), F32),
            pltpu.VMEM((14, 16, nz // 2), F32),
            pltpu.VMEM((nz // 256, 16, 128), F32),
        ],
    )
    left, right = moved(p2, "gx", 2), moved(p2, "gx", -2)
    down, up = moved(p2, "gy", 2), moved(p2, "gy", -2)
    here = jnp.stack([moved(p2, "gx", 1), p2, moved(p2, "gx", -1)])
    below, above = moved(here, "gy", 1), moved(here, "gy", -1)
    coarse = call(
        coarse_level_body,
        shape(2, 2, nz // 4),
        (left, right, down, up, below, here, above),
        [
            pltpu.VMEM((5, 9, 8, nz // 4), F32),
            pltpu.VMEM((7, 8, 8, nz // 4), F32),
            pltpu.VMEM((10, 8, nz // 4), F32),
        ],
    )
    return (fine, middle, coarse)


def solution(mesh):
    placed = P("gx", "gy", None)
    return jax.shard_map(
        shards,
        mesh=mesh,
        in_specs=(placed,) * 6,
        out_specs=(placed,) * 3,
        check_vma=False,
    )
```

```python
import functools

import jax
import jax.numpy as jnp
from jax import lax
from jax.experimental import pallas as pl
from jax.experimental.pallas import tpu as pltpu
from jax.sharding import PartitionSpec as P

F32 = jnp.float32
BF16 = jnp.bfloat16

U, F, A, BX, BY, BZ = range(6)
PAIRS = ((U, F), (A, BY), (BX, BZ))
H = 4


def iota(shape, dim):
    return lax.broadcasted_iota(jnp.int32, shape, dim)


def call(body, outs, args, scratch=(), flops=1_000_000, nbytes=2_000_000, space=pltpu.VMEM, grant=48 << 10):
    vmem = pl.BlockSpec(memory_space=pltpu.VMEM)
    return pl.pallas_call(
        body,
        out_shape=outs,
        in_specs=[pl.BlockSpec(memory_space=space)] * len(args),
        out_specs=jax.tree.map(lambda _: vmem, outs),
        scratch_shapes=list(scratch),
        compiler_params=pltpu.CompilerParams(vmem_limit_bytes=grant << 10),
        cost_estimate=pl.CostEstimate(flops=flops, bytes_accessed=nbytes, transcendentals=0),
    )(*args)


def pair_low(first, second):
    return jnp.where(iota(first.shape, 0) < 4, first, pltpu.roll(second, 4, 0))


def pair_high(first, second):
    return jnp.where(iota(first.shape, 0) >= 4, first, pltpu.roll(second, 4, 0))


def pack_body(u, f, a, bx, by, bz, own, xl, xh, yl, yh, uv, fv, av, bxv, byv, bzv, sems):
    fields = (uv, fv, av, bxv, byv, bzv)
    copies = [pltpu.make_async_copy(src, dst, sems.at[k]) for k, (src, dst) in enumerate(zip((u, f, a, bx, by, bz), fields))]
    for copy in copies:
        copy.start()
    for copy in copies:
        copy.wait()
    cut = bxv[3].astype(F32)
    for k, ref in enumerate(fields):
        for j in range(H):
            low, high = ref[j].astype(F32), ref[4 + j].astype(F32)
            own[k * 8 + j] = low
            own[k * 8 + 4 + j] = high
            if j == 3:
                if k == F:
                    low = low + cut * uv[4]
                elif k == A:
                    low = low + cut
                elif k == BX:
                    low = jnp.zeros_like(low)
            if j == 0:
                if k == F:
                    high = high + cut * uv[3]
                elif k == A:
                    high = high + cut
            xl[k * H + j] = low
            xh[k * H + j] = high
    row = iota(u.shape[1:], 0)
    for p in range(u.shape[0]):
        v = [own[k * 8 + p] for k in range(6)]
        face = v[BY]
        low = list(v)
        low[F] = v[F] + jnp.where(row == 3, face * pltpu.roll(v[U], 7, 0), 0.0)
        low[A] = v[A] + jnp.where(row == 3, face, 0.0)
        low[BY] = jnp.where(row == 3, 0.0, face)
        high = list(v)
        below = pltpu.roll(face, 1, 0)
        high[F] = v[F] + jnp.where(row == 4, below * pltpu.roll(v[U], 1, 0), 0.0)
        high[A] = v[A] + jnp.where(row == 4, below, 0.0)
        for n, (i, j) in enumerate(PAIRS):
            yl[n * 8 + p] = pair_low(low[i], low[j])
            yh[n * 8 + p] = pair_high(high[i], high[j])


def beside(count):
    at = lax.axis_index("gx")
    return [jnp.where(at >= d, 1.0, 0.0) if s < 0 else jnp.where(at < count - d, 1.0, 0.0) for d in (1, 2) for s in (-1, 1)]


def corner_body(count, xlr, xhr, ycl, ych):
    lower, upper = beside(count)[:2]
    for p in range(8):
        v = [xhr[k * H + p] * lower if p < 4 else xlr[k * H + p - 4] * upper for k in range(6)]
        for n, (i, j) in enumerate(PAIRS):
            ycl[n * 8 + p] = pair_low(v[i], v[j])
            ych[n * 8 + p] = pair_high(v[i], v[j])


def halves(n):
    row, col = iota((n, n // 2), 0), iota((n, n // 2), 1)
    both = jnp.where(row // 2 == col, 1.0, 0.0).astype(BF16)
    odd = jnp.where(row == 2 * col + 1, 1.0, 0.0).astype(BF16)
    return both, odd


def exact_dot(x, m):
    n = x.shape[0]
    one = x.astype(BF16)
    rest = x - one.astype(F32)
    two = rest.astype(BF16)
    three = (rest - two.astype(F32)).astype(BF16)
    y = jnp.dot(
        jnp.concatenate([one.astype(F32), two.astype(F32), three.astype(F32)], axis=0).astype(BF16),
        m,
        preferred_element_type=F32,
    )
    return (y[2 * n :] + y[n : 2 * n]) + y[:n]


def put(ref, at, x):
    for g in range(x.shape[1] // 128):
        ref[g, at : at + x.shape[0]] = x[:, 128 * g : 128 * g + 128]


def every_other(ref, first, n, width):
    return jnp.concatenate([ref[g, pl.ds(first, n, 2)] for g in range(width // 128)], axis=1)


def below_z(face):
    return jnp.where(iota(face.shape, face.ndim - 1) == 0, 0.0, pltpu.roll(face, 1, face.ndim - 1))


def coarse_body(count, own, xhr, yhr, c1, c2, rows, edge, fine, small):
    nz = own.shape[2]
    both, odd = halves(nz)
    both2, odd2 = halves(nz // 2)

    def even_odd(n):
        return every_other(rows, 0, n, nz), every_other(rows, 1, n, nz)

    def pairs(k):
        for i in range(4):
            put(rows, 8 * i, own[k * 8 + 2 * i] + own[k * 8 + 2 * i + 1])
        return even_odd(16)

    e, o = pairs(A)
    a_in = e + o
    e, o = pairs(BZ)
    bz_in = e + o
    e, o = pairs(BY)
    by_in = o
    for i in range(4):
        put(rows, 8 * i, own[BX * 8 + 2 * i + 1])
    e, o = even_odd(16)
    bx_in = e + o
    put(rows, 0, xhr[BX * H + 3] * beside(count)[0])
    e, o = even_odd(4)
    edge[0:4] = e + o
    for i in range(4):
        edge[4 + i : 5 + i] = yhr[8 + 2 * i, 3:4] + yhr[8 + 2 * i + 1, 3:4]
    out = exact_dot(jnp.concatenate([a_in, bx_in, by_in, edge[...]], axis=0), both)
    a1, bx1, by1, edges = out[0:16] * 0.125, out[16:32] * 0.25, out[32:48] * 0.25, out[48:56] * 0.25
    bz1 = exact_dot(bz_in, odd) * 0.25
    c1[1] = bx1
    c1[2] = by1
    c1[3] = bz1
    fine[0, 0:8] = edges
    fine[1, 0:4] = edges[0:4]
    fine[1, 4:20] = bx1
    lower_x = fine[1, 0:16]
    fine[2, 1:17] = by1
    lower_y = fine[2, 0:16]
    for i in range(4):
        fine[3, 4 * i : 4 * i + 4] = jnp.broadcast_to(fine[0, 4 + i : 5 + i], (4, nz // 2))
    lower_y = jnp.where(iota(lower_y.shape, 0) % 4 == 0, fine[3, 0:16], lower_y)
    c1[0] = a1 + 0.25 * ((bx1 + lower_x) + (by1 + lower_y) + (bz1 + below_z(bz1)))

    def split(x):
        put(rows, 0, x)
        n = x.shape[0] // 2
        return every_other(rows, 0, n, nz // 2), every_other(rows, 1, n, nz // 2)

    def layers(t):
        small[0:8] = t
        top = small[0:2] + small[2:4]
        bottom = small[4:6] + small[6:8]
        return top, bottom

    e, o = split(a1)
    a_t = layers(e + o)
    e, o = split(bz1)
    bz_t = layers(e + o)
    e, o = split(by1)
    by_t = layers(o)
    e, o = split(bx1)
    small[0:8] = e + o
    bx_t = (small[2:4], small[6:8])
    e, o = split(edges)
    small[0:4] = e + o
    small[8:10] = a_t[0]
    small[10:12] = a_t[1]
    small[12:14] = by_t[0]
    small[14:16] = by_t[1]
    small[16:18] = bx_t[0]
    small[18:20] = bx_t[1]
    small[20:24] = small[0:4]
    small[24:26] = bz_t[0]
    small[26:28] = bz_t[1]
    small[28:32] = small[0:4]
    out = exact_dot(small[8:24], both2)
    out_z = exact_dot(small[24:32], odd2)[0:4] * 0.25
    a2, by2, bx2, edges = out[0:4] * 0.125, out[4:8] * 0.25, out[8:12] * 0.25, out[12:16] * 0.25
    w = nz // 4
    c2[4:8] = bx2
    c2[8:12] = by2
    c2[12:16] = out_z
    small[0:2, 0:w] = edges[0:2]
    small[2:6, 0:w] = bx2
    lower_x = small[0:4, 0:w]
    small[8:12, 0:w] = by2
    small[16:20, 0:w] = edges
    small[24:25, 0:w] = small[18:19, 0:w]
    small[25:26, 0:w] = small[8:9, 0:w]
    small[26:27, 0:w] = small[19:20, 0:w]
    small[27:28, 0:w] = small[10:11, 0:w]
    lower_y = small[24:28, 0:w]
    c2[0:4] = a2 + 0.0625 * ((bx2 + lower_x) + (by2 + lower_y) + (out_z + below_z(out_z)))


def set_weights(weights, w, inverse, source, up_x, low_x, up_y, up_z):
    lane = iota(inverse.shape, 1)
    nz = inverse.shape[1]
    weights[0, w] = source * inverse
    weights[1, w] = up_x * inverse
    weights[2, w] = low_x * inverse
    weights[3, w] = up_y * inverse
    weights[4, w] = pltpu.roll(up_y, 1, 0) * inverse
    weights[5, w] = jnp.where(lane == nz - 1, 0.0, up_z) * inverse
    weights[6, w] = jnp.where(lane == 0, 0.0, pltpu.roll(up_z, 1, 1)) * inverse


def relaxed(weights, held, w):
    here = held[w + 1]
    ny, nz = here.shape
    x = weights[1, w] * held[w + 2] + weights[2, w] * held[w]
    y = weights[3, w] * pltpu.roll(here, ny - 1, 0) + weights[4, w] * pltpu.roll(here, 1, 0)
    z = weights[5, w] * pltpu.roll(here, nz - 1, 1) + weights[6, w] * pltpu.roll(here, 1, 1)
    return ((weights[0, w] + x) + (y + z)), here


def smooth(weights, held, unroll):
    count = weights.shape[1]
    spare = (weights.shape[2], weights.shape[3])
    parity = (iota(spare, 0) + iota(spare, 1)) % 2
    for step in range(4):

        def one(w, carry, step=step):
            new, here = relaxed(weights, held, w)
            held[w + 1] = jnp.where((parity + w + step) % 2 == 0, new, here)
            return carry

        if unroll:
            for w in range(step, count - step):
                one(w, 0)
        else:
            lax.fori_loop(step, count - step, one, 0, unroll=2)


def fine_body(count, own, xlr, xhr, ylr, yhr, yclr, ychr, c1, out, p1, win, weights, held, diag, rows):
    nz = own.shape[2]
    first = iota((8, nz), 0) < 4
    lower, upper = beside(count)[:2]

    for w in range(16):
        for n, pair in enumerate(PAIRS):
            if w < 4:
                below, above = ychr[n * 8 + w], yclr[n * 8 + w]
            elif w < 12:
                below, above = yhr[n * 8 + w - 4], ylr[n * 8 + w - 4]
            else:
                below, above = ychr[n * 8 + w - 8], yclr[n * 8 + w - 8]
            for side, k in enumerate(pair):
                if side:
                    halo = pltpu.roll(jnp.where(first, below, above), 4, 0)
                else:
                    halo = jnp.where(first, above, below)
                if w < 4:
                    mid = xhr[k * H + w] * lower
                elif w < 12:
                    mid = own[k * 8 + w - 4]
                else:
                    mid = xlr[k * H + w - 12] * upper
                if k == U:
                    held[w + 1, 0:8] = mid
                    held[w + 1, 8:16] = halo
                else:
                    win[k - 1, w + 1, 0:8] = mid
                    win[k - 1, w + 1, 8:16] = halo
    zero = jnp.zeros((16, nz), F32)
    held[0] = zero
    held[17] = zero
    win[BX - 1, 0] = zero

    def prepare(w, carry):
        av, bxv, byv, bzv = win[A - 1, w + 1], win[BX - 1, w + 1], win[BY - 1, w + 1], win[BZ - 1, w + 1]
        low_x = win[BX - 1, w]
        total = av + ((bxv + low_x) + (byv + pltpu.roll(byv, 1, 0)) + (bzv + below_z(bzv)))
        inside = av > 0.0
        inverse = jnp.where(inside, 1.0 / jnp.where(inside, total, 1.0), 0.0)
        set_weights(weights, w, inverse, win[F - 1, w + 1], bxv, low_x, byv, bzv)
        diag[w] = total[0:8]
        return carry

    lax.fori_loop(0, 16, prepare, 0, unroll=2)
    smooth(weights, held, False)
    for i in range(4):
        total = None
        for j in range(2):
            w = 4 + 2 * i + j
            new, here = relaxed(weights, held, w)
            out[w - 4] = here[0:8]
            res = diag[w] * (new[0:8] - here[0:8])
            total = res if total is None else total + res
        put(rows, 8 * i, total)
    both, _ = halves(nz)
    p1[0] = exact_dot(every_other(rows, 0, 16, nz) + every_other(rows, 1, 16, nz), both) * 0.125
    for k in range(4):
        p1[1 + k] = c1[k]


def middle_body(count, left, here, right, c2, out, p2, win, weights, held, rows):
    nz = here.shape[3]
    first = iota((8, nz), 0) < 4
    lower, upper = beside(count)[:2]
    zero = jnp.zeros((16, nz), F32)
    win[2, 0] = zero
    for b, (source, there) in enumerate(((left, lower), (here, None), (right, upper))):
        for k in range(5):
            for half in range(2):
                at = slice(8 * half, 8 * half + 8)
                below, mid, above = source[0, k, at], source[1, k, at], source[2, k, at]
                if k == 1 and there is not None:
                    below, mid, above = below * there, mid * there, above * there
                w = 4 * b + 2 * half + 1
                win[k, w, 0:8] = jnp.where(first, mid, pltpu.roll(above, 4, 0))
                win[k, w, 8:16] = jnp.where(first, 0.0, pltpu.roll(below, 4, 0))
                win[k, w + 1, 0:8] = jnp.where(first, pltpu.roll(mid, 4, 0), above)
                win[k, w + 1, 8:16] = jnp.where(first, 0.0, below)
    for w in range(12):
        total = win[1, w + 1]
        inside = total > 0.0
        inverse = jnp.where(inside, 0.25 / jnp.where(inside, total, 1.0), 0.0)
        set_weights(weights, w, inverse, 4.0 * win[0, w + 1], win[2, w + 1], win[2, w], win[3, w + 1], win[4, w + 1])
        held[w + 1] = zero
    held[0] = zero
    held[13] = zero
    smooth(weights, held, True)
    for i in range(2):
        total = None
        for j in range(2):
            w = 4 + 2 * i + j
            new, now = relaxed(weights, held, w)
            out[w - 4] = now[0:4]
            res = win[1, w + 1, 0:8] * (new[0:8] - now[0:8])
            total = res if total is None else total + res
        put(rows, 8 * i, total)
    both, _ = halves(nz)
    coarse = exact_dot(every_other(rows, 0, 8, nz) + every_other(rows, 1, 8, nz), both) * 0.125
    p2[0:2] = coarse[0:2]
    p2[2:4] = coarse[4:6]
    p2[4:20] = c2[...]


def coarse_level_body(count, left, mid, right, down, up, out, win, weights, held):
    win[...] = jnp.zeros(win.shape, F32)
    near = beside(count)
    for k in range(5):
        factor = near if k == 1 else [1.0] * 4
        win[k, 1, 3:5] = left[3, 4 * k + 2 : 4 * k + 4] * factor[2]
        win[k, 8, 3:5] = right[3, 4 * k : 4 * k + 2] * factor[3]
        for i in range(2):
            at = 4 * k + 2 * i
            win[k, 4 + i, 0:1] = down[at + 1 : at + 2]
            win[k, 4 + i, 7:8] = up[at : at + 1]
            for b, (source, there) in enumerate(((left, factor[0]), (mid, 1.0), (right, factor[1]))):
                for j in range(3):
                    win[k, 2 + 2 * b + i, 1 + 2 * j : 3 + 2 * j] = source[j, at : at + 2] * there
    held[...] = jnp.zeros(held.shape, F32)
    for w in range(8):
        total = win[1, w + 1]
        inside = total > 0.0
        inverse = jnp.where(inside, 0.0625 / jnp.where(inside, total, 1.0), 0.0)
        set_weights(weights, w, inverse, 16.0 * win[0, w + 1], win[2, w + 1], win[2, w], win[3, w + 1], win[4, w + 1])
    smooth(weights, held, True)
    for i in range(2):
        out[i] = held[4 + i, 3:5]


def along_y(block, by):
    count = lax.axis_size("gy")
    return lax.ppermute(block, "gy", [(i, i + by) for i in range(count) if 0 <= i + by < count])


def round_x(block, by):
    count = lax.axis_size("gx")
    return lax.ppermute(block, "gx", [(i, (i + by) % count) for i in range(count)])


def shape(*dims):
    return jax.ShapeDtypeStruct(dims, F32)


def shards(solution, right_side, alpha, beta_x, beta_y, beta_z):
    args = (solution, right_side, alpha, beta_x, beta_y, beta_z)
    nz = solution.shape[2]
    count = lax.axis_size("gx")
    sent = shape(24, 8, nz)
    own, xl, xh, yl, yh = call(
        pack_body,
        (shape(48, 8, nz),) + (sent,) * 4,
        args,
        [pltpu.VMEM(x.shape, x.dtype) for x in args] + [pltpu.SemaphoreType.DMA((6,))],
        space=pltpu.HBM,
        grant=56 << 10,
    )
    xlr, xhr = round_x(xl, -1), round_x(xh, 1)
    ylr, yhr = along_y(yl, -1), along_y(yh, 1)
    ycl, ych = call(functools.partial(corner_body, count), (sent,) * 2, (xlr, xhr))
    yclr, ychr = along_y(ycl, -1), along_y(ych, 1)
    c1, c2 = call(
        functools.partial(coarse_body, count),
        (shape(4, 16, nz // 2), shape(16, nz // 4)),
        (own, xhr, yhr),
        [
            pltpu.VMEM((nz // 128, 32, 128), F32),
            pltpu.VMEM((8, nz), F32),
            pltpu.VMEM((4, 24, nz // 2), F32),
            pltpu.VMEM((32, nz // 2), F32),
        ],
    )
    fine, p1 = call(
        functools.partial(fine_body, count),
        (shape(8, 8, nz), shape(5, 16, nz // 2)),
        (own, xlr, xhr, ylr, yhr, yclr, ychr, c1),
        [
            pltpu.VMEM((5, 17, 16, nz), F32),
            pltpu.VMEM((7, 16, 16, nz), F32),
            pltpu.VMEM((18, 16, nz), F32),
            pltpu.VMEM((16, 8, nz), F32),
            pltpu.VMEM((nz // 128, 32, 128), F32),
        ],
        flops=20_000_000,
        nbytes=20_000_000,
    )
    here = jnp.stack([along_y(p1, 1), p1, along_y(p1, -1)])
    left, right = round_x(here, 1), round_x(here, -1)
    middle, p2 = call(
        functools.partial(middle_body, count),
        (shape(4, 4, nz // 2), shape(20, nz // 4)),
        (left, here, right, c2),
        [
            pltpu.VMEM((5, 13, 16, nz // 2), F32),
            pltpu.VMEM((7, 12, 16, nz // 2), F32),
            pltpu.VMEM((14, 16, nz // 2), F32),
            pltpu.VMEM((nz // 256, 16, 128), F32),
        ],
    )
    before, after = round_x(p2, 1), round_x(p2, -1)
    below, above = along_y(p2, 1), along_y(p2, -1)
    down, up = along_y(p2, 2), along_y(p2, -2)
    left = round_x(jnp.stack([below, p2, above, before]), 1)
    right = round_x(jnp.stack([below, p2, above, after]), -1)
    coarse = call(
        functools.partial(coarse_level_body, count),
        shape(2, 2, nz // 4),
        (left, jnp.stack([below, p2, above]), right, down, up),
        [
            pltpu.VMEM((5, 9, 8, nz // 4), F32),
            pltpu.VMEM((7, 8, 8, nz // 4), F32),
            pltpu.VMEM((10, 8, nz // 4), F32),
        ],
    )
    return (fine, middle, coarse)


def solution(mesh):
    placed = P("gx", "gy", None)
    return jax.shard_map(
        shards,
        mesh=mesh,
        in_specs=(placed,) * 6,
        out_specs=(placed,) * 3,
        check_vma=False,
    )
```

```python
import functools

import jax
import jax.numpy as jnp
from jax import lax
from jax.experimental import pallas as pl
from jax.experimental.pallas import tpu as pltpu
from jax.sharding import PartitionSpec as P

F32 = jnp.float32
BF16 = jnp.bfloat16

U, F, A, BX, BY, BZ = range(6)
PAIRS = ((U, F), (A, BY), (BX, BZ))
H = 4


def iota(shape, dim):
    return lax.broadcasted_iota(jnp.int32, shape, dim)


def call(body, outs, args, scratch=(), flops=1_000_000, nbytes=2_000_000, space=pltpu.VMEM, grant=48 << 10):
    vmem = pl.BlockSpec(memory_space=pltpu.VMEM)
    return pl.pallas_call(
        body,
        out_shape=outs,
        in_specs=[pl.BlockSpec(memory_space=space)] * len(args),
        out_specs=jax.tree.map(lambda _: vmem, outs),
        scratch_shapes=list(scratch),
        compiler_params=pltpu.CompilerParams(vmem_limit_bytes=grant << 10),
        cost_estimate=pl.CostEstimate(flops=flops, bytes_accessed=nbytes, transcendentals=0),
    )(*args)


def pair_low(first, second):
    return jnp.where(iota(first.shape, 0) < 4, first, pltpu.roll(second, 4, 0))


def pair_high(first, second):
    return jnp.where(iota(first.shape, 0) >= 4, first, pltpu.roll(second, 4, 0))


def pack_body(u, f, a, bx, by, bz, own, xl, xh, yl, yh, uv, fv, av, bxv, byv, bzv, sems):
    fields = (uv, fv, av, bxv, byv, bzv)
    copies = [pltpu.make_async_copy(src, dst, sems.at[k]) for k, (src, dst) in enumerate(zip((u, f, a, bx, by, bz), fields))]
    for copy in copies:
        copy.start()
    for copy in copies:
        copy.wait()
    cut = bxv[3].astype(F32)
    for k, ref in enumerate(fields):
        for j in range(H):
            low, high = ref[j].astype(F32), ref[4 + j].astype(F32)
            own[k * 8 + j] = low
            own[k * 8 + 4 + j] = high
            if j == 3:
                if k == F:
                    low = low + cut * uv[4]
                elif k == A:
                    low = low + cut
                elif k == BX:
                    low = jnp.zeros_like(low)
            if j == 0:
                if k == F:
                    high = high + cut * uv[3]
                elif k == A:
                    high = high + cut
            xl[k * H + j] = low
            xh[k * H + j] = high
    row = iota(u.shape[1:], 0)
    for p in range(u.shape[0]):
        v = [own[k * 8 + p] for k in range(6)]
        face = v[BY]
        low = list(v)
        low[F] = v[F] + jnp.where(row == 3, face * pltpu.roll(v[U], 7, 0), 0.0)
        low[A] = v[A] + jnp.where(row == 3, face, 0.0)
        low[BY] = jnp.where(row == 3, 0.0, face)
        high = list(v)
        below = pltpu.roll(face, 1, 0)
        high[F] = v[F] + jnp.where(row == 4, below * pltpu.roll(v[U], 1, 0), 0.0)
        high[A] = v[A] + jnp.where(row == 4, below, 0.0)
        for n, (i, j) in enumerate(PAIRS):
            yl[n * 8 + p] = pair_low(low[i], low[j])
            yh[n * 8 + p] = pair_high(high[i], high[j])


def beside(count):
    at = lax.axis_index("gx")
    return [jnp.where(at >= d, 1.0, 0.0) if s < 0 else jnp.where(at < count - d, 1.0, 0.0) for d in (1, 2) for s in (-1, 1)]


CORNER = (
    [(1, (k,)) for k in range(6)]
    + [(2, (U,)), (2, (BY,)), (2, (BX,)), (2, (F, A)), (2, (BZ,))]
    + [(3, (U, BY)), (3, (F, A)), (3, (BX, BZ)), (4, (U, BY)), (4, (BX,))]
)


def nearest(shape):
    row = iota(shape, 0)
    return (row < 2) | (row >= 6)


def halo_rows(k, p, ylr, yhr):
    n, side = next((n, pair.index(k)) for n, pair in enumerate(PAIRS) if k in pair)
    above, below = ylr[n * 8 + p], yhr[n * 8 + p]
    first = iota(above.shape, 0) < 4
    if side:
        return pltpu.roll(jnp.where(first, below, above), 4, 0)
    return jnp.where(first, above, below)


def corner_body(ylr, yhr, xcl, xch):
    near = nearest(ylr.shape[1:])
    for out, plane in ((xcl, lambda d: d - 1), (xch, lambda d: 8 - d)):
        for t, (d, fields) in enumerate(CORNER):
            tile = halo_rows(fields[0], plane(d), ylr, yhr)
            if len(fields) == 2:
                tile = jnp.where(near, tile, pltpu.roll(halo_rows(fields[1], plane(d), ylr, yhr), 4, 0))
            out[t] = tile


def corner_rows(k, d, tiles):
    for t, (distance, fields) in enumerate(CORNER):
        if distance == d and k in fields:
            tile = tiles[t]
            if len(fields) == 1:
                return tile
            if fields[1] == k:
                tile = pltpu.roll(tile, 4, 0)
            return jnp.where(nearest(tile.shape), tile, 0.0)
    return jnp.zeros(tiles.shape[1:], F32)


def halves(n):
    row, col = iota((n, n // 2), 0), iota((n, n // 2), 1)
    both = jnp.where(row // 2 == col, 1.0, 0.0).astype(BF16)
    odd = jnp.where(row == 2 * col + 1, 1.0, 0.0).astype(BF16)
    return both, odd


def exact_dot(x, m):
    n = x.shape[0]
    one = x.astype(BF16)
    rest = x - one.astype(F32)
    two = rest.astype(BF16)
    three = (rest - two.astype(F32)).astype(BF16)
    y = jnp.dot(
        jnp.concatenate([one.astype(F32), two.astype(F32), three.astype(F32)], axis=0).astype(BF16),
        m,
        preferred_element_type=F32,
    )
    return (y[2 * n :] + y[n : 2 * n]) + y[:n]


def put(ref, at, x):
    for g in range(x.shape[1] // 128):
        ref[g, at : at + x.shape[0]] = x[:, 128 * g : 128 * g + 128]


def every_other(ref, first, n, width):
    return jnp.concatenate([ref[g, pl.ds(first, n, 2)] for g in range(width // 128)], axis=1)


def below_z(face):
    return jnp.where(iota(face.shape, face.ndim - 1) == 0, 0.0, pltpu.roll(face, 1, face.ndim - 1))


def coarse_body(count, own, xhr, yhr, c1, c2, rows, edge, fine, small):
    nz = own.shape[2]
    both, odd = halves(nz)
    both2, odd2 = halves(nz // 2)

    def even_odd(n):
        return every_other(rows, 0, n, nz), every_other(rows, 1, n, nz)

    def pairs(k):
        for i in range(4):
            put(rows, 8 * i, own[k * 8 + 2 * i] + own[k * 8 + 2 * i + 1])
        return even_odd(16)

    e, o = pairs(A)
    a_in = e + o
    e, o = pairs(BZ)
    bz_in = e + o
    e, o = pairs(BY)
    by_in = o
    for i in range(4):
        put(rows, 8 * i, own[BX * 8 + 2 * i + 1])
    e, o = even_odd(16)
    bx_in = e + o
    put(rows, 0, xhr[BX * H + 3] * beside(count)[0])
    e, o = even_odd(4)
    edge[0:4] = e + o
    for i in range(4):
        edge[4 + i : 5 + i] = yhr[8 + 2 * i, 3:4] + yhr[8 + 2 * i + 1, 3:4]
    out = exact_dot(jnp.concatenate([a_in, bx_in, by_in, edge[...]], axis=0), both)
    a1, bx1, by1, edges = out[0:16] * 0.125, out[16:32] * 0.25, out[32:48] * 0.25, out[48:56] * 0.25
    bz1 = exact_dot(bz_in, odd) * 0.25
    c1[1] = bx1
    c1[2] = by1
    c1[3] = bz1
    fine[0, 0:8] = edges
    fine[1, 0:4] = edges[0:4]
    fine[1, 4:20] = bx1
    lower_x = fine[1, 0:16]
    fine[2, 1:17] = by1
    lower_y = fine[2, 0:16]
    for i in range(4):
        fine[3, 4 * i : 4 * i + 4] = jnp.broadcast_to(fine[0, 4 + i : 5 + i], (4, nz // 2))
    lower_y = jnp.where(iota(lower_y.shape, 0) % 4 == 0, fine[3, 0:16], lower_y)
    c1[0] = a1 + 0.25 * ((bx1 + lower_x) + (by1 + lower_y) + (bz1 + below_z(bz1)))

    def split(x):
        put(rows, 0, x)
        n = x.shape[0] // 2
        return every_other(rows, 0, n, nz // 2), every_other(rows, 1, n, nz // 2)

    def layers(t):
        small[0:8] = t
        top = small[0:2] + small[2:4]
        bottom = small[4:6] + small[6:8]
        return top, bottom

    e, o = split(a1)
    a_t = layers(e + o)
    e, o = split(bz1)
    bz_t = layers(e + o)
    e, o = split(by1)
    by_t = layers(o)
    e, o = split(bx1)
    small[0:8] = e + o
    bx_t = (small[2:4], small[6:8])
    e, o = split(edges)
    small[0:4] = e + o
    small[8:10] = a_t[0]
    small[10:12] = a_t[1]
    small[12:14] = by_t[0]
    small[14:16] = by_t[1]
    small[16:18] = bx_t[0]
    small[18:20] = bx_t[1]
    small[20:24] = small[0:4]
    small[24:26] = bz_t[0]
    small[26:28] = bz_t[1]
    small[28:32] = small[0:4]
    out = exact_dot(small[8:24], both2)
    out_z = exact_dot(small[24:32], odd2)[0:4] * 0.25
    a2, by2, bx2, edges = out[0:4] * 0.125, out[4:8] * 0.25, out[8:12] * 0.25, out[12:16] * 0.25
    w = nz // 4
    c2[4:8] = bx2
    c2[8:12] = by2
    c2[12:16] = out_z
    small[0:2, 0:w] = edges[0:2]
    small[2:6, 0:w] = bx2
    lower_x = small[0:4, 0:w]
    small[8:12, 0:w] = by2
    small[16:20, 0:w] = edges
    small[24:25, 0:w] = small[18:19, 0:w]
    small[25:26, 0:w] = small[8:9, 0:w]
    small[26:27, 0:w] = small[19:20, 0:w]
    small[27:28, 0:w] = small[10:11, 0:w]
    lower_y = small[24:28, 0:w]
    c2[0:4] = a2 + 0.0625 * ((bx2 + lower_x) + (by2 + lower_y) + (out_z + below_z(out_z)))


def set_weights(weights, w, inverse, source, up_x, low_x, up_y, up_z):
    lane = iota(inverse.shape, 1)
    nz = inverse.shape[1]
    weights[0, w] = source * inverse
    weights[1, w] = up_x * inverse
    weights[2, w] = low_x * inverse
    weights[3, w] = up_y * inverse
    weights[4, w] = pltpu.roll(up_y, 1, 0) * inverse
    weights[5, w] = jnp.where(lane == nz - 1, 0.0, up_z) * inverse
    weights[6, w] = jnp.where(lane == 0, 0.0, pltpu.roll(up_z, 1, 1)) * inverse


def relaxed(weights, held, w):
    here = held[w + 1]
    ny, nz = here.shape
    x = weights[1, w] * held[w + 2] + weights[2, w] * held[w]
    y = weights[3, w] * pltpu.roll(here, ny - 1, 0) + weights[4, w] * pltpu.roll(here, 1, 0)
    z = weights[5, w] * pltpu.roll(here, nz - 1, 1) + weights[6, w] * pltpu.roll(here, 1, 1)
    return ((weights[0, w] + x) + (y + z)), here


def smooth(weights, held, unroll):
    count = weights.shape[1]
    spare = (weights.shape[2], weights.shape[3])
    parity = (iota(spare, 0) + iota(spare, 1)) % 2
    for step in range(4):

        def one(w, carry, step=step):
            new, here = relaxed(weights, held, w)
            held[w + 1] = jnp.where((parity + w + step) % 2 == 0, new, here)
            return carry

        if unroll:
            for w in range(step, count - step):
                one(w, 0)
        else:
            lax.fori_loop(step, count - step, one, 0, unroll=2)


def fine_body(count, own, xlr, xhr, ylr, yhr, xclr, xchr, c1, out, p1, win, weights, held, diag, rows):
    nz = own.shape[2]
    lower, upper = beside(count)[:2]

    for w in range(16):
        for k in range(6):
            if w < 4:
                mid, halo, there = xhr[k * H + w], corner_rows(k, 4 - w, xchr), lower
            elif w < 12:
                mid, halo, there = own[k * 8 + w - 4], halo_rows(k, w - 4, ylr, yhr), None
            else:
                mid, halo, there = xlr[k * H + w - 12], corner_rows(k, w - 11, xclr), upper
            if there is not None and k in (U, A, BX):
                mid, halo = mid * there, halo * there
            if k == U:
                held[w + 1, 0:8] = mid
                held[w + 1, 8:16] = halo
            else:
                win[k - 1, w + 1, 0:8] = mid
                win[k - 1, w + 1, 8:16] = halo
    zero = jnp.zeros((16, nz), F32)
    held[0] = zero
    held[17] = zero
    win[BX - 1, 0] = zero

    def prepare(w, carry):
        av, bxv, byv, bzv = win[A - 1, w + 1], win[BX - 1, w + 1], win[BY - 1, w + 1], win[BZ - 1, w + 1]
        low_x = win[BX - 1, w]
        total = av + ((bxv + low_x) + (byv + pltpu.roll(byv, 1, 0)) + (bzv + below_z(bzv)))
        inside = av > 0.0
        inverse = jnp.where(inside, 1.0 / jnp.where(inside, total, 1.0), 0.0)
        set_weights(weights, w, inverse, win[F - 1, w + 1], bxv, low_x, byv, bzv)
        diag[w] = total[0:8]
        return carry

    lax.fori_loop(0, 16, prepare, 0, unroll=2)
    smooth(weights, held, False)
    for i in range(4):
        total = None
        for j in range(2):
            w = 4 + 2 * i + j
            new, here = relaxed(weights, held, w)
            out[w - 4] = here[0:8]
            res = diag[w] * (new[0:8] - here[0:8])
            total = res if total is None else total + res
        put(rows, 8 * i, total)
    both, _ = halves(nz)
    p1[0] = exact_dot(every_other(rows, 0, 16, nz) + every_other(rows, 1, 16, nz), both) * 0.125
    for k in range(4):
        p1[1 + k] = c1[k]


def middle_body(count, left, here, right, c2, out, p2, win, weights, held, rows):
    nz = here.shape[3]
    first = iota((8, nz), 0) < 4
    lower, upper = beside(count)[:2]
    zero = jnp.zeros((16, nz), F32)
    win[2, 0] = zero
    for b, (source, there) in enumerate(((left, lower), (here, None), (right, upper))):
        for k in range(5):
            for half in range(2):
                at = slice(8 * half, 8 * half + 8)
                below, mid, above = source[0, k, at], source[1, k, at], source[2, k, at]
                if k == 1 and there is not None:
                    below, mid, above = below * there, mid * there, above * there
                w = 4 * b + 2 * half + 1
                win[k, w, 0:8] = jnp.where(first, mid, pltpu.roll(above, 4, 0))
                win[k, w, 8:16] = jnp.where(first, 0.0, pltpu.roll(below, 4, 0))
                win[k, w + 1, 0:8] = jnp.where(first, pltpu.roll(mid, 4, 0), above)
                win[k, w + 1, 8:16] = jnp.where(first, 0.0, below)
    for w in range(12):
        total = win[1, w + 1]
        inside = total > 0.0
        inverse = jnp.where(inside, 0.25 / jnp.where(inside, total, 1.0), 0.0)
        set_weights(weights, w, inverse, 4.0 * win[0, w + 1], win[2, w + 1], win[2, w], win[3, w + 1], win[4, w + 1])
        held[w + 1] = zero
    held[0] = zero
    held[13] = zero
    smooth(weights, held, True)
    for i in range(2):
        total = None
        for j in range(2):
            w = 4 + 2 * i + j
            new, now = relaxed(weights, held, w)
            out[w - 4] = now[0:4]
            res = win[1, w + 1, 0:8] * (new[0:8] - now[0:8])
            total = res if total is None else total + res
        put(rows, 8 * i, total)
    both, _ = halves(nz)
    coarse = exact_dot(every_other(rows, 0, 8, nz) + every_other(rows, 1, 8, nz), both) * 0.125
    p2[0:2] = coarse[0:2]
    p2[2:4] = coarse[4:6]
    p2[4:20] = c2[...]


def coarse_level_body(count, left, mid, right, down, up, out, win, weights, held):
    win[...] = jnp.zeros(win.shape, F32)
    near = beside(count)
    for k in range(5):
        factor = near if k == 1 else [1.0] * 4
        win[k, 1, 3:5] = left[3, 4 * k + 2 : 4 * k + 4] * factor[2]
        win[k, 8, 3:5] = right[3, 4 * k : 4 * k + 2] * factor[3]
        for i in range(2):
            at = 4 * k + 2 * i
            win[k, 4 + i, 0:1] = down[at + 1 : at + 2]
            win[k, 4 + i, 7:8] = up[at : at + 1]
            for b, (source, there) in enumerate(((left, factor[0]), (mid, 1.0), (right, factor[1]))):
                for j in range(3):
                    win[k, 2 + 2 * b + i, 1 + 2 * j : 3 + 2 * j] = source[j, at : at + 2] * there
    held[...] = jnp.zeros(held.shape, F32)
    for w in range(8):
        total = win[1, w + 1]
        inside = total > 0.0
        inverse = jnp.where(inside, 0.0625 / jnp.where(inside, total, 1.0), 0.0)
        set_weights(weights, w, inverse, 16.0 * win[0, w + 1], win[2, w + 1], win[2, w], win[3, w + 1], win[4, w + 1])
    smooth(weights, held, True)
    for i in range(2):
        out[i] = held[4 + i, 3:5]


def along_y(block, by):
    count = lax.axis_size("gy")
    return lax.ppermute(block, "gy", [(i, i + by) for i in range(count) if 0 <= i + by < count])


def round_x(block, by):
    count = lax.axis_size("gx")
    return lax.ppermute(block, "gx", [(i, (i + by) % count) for i in range(count)])


def shape(*dims):
    return jax.ShapeDtypeStruct(dims, F32)


def shards(solution, right_side, alpha, beta_x, beta_y, beta_z):
    args = (solution, right_side, alpha, beta_x, beta_y, beta_z)
    nz = solution.shape[2]
    count = lax.axis_size("gx")
    sent = shape(24, 8, nz)
    own, xl, xh, yl, yh = call(
        pack_body,
        (shape(48, 8, nz),) + (sent,) * 4,
        args,
        [pltpu.VMEM(x.shape, x.dtype) for x in args] + [pltpu.SemaphoreType.DMA((6,))],
        space=pltpu.HBM,
        grant=56 << 10,
    )
    ylr, yhr = along_y(yl, -1), along_y(yh, 1)
    xlr, xhr = round_x(xl, -1), round_x(xh, 1)
    xcl, xch = call(corner_body, (shape(len(CORNER), 8, nz),) * 2, (ylr, yhr))
    xclr, xchr = round_x(xcl, -1), round_x(xch, 1)
    c1, c2 = call(
        functools.partial(coarse_body, count),
        (shape(4, 16, nz // 2), shape(16, nz // 4)),
        (own, xhr, yhr),
        [
            pltpu.VMEM((nz // 128, 32, 128), F32),
            pltpu.VMEM((8, nz), F32),
            pltpu.VMEM((4, 24, nz // 2), F32),
            pltpu.VMEM((32, nz // 2), F32),
        ],
    )
    fine, p1 = call(
        functools.partial(fine_body, count),
        (shape(8, 8, nz), shape(5, 16, nz // 2)),
        (own, xlr, xhr, ylr, yhr, xclr, xchr, c1),
        [
            pltpu.VMEM((5, 17, 16, nz), F32),
            pltpu.VMEM((7, 16, 16, nz), F32),
            pltpu.VMEM((18, 16, nz), F32),
            pltpu.VMEM((16, 8, nz), F32),
            pltpu.VMEM((nz // 128, 32, 128), F32),
        ],
        flops=20_000_000,
        nbytes=20_000_000,
    )
    here = jnp.stack([along_y(p1, 1), p1, along_y(p1, -1)])
    left, right = round_x(here, 1), round_x(here, -1)
    middle, p2 = call(
        functools.partial(middle_body, count),
        (shape(4, 4, nz // 2), shape(20, nz // 4)),
        (left, here, right, c2),
        [
            pltpu.VMEM((5, 13, 16, nz // 2), F32),
            pltpu.VMEM((7, 12, 16, nz // 2), F32),
            pltpu.VMEM((14, 16, nz // 2), F32),
            pltpu.VMEM((nz // 256, 16, 128), F32),
        ],
    )
    before, after = round_x(p2, 1), round_x(p2, -1)
    below, above = along_y(p2, 1), along_y(p2, -1)
    down, up = along_y(p2, 2), along_y(p2, -2)
    left = round_x(jnp.stack([below, p2, above, before]), 1)
    right = round_x(jnp.stack([below, p2, above, after]), -1)
    coarse = call(
        functools.partial(coarse_level_body, count),
        shape(2, 2, nz // 4),
        (left, jnp.stack([below, p2, above]), right, down, up),
        [
            pltpu.VMEM((5, 9, 8, nz // 4), F32),
            pltpu.VMEM((7, 8, 8, nz // 4), F32),
            pltpu.VMEM((10, 8, nz // 4), F32),
        ],
    )
    return (fine, middle, coarse)


def solution(mesh):
    placed = P("gx", "gy", None)
    return jax.shard_map(
        shards,
        mesh=mesh,
        in_specs=(placed,) * 6,
        out_specs=(placed,) * 3,
        check_vma=False,
    )
```

```python
import functools

import jax
import jax.numpy as jnp
from jax import lax
from jax.experimental import pallas as pl
from jax.experimental.pallas import tpu as pltpu
from jax.sharding import PartitionSpec as P

F32 = jnp.float32
BF16 = jnp.bfloat16

U, F, A, BX, BY, BZ = range(6)
PAIRS = ((U, F), (A, BY), (BX, BZ))
H = 4


def iota(shape, dim):
    return lax.broadcasted_iota(jnp.int32, shape, dim)


def call(body, outs, args, scratch=(), flops=1_000_000, nbytes=2_000_000, space=pltpu.VMEM, grant=48 << 10):
    vmem = pl.BlockSpec(memory_space=pltpu.VMEM)
    return pl.pallas_call(
        body,
        out_shape=outs,
        in_specs=[pl.BlockSpec(memory_space=space)] * len(args),
        out_specs=jax.tree.map(lambda _: vmem, outs),
        scratch_shapes=list(scratch),
        compiler_params=pltpu.CompilerParams(vmem_limit_bytes=grant << 10),
        cost_estimate=pl.CostEstimate(flops=flops, bytes_accessed=nbytes, transcendentals=0),
    )(*args)


def pair_low(first, second):
    return jnp.where(iota(first.shape, 0) < 4, first, pltpu.roll(second, 4, 0))


def pair_high(first, second):
    return jnp.where(iota(first.shape, 0) >= 4, first, pltpu.roll(second, 4, 0))


def pack_body(u, f, a, bx, by, bz, own, xl, xh, yl, yh, uv, fv, av, bxv, byv, bzv, sems):
    fields = (uv, fv, av, bxv, byv, bzv)
    copies = [pltpu.make_async_copy(src, dst, sems.at[k]) for k, (src, dst) in enumerate(zip((u, f, a, bx, by, bz), fields))]
    for copy in copies:
        copy.start()
    for copy in copies:
        copy.wait()
    cut = bxv[3].astype(F32)
    for k, ref in enumerate(fields):
        for j in range(H):
            low, high = ref[j].astype(F32), ref[4 + j].astype(F32)
            own[k * 8 + j] = low
            own[k * 8 + 4 + j] = high
            if j == 3:
                if k == F:
                    low = low + cut * uv[4]
                elif k == A:
                    low = low + cut
                elif k == BX:
                    low = jnp.zeros_like(low)
            if j == 0:
                if k == F:
                    high = high + cut * uv[3]
                elif k == A:
                    high = high + cut
            xl[k * H + j] = low
            xh[k * H + j] = high
    row = iota(u.shape[1:], 0)
    for p in range(u.shape[0]):
        v = [own[k * 8 + p] for k in range(6)]
        face = v[BY]
        low = list(v)
        low[F] = v[F] + jnp.where(row == 3, face * pltpu.roll(v[U], 7, 0), 0.0)
        low[A] = v[A] + jnp.where(row == 3, face, 0.0)
        low[BY] = jnp.where(row == 3, 0.0, face)
        high = list(v)
        below = pltpu.roll(face, 1, 0)
        high[F] = v[F] + jnp.where(row == 4, below * pltpu.roll(v[U], 1, 0), 0.0)
        high[A] = v[A] + jnp.where(row == 4, below, 0.0)
        for n, (i, j) in enumerate(PAIRS):
            yl[n * 8 + p] = pair_low(low[i], low[j])
            yh[n * 8 + p] = pair_high(high[i], high[j])


def beside(count):
    at = lax.axis_index("gx")
    return [jnp.where(at >= d, 1.0, 0.0) if s < 0 else jnp.where(at < count - d, 1.0, 0.0) for d in (1, 2) for s in (-1, 1)]


CORNER = (
    [(1, (k,)) for k in range(6)]
    + [(2, (U,)), (2, (BY,)), (2, (BX,)), (2, (F, A)), (2, (BZ,))]
    + [(3, (U, BY)), (3, (F, A)), (3, (BX, BZ)), (4, (U, BY)), (4, (BX,))]
)


def nearest(shape):
    row = iota(shape, 0)
    return (row < 2) | (row >= 6)


def halo_rows(k, p, ylr, yhr):
    n, side = next((n, pair.index(k)) for n, pair in enumerate(PAIRS) if k in pair)
    above, below = ylr[n * 8 + p], yhr[n * 8 + p]
    first = iota(above.shape, 0) < 4
    if side:
        return pltpu.roll(jnp.where(first, below, above), 4, 0)
    return jnp.where(first, above, below)


def corner_body(ylr, yhr, xcl, xch):
    near = nearest(ylr.shape[1:])
    for out, plane in ((xcl, lambda d: d - 1), (xch, lambda d: 8 - d)):
        for t, (d, fields) in enumerate(CORNER):
            tile = halo_rows(fields[0], plane(d), ylr, yhr)
            if len(fields) == 2:
                tile = jnp.where(near, tile, pltpu.roll(halo_rows(fields[1], plane(d), ylr, yhr), 4, 0))
            out[t] = tile


def corner_rows(k, d, tiles):
    for t, (distance, fields) in enumerate(CORNER):
        if distance == d and k in fields:
            tile = tiles[t]
            if len(fields) == 1:
                return tile
            if fields[1] == k:
                tile = pltpu.roll(tile, 4, 0)
            return jnp.where(nearest(tile.shape), tile, 0.0)
    return jnp.zeros(tiles.shape[1:], F32)


def halves(n):
    row, col = iota((n, n // 2), 0), iota((n, n // 2), 1)
    both = jnp.where(row // 2 == col, 1.0, 0.0).astype(BF16)
    odd = jnp.where(row == 2 * col + 1, 1.0, 0.0).astype(BF16)
    return both, odd


def exact_dot(x, m):
    n = x.shape[0]
    one = x.astype(BF16)
    rest = x - one.astype(F32)
    two = rest.astype(BF16)
    three = (rest - two.astype(F32)).astype(BF16)
    y = jnp.dot(
        jnp.concatenate([one.astype(F32), two.astype(F32), three.astype(F32)], axis=0).astype(BF16),
        m,
        preferred_element_type=F32,
    )
    return (y[2 * n :] + y[n : 2 * n]) + y[:n]


def put(ref, at, x):
    for g in range(x.shape[1] // 128):
        ref[g, at : at + x.shape[0]] = x[:, 128 * g : 128 * g + 128]


def every_other(ref, first, n, width):
    return jnp.concatenate([ref[g, pl.ds(first, n, 2)] for g in range(width // 128)], axis=1)


def below_z(face):
    return jnp.where(iota(face.shape, face.ndim - 1) == 0, 0.0, pltpu.roll(face, 1, face.ndim - 1))


def coarse_body(count, own, xhr, yhr, c1, c2, rows, edge, fine, small):
    nz = own.shape[2]
    both, odd = halves(nz)
    both2, odd2 = halves(nz // 2)

    def even_odd(n):
        return every_other(rows, 0, n, nz), every_other(rows, 1, n, nz)

    def pairs(k):
        for i in range(4):
            put(rows, 8 * i, own[k * 8 + 2 * i] + own[k * 8 + 2 * i + 1])
        return even_odd(16)

    e, o = pairs(A)
    a_in = e + o
    e, o = pairs(BZ)
    bz_in = e + o
    e, o = pairs(BY)
    by_in = o
    for i in range(4):
        put(rows, 8 * i, own[BX * 8 + 2 * i + 1])
    e, o = even_odd(16)
    bx_in = e + o
    put(rows, 0, xhr[BX * H + 3] * beside(count)[0])
    e, o = even_odd(4)
    edge[0:4] = e + o
    for i in range(4):
        edge[4 + i : 5 + i] = yhr[8 + 2 * i, 3:4] + yhr[8 + 2 * i + 1, 3:4]
    out = exact_dot(jnp.concatenate([a_in, bx_in, by_in, edge[...]], axis=0), both)
    a1, bx1, by1, edges = out[0:16] * 0.125, out[16:32] * 0.25, out[32:48] * 0.25, out[48:56] * 0.25
    bz1 = exact_dot(bz_in, odd) * 0.25
    c1[1] = bx1
    c1[2] = by1
    c1[3] = bz1
    fine[0, 0:8] = edges
    fine[1, 0:4] = edges[0:4]
    fine[1, 4:20] = bx1
    lower_x = fine[1, 0:16]
    fine[2, 1:17] = by1
    lower_y = fine[2, 0:16]
    for i in range(4):
        fine[3, 4 * i : 4 * i + 4] = jnp.broadcast_to(fine[0, 4 + i : 5 + i], (4, nz // 2))
    lower_y = jnp.where(iota(lower_y.shape, 0) % 4 == 0, fine[3, 0:16], lower_y)
    c1[0] = a1 + 0.25 * ((bx1 + lower_x) + (by1 + lower_y) + (bz1 + below_z(bz1)))

    def split(x):
        put(rows, 0, x)
        n = x.shape[0] // 2
        return every_other(rows, 0, n, nz // 2), every_other(rows, 1, n, nz // 2)

    def layers(t):
        small[0:8] = t
        top = small[0:2] + small[2:4]
        bottom = small[4:6] + small[6:8]
        return top, bottom

    e, o = split(a1)
    a_t = layers(e + o)
    e, o = split(bz1)
    bz_t = layers(e + o)
    e, o = split(by1)
    by_t = layers(o)
    e, o = split(bx1)
    small[0:8] = e + o
    bx_t = (small[2:4], small[6:8])
    e, o = split(edges)
    small[0:4] = e + o
    small[8:10] = a_t[0]
    small[10:12] = a_t[1]
    small[12:14] = by_t[0]
    small[14:16] = by_t[1]
    small[16:18] = bx_t[0]
    small[18:20] = bx_t[1]
    small[20:24] = small[0:4]
    small[24:26] = bz_t[0]
    small[26:28] = bz_t[1]
    small[28:32] = small[0:4]
    out = exact_dot(small[8:24], both2)
    out_z = exact_dot(small[24:32], odd2)[0:4] * 0.25
    a2, by2, bx2, edges = out[0:4] * 0.125, out[4:8] * 0.25, out[8:12] * 0.25, out[12:16] * 0.25
    w = nz // 4
    c2[4:8] = bx2
    c2[8:12] = by2
    c2[12:16] = out_z
    small[0:2, 0:w] = edges[0:2]
    small[2:6, 0:w] = bx2
    lower_x = small[0:4, 0:w]
    small[8:12, 0:w] = by2
    small[16:20, 0:w] = edges
    small[24:25, 0:w] = small[18:19, 0:w]
    small[25:26, 0:w] = small[8:9, 0:w]
    small[26:27, 0:w] = small[19:20, 0:w]
    small[27:28, 0:w] = small[10:11, 0:w]
    lower_y = small[24:28, 0:w]
    c2[0:4] = a2 + 0.0625 * ((bx2 + lower_x) + (by2 + lower_y) + (out_z + below_z(out_z)))


def set_weights(weights, w, inverse, source, up_x, low_x, up_y, up_z):
    lane = iota(inverse.shape, 1)
    nz = inverse.shape[1]
    weights[0, w] = source * inverse
    weights[1, w] = up_x * inverse
    weights[2, w] = low_x * inverse
    weights[3, w] = up_y * inverse
    weights[4, w] = pltpu.roll(up_y, 1, 0) * inverse
    weights[5, w] = jnp.where(lane == nz - 1, 0.0, up_z) * inverse
    weights[6, w] = jnp.where(lane == 0, 0.0, pltpu.roll(up_z, 1, 1)) * inverse


def relaxed(weights, held, w):
    here = held[w + 1]
    ny, nz = here.shape
    x = weights[1, w] * held[w + 2] + weights[2, w] * held[w]
    y = weights[3, w] * pltpu.roll(here, ny - 1, 0) + weights[4, w] * pltpu.roll(here, 1, 0)
    z = weights[5, w] * pltpu.roll(here, nz - 1, 1) + weights[6, w] * pltpu.roll(here, 1, 1)
    return ((weights[0, w] + x) + (y + z)), here


def coloured(shape):
    parity = (iota(shape, 0) + iota(shape, 1)) % 2
    return [parity == 0, parity == 1]


def smooth(weights, held, first):
    count = weights.shape[1]
    colours = coloured((weights.shape[2], weights.shape[3]))
    for step in range(first, 4):
        for w in range(step, count - step):
            new, here = relaxed(weights, held, w)
            held[w + 1] = jnp.where(colours[(w + step) % 2], new, here)


def fine_body(count, own, xlr, xhr, ylr, yhr, xclr, xchr, c1, out, p1, win, weights, held, diag, rows):
    nz = own.shape[2]
    lower, upper = beside(count)[:2]

    for w in range(16):
        for k in range(6):
            if w < 4:
                mid, halo, there = xhr[k * H + w], corner_rows(k, 4 - w, xchr), lower
            elif w < 12:
                mid, halo, there = own[k * 8 + w - 4], halo_rows(k, w - 4, ylr, yhr), None
            else:
                mid, halo, there = xlr[k * H + w - 12], corner_rows(k, w - 11, xclr), upper
            if there is not None and k in (U, A, BX):
                mid, halo = mid * there, halo * there
            if k == U:
                held[w + 1, 0:8] = mid
                held[w + 1, 8:16] = halo
            else:
                win[k - 1, w + 1, 0:8] = mid
                win[k - 1, w + 1, 8:16] = halo
    zero = jnp.zeros((16, nz), F32)
    held[0] = zero
    held[17] = zero
    win[BX - 1, 0] = zero

    for w in range(16):
        av, bxv, byv, bzv = win[A - 1, w + 1], win[BX - 1, w + 1], win[BY - 1, w + 1], win[BZ - 1, w + 1]
        low_x = win[BX - 1, w]
        total = av + ((bxv + low_x) + (byv + pltpu.roll(byv, 1, 0)) + (bzv + below_z(bzv)))
        inside = av > 0.0
        inverse = jnp.where(inside, 1.0 / jnp.where(inside, total, 1.0), 0.0)
        set_weights(weights, w, inverse, win[F - 1, w + 1], bxv, low_x, byv, bzv)
        diag[w] = total[0:8]
    smooth(weights, held, 0)
    for i in range(4):
        total = None
        for j in range(2):
            w = 4 + 2 * i + j
            new, here = relaxed(weights, held, w)
            out[w - 4] = here[0:8]
            res = diag[w] * (new[0:8] - here[0:8])
            total = res if total is None else total + res
        put(rows, 8 * i, total)
    both, _ = halves(nz)
    p1[0] = exact_dot(every_other(rows, 0, 16, nz) + every_other(rows, 1, 16, nz), both) * 0.125
    for k in range(4):
        p1[1 + k] = c1[k]


def middle_body(count, left, here, right, c2, out, p2, win, weights, held, rows):
    nz = here.shape[3]
    first = iota((8, nz), 0) < 4
    lower, upper = beside(count)[:2]
    zero = jnp.zeros((16, nz), F32)
    win[2, 0] = zero
    colours = coloured((16, nz))
    for b, (source, there) in enumerate(((left, lower), (here, None), (right, upper))):
        for k in range(5):
            for half in range(2):
                at = slice(8 * half, 8 * half + 8)
                below, mid, above = source[0, k, at], source[1, k, at], source[2, k, at]
                if k == 1 and there is not None:
                    below, mid, above = below * there, mid * there, above * there
                w = 4 * b + 2 * half + 1
                win[k, w, 0:8] = jnp.where(first, mid, pltpu.roll(above, 4, 0))
                win[k, w, 8:16] = jnp.where(first, 0.0, pltpu.roll(below, 4, 0))
                win[k, w + 1, 0:8] = jnp.where(first, pltpu.roll(mid, 4, 0), above)
                win[k, w + 1, 8:16] = jnp.where(first, 0.0, below)
    for w in range(12):
        total = win[1, w + 1]
        inside = total > 0.0
        inverse = jnp.where(inside, 0.25 / jnp.where(inside, total, 1.0), 0.0)
        set_weights(weights, w, inverse, 4.0 * win[0, w + 1], win[2, w + 1], win[2, w], win[3, w + 1], win[4, w + 1])
        held[w + 1] = jnp.where(colours[w % 2], weights[0, w], 0.0)
    held[0] = zero
    held[13] = zero
    smooth(weights, held, 1)
    for i in range(2):
        total = None
        for j in range(2):
            w = 4 + 2 * i + j
            new, now = relaxed(weights, held, w)
            out[w - 4] = now[0:4]
            res = win[1, w + 1, 0:8] * (new[0:8] - now[0:8])
            total = res if total is None else total + res
        put(rows, 8 * i, total)
    both, _ = halves(nz)
    coarse = exact_dot(every_other(rows, 0, 8, nz) + every_other(rows, 1, 8, nz), both) * 0.125
    p2[0:2] = coarse[0:2]
    p2[2:4] = coarse[4:6]
    p2[4:20] = c2[...]


def coarse_level_body(count, left, mid, right, down, up, out, win, weights, held):
    win[...] = jnp.zeros(win.shape, F32)
    near = beside(count)
    for k in range(5):
        factor = near if k == 1 else [1.0] * 4
        win[k, 1, 3:5] = left[3, 4 * k + 2 : 4 * k + 4] * factor[2]
        win[k, 8, 3:5] = right[3, 4 * k : 4 * k + 2] * factor[3]
        for i in range(2):
            at = 4 * k + 2 * i
            win[k, 4 + i, 0:1] = down[at + 1 : at + 2]
            win[k, 4 + i, 7:8] = up[at : at + 1]
            for b, (source, there) in enumerate(((left, factor[0]), (mid, 1.0), (right, factor[1]))):
                for j in range(3):
                    win[k, 2 + 2 * b + i, 1 + 2 * j : 3 + 2 * j] = source[j, at : at + 2] * there
    held[0] = jnp.zeros(held.shape[1:], F32)
    held[9] = jnp.zeros(held.shape[1:], F32)
    colours = coloured(held.shape[1:])
    for w in range(8):
        total = win[1, w + 1]
        inside = total > 0.0
        inverse = jnp.where(inside, 0.0625 / jnp.where(inside, total, 1.0), 0.0)
        set_weights(weights, w, inverse, 16.0 * win[0, w + 1], win[2, w + 1], win[2, w], win[3, w + 1], win[4, w + 1])
        held[w + 1] = jnp.where(colours[w % 2], weights[0, w], 0.0)
    smooth(weights, held, 1)
    for i in range(2):
        out[i] = held[4 + i, 3:5]


def along_y(block, by):
    count = lax.axis_size("gy")
    return lax.ppermute(block, "gy", [(i, i + by) for i in range(count) if 0 <= i + by < count])


def round_x(block, by):
    count = lax.axis_size("gx")
    return lax.ppermute(block, "gx", [(i, (i + by) % count) for i in range(count)])


def shape(*dims):
    return jax.ShapeDtypeStruct(dims, F32)


def shards(solution, right_side, alpha, beta_x, beta_y, beta_z):
    args = (solution, right_side, alpha, beta_x, beta_y, beta_z)
    nz = solution.shape[2]
    count = lax.axis_size("gx")
    sent = shape(24, 8, nz)
    own, xl, xh, yl, yh = call(
        pack_body,
        (shape(48, 8, nz),) + (sent,) * 4,
        tuple(pltpu.with_memory_space_constraint(x, pltpu.HBM) for x in args),
        [pltpu.VMEM(x.shape, x.dtype) for x in args] + [pltpu.SemaphoreType.DMA((6,))],
        space=pltpu.HBM,
    )
    ylr, yhr = along_y(yl, -1), along_y(yh, 1)
    xlr, xhr = round_x(xl, -1), round_x(xh, 1)
    xcl, xch = call(corner_body, (shape(len(CORNER), 8, nz),) * 2, (ylr, yhr))
    xclr, xchr = round_x(xcl, -1), round_x(xch, 1)
    c1, c2 = call(
        functools.partial(coarse_body, count),
        (shape(4, 16, nz // 2), shape(16, nz // 4)),
        (own, xhr, yhr),
        [
            pltpu.VMEM((nz // 128, 32, 128), F32),
            pltpu.VMEM((8, nz), F32),
            pltpu.VMEM((4, 24, nz // 2), F32),
            pltpu.VMEM((32, nz // 2), F32),
        ],
    )
    fine, p1 = call(
        functools.partial(fine_body, count),
        (shape(8, 8, nz), shape(5, 16, nz // 2)),
        (own, xlr, xhr, ylr, yhr, xclr, xchr, c1),
        [
            pltpu.VMEM((5, 17, 16, nz), F32),
            pltpu.VMEM((7, 16, 16, nz), F32),
            pltpu.VMEM((18, 16, nz), F32),
            pltpu.VMEM((16, 8, nz), F32),
            pltpu.VMEM((nz // 128, 32, 128), F32),
        ],
        flops=20_000_000,
        nbytes=20_000_000,
    )
    here = jnp.stack([along_y(p1, 1), p1, along_y(p1, -1)])
    left, right = round_x(here, 1), round_x(here, -1)
    middle, p2 = call(
        functools.partial(middle_body, count),
        (shape(4, 4, nz // 2), shape(20, nz // 4)),
        (left, here, right, c2),
        [
            pltpu.VMEM((5, 13, 16, nz // 2), F32),
            pltpu.VMEM((7, 12, 16, nz // 2), F32),
            pltpu.VMEM((14, 16, nz // 2), F32),
            pltpu.VMEM((nz // 256, 16, 128), F32),
        ],
    )
    before, after = round_x(p2, 1), round_x(p2, -1)
    below, above = along_y(p2, 1), along_y(p2, -1)
    down, up = along_y(p2, 2), along_y(p2, -2)
    left = round_x(jnp.stack([below, p2, above, before]), 1)
    right = round_x(jnp.stack([below, p2, above, after]), -1)
    coarse = call(
        functools.partial(coarse_level_body, count),
        shape(2, 2, nz // 4),
        (left, jnp.stack([below, p2, above]), right, down, up),
        [
            pltpu.VMEM((5, 9, 8, nz // 4), F32),
            pltpu.VMEM((7, 8, 8, nz // 4), F32),
            pltpu.VMEM((10, 8, nz // 4), F32),
        ],
    )
    return (fine, middle, coarse)


def solution(mesh):
    placed = P("gx", "gy", None)
    return jax.shard_map(
        shards,
        mesh=mesh,
        in_specs=(placed,) * 6,
        out_specs=(placed,) * 3,
        check_vma=False,
    )
```

```python
import functools

import jax
import jax.numpy as jnp
from jax import lax
from jax.experimental import pallas as pl
from jax.experimental.pallas import tpu as pltpu
from jax.sharding import PartitionSpec as P

F32 = jnp.float32
BF16 = jnp.bfloat16

U, F, A, BX, BY, BZ = range(6)
PAIRS = ((U, F), (A, BY), (BX, BZ))
H = 4


def iota(shape, dim):
    return lax.broadcasted_iota(jnp.int32, shape, dim)


def call(body, outs, args, scratch=(), flops=1_000_000, nbytes=2_000_000, space=pltpu.VMEM, grant=48 << 10):
    vmem = pl.BlockSpec(memory_space=pltpu.VMEM)
    return pl.pallas_call(
        body,
        out_shape=outs,
        in_specs=[pl.BlockSpec(memory_space=space)] * len(args),
        out_specs=jax.tree.map(lambda _: vmem, outs),
        scratch_shapes=list(scratch),
        compiler_params=pltpu.CompilerParams(vmem_limit_bytes=grant << 10),
        cost_estimate=pl.CostEstimate(flops=flops, bytes_accessed=nbytes, transcendentals=0),
    )(*args)


def pair_low(first, second):
    return jnp.where(iota(first.shape, 0) < 4, first, pltpu.roll(second, 4, 0))


def pair_high(first, second):
    return jnp.where(iota(first.shape, 0) >= 4, first, pltpu.roll(second, 4, 0))


def pack_body(u, f, a, bx, by, bz, own, yh, yl, xl, xh, uv, fv, av, bxv, byv, bzv, sems):
    fields = (uv, fv, av, bxv, byv, bzv)
    copies = [pltpu.make_async_copy(src, dst, sems.at[k]) for k, (src, dst) in enumerate(zip((u, f, a, bx, by, bz), fields))]
    for copy in copies:
        copy.start()
    for copy in copies:
        copy.wait()
    cut = bxv[3].astype(F32)
    for k, ref in enumerate(fields):
        for j in range(H):
            low, high = ref[j].astype(F32), ref[4 + j].astype(F32)
            own[k * 8 + j] = low
            own[k * 8 + 4 + j] = high
            if j == 3:
                if k == F:
                    low = low + cut * uv[4]
                elif k == A:
                    low = low + cut
                elif k == BX:
                    low = jnp.zeros_like(low)
            if j == 0:
                if k == F:
                    high = high + cut * uv[3]
                elif k == A:
                    high = high + cut
            xl[k * H + j] = low
            xh[k * H + j] = high
    row = iota(u.shape[1:], 0)
    for p in range(u.shape[0]):
        v = [own[k * 8 + p] for k in range(6)]
        face = v[BY]
        low = list(v)
        low[F] = v[F] + jnp.where(row == 3, face * pltpu.roll(v[U], 7, 0), 0.0)
        low[A] = v[A] + jnp.where(row == 3, face, 0.0)
        low[BY] = jnp.where(row == 3, 0.0, face)
        high = list(v)
        below = pltpu.roll(face, 1, 0)
        high[F] = v[F] + jnp.where(row == 4, below * pltpu.roll(v[U], 1, 0), 0.0)
        high[A] = v[A] + jnp.where(row == 4, below, 0.0)
        for n, (i, j) in enumerate(PAIRS):
            yl[n * 8 + p] = pair_low(low[i], low[j])
            yh[n * 8 + p] = pair_high(high[i], high[j])


def beside(count):
    at = lax.axis_index("gx")
    return [jnp.where(at >= d, 1.0, 0.0) if s < 0 else jnp.where(at < count - d, 1.0, 0.0) for d in (1, 2) for s in (-1, 1)]


CORNER = (
    [(1, (k,)) for k in range(6)]
    + [(2, (U,)), (2, (BY,)), (2, (BX,)), (2, (F, A)), (2, (BZ,))]
    + [(3, (U, BY)), (3, (F, A)), (3, (BX, BZ)), (4, (U, BY)), (4, (BX,))]
)


def nearest(shape):
    row = iota(shape, 0)
    return (row < 2) | (row >= 6)


def halo_rows(k, p, ylr, yhr):
    n, side = next((n, pair.index(k)) for n, pair in enumerate(PAIRS) if k in pair)
    above, below = ylr[n * 8 + p], yhr[n * 8 + p]
    first = iota(above.shape, 0) < 4
    if side:
        return pltpu.roll(jnp.where(first, below, above), 4, 0)
    return jnp.where(first, above, below)


def corner_body(yhr, ylr, xcl, xch):
    near = nearest(ylr.shape[1:])
    for out, plane in ((xcl, lambda d: d - 1), (xch, lambda d: 8 - d)):
        for t, (d, fields) in enumerate(CORNER):
            tile = halo_rows(fields[0], plane(d), ylr, yhr)
            if len(fields) == 2:
                tile = jnp.where(near, tile, pltpu.roll(halo_rows(fields[1], plane(d), ylr, yhr), 4, 0))
            out[t] = tile


def corner_rows(k, d, tiles):
    for t, (distance, fields) in enumerate(CORNER):
        if distance == d and k in fields:
            tile = tiles[t]
            if len(fields) == 1:
                return tile
            if fields[1] == k:
                tile = pltpu.roll(tile, 4, 0)
            return jnp.where(nearest(tile.shape), tile, 0.0)
    return jnp.zeros(tiles.shape[1:], F32)


def halves(n):
    row, col = iota((n, n // 2), 0), iota((n, n // 2), 1)
    both = jnp.where(row // 2 == col, 1.0, 0.0).astype(BF16)
    odd = jnp.where(row == 2 * col + 1, 1.0, 0.0).astype(BF16)
    return both, odd


def exact_dot(x, m):
    n = x.shape[0]
    one = x.astype(BF16)
    rest = x - one.astype(F32)
    two = rest.astype(BF16)
    three = (rest - two.astype(F32)).astype(BF16)
    y = jnp.dot(
        jnp.concatenate([one.astype(F32), two.astype(F32), three.astype(F32)], axis=0).astype(BF16),
        m,
        preferred_element_type=F32,
    )
    return (y[2 * n :] + y[n : 2 * n]) + y[:n]


def put(ref, at, x):
    for g in range(x.shape[1] // 128):
        ref[g, at : at + x.shape[0]] = x[:, 128 * g : 128 * g + 128]


def every_other(ref, first, n, width):
    return jnp.concatenate([ref[g, pl.ds(first, n, 2)] for g in range(width // 128)], axis=1)


def below_z(face):
    return jnp.where(iota(face.shape, face.ndim - 1) == 0, 0.0, pltpu.roll(face, 1, face.ndim - 1))


def coarse_body(count, own, xhr, yhr, c1, c2, rows, edge, fine, small):
    nz = own.shape[2]
    both, odd = halves(nz)
    both2, odd2 = halves(nz // 2)

    def even_odd(n):
        return every_other(rows, 0, n, nz), every_other(rows, 1, n, nz)

    def pairs(k):
        for i in range(4):
            put(rows, 8 * i, own[k * 8 + 2 * i] + own[k * 8 + 2 * i + 1])
        return even_odd(16)

    e, o = pairs(A)
    a_in = e + o
    e, o = pairs(BZ)
    bz_in = e + o
    e, o = pairs(BY)
    by_in = o
    for i in range(4):
        put(rows, 8 * i, own[BX * 8 + 2 * i + 1])
    e, o = even_odd(16)
    bx_in = e + o
    put(rows, 0, xhr[BX * H + 3] * beside(count)[0])
    e, o = even_odd(4)
    edge[0:4] = e + o
    for i in range(4):
        edge[4 + i : 5 + i] = yhr[8 + 2 * i, 3:4] + yhr[8 + 2 * i + 1, 3:4]
    out = exact_dot(jnp.concatenate([a_in, bx_in, by_in, edge[...]], axis=0), both)
    a1, bx1, by1, edges = out[0:16] * 0.125, out[16:32] * 0.25, out[32:48] * 0.25, out[48:56] * 0.25
    bz1 = exact_dot(bz_in, odd) * 0.25
    c1[1] = bx1
    c1[2] = by1
    c1[3] = bz1
    fine[0, 0:8] = edges
    fine[1, 0:4] = edges[0:4]
    fine[1, 4:20] = bx1
    lower_x = fine[1, 0:16]
    fine[2, 1:17] = by1
    lower_y = fine[2, 0:16]
    for i in range(4):
        fine[3, 4 * i : 4 * i + 4] = jnp.broadcast_to(fine[0, 4 + i : 5 + i], (4, nz // 2))
    lower_y = jnp.where(iota(lower_y.shape, 0) % 4 == 0, fine[3, 0:16], lower_y)
    c1[0] = a1 + 0.25 * ((bx1 + lower_x) + (by1 + lower_y) + (bz1 + below_z(bz1)))

    def split(x):
        put(rows, 0, x)
        n = x.shape[0] // 2
        return every_other(rows, 0, n, nz // 2), every_other(rows, 1, n, nz // 2)

    def layers(t):
        small[0:8] = t
        top = small[0:2] + small[2:4]
        bottom = small[4:6] + small[6:8]
        return top, bottom

    e, o = split(a1)
    a_t = layers(e + o)
    e, o = split(bz1)
    bz_t = layers(e + o)
    e, o = split(by1)
    by_t = layers(o)
    e, o = split(bx1)
    small[0:8] = e + o
    bx_t = (small[2:4], small[6:8])
    e, o = split(edges)
    small[0:4] = e + o
    small[8:10] = a_t[0]
    small[10:12] = a_t[1]
    small[12:14] = by_t[0]
    small[14:16] = by_t[1]
    small[16:18] = bx_t[0]
    small[18:20] = bx_t[1]
    small[20:24] = small[0:4]
    small[24:26] = bz_t[0]
    small[26:28] = bz_t[1]
    small[28:32] = small[0:4]
    out = exact_dot(small[8:24], both2)
    out_z = exact_dot(small[24:32], odd2)[0:4] * 0.25
    a2, by2, bx2, edges = out[0:4] * 0.125, out[4:8] * 0.25, out[8:12] * 0.25, out[12:16] * 0.25
    w = nz // 4
    c2[4:8] = bx2
    c2[8:12] = by2
    c2[12:16] = out_z
    small[0:2, 0:w] = edges[0:2]
    small[2:6, 0:w] = bx2
    lower_x = small[0:4, 0:w]
    small[8:12, 0:w] = by2
    small[16:20, 0:w] = edges
    small[24:25, 0:w] = small[18:19, 0:w]
    small[25:26, 0:w] = small[8:9, 0:w]
    small[26:27, 0:w] = small[19:20, 0:w]
    small[27:28, 0:w] = small[10:11, 0:w]
    lower_y = small[24:28, 0:w]
    c2[0:4] = a2 + 0.0625 * ((bx2 + lower_x) + (by2 + lower_y) + (out_z + below_z(out_z)))


def set_weights(weights, w, inverse, source, up_x, low_x, up_y, up_z):
    lane = iota(inverse.shape, 1)
    nz = inverse.shape[1]
    weights[0, w] = source * inverse
    weights[1, w] = up_x * inverse
    weights[2, w] = low_x * inverse
    weights[3, w] = up_y * inverse
    weights[4, w] = pltpu.roll(up_y, 1, 0) * inverse
    weights[5, w] = jnp.where(lane == nz - 1, 0.0, up_z) * inverse
    weights[6, w] = jnp.where(lane == 0, 0.0, pltpu.roll(up_z, 1, 1)) * inverse


def relaxed(weights, held, w):
    here = held[w + 1]
    ny, nz = here.shape
    x = weights[1, w] * held[w + 2] + weights[2, w] * held[w]
    y = weights[3, w] * pltpu.roll(here, ny - 1, 0) + weights[4, w] * pltpu.roll(here, 1, 0)
    z = weights[5, w] * pltpu.roll(here, nz - 1, 1) + weights[6, w] * pltpu.roll(here, 1, 1)
    return ((weights[0, w] + x) + (y + z)), here


def coloured(shape):
    parity = (iota(shape, 0) + iota(shape, 1)) % 2
    return [parity == 0, parity == 1]


def smooth(weights, held, first):
    count = weights.shape[1]
    colours = coloured((weights.shape[2], weights.shape[3]))
    for step in range(first, 4):
        for w in range(step, count - step):
            new, here = relaxed(weights, held, w)
            held[w + 1] = jnp.where(colours[(w + step) % 2], new, here)


def fine_body(count, own, xlr, xhr, yhr, ylr, xclr, xchr, c1, out, p1, win, weights, held, diag, rows):
    nz = own.shape[2]
    lower, upper = beside(count)[:2]

    for w in range(16):
        for k in range(6):
            if w < 4:
                mid, halo, there = xhr[k * H + w], corner_rows(k, 4 - w, xchr), lower
            elif w < 12:
                mid, halo, there = own[k * 8 + w - 4], halo_rows(k, w - 4, ylr, yhr), None
            else:
                mid, halo, there = xlr[k * H + w - 12], corner_rows(k, w - 11, xclr), upper
            if there is not None and k in (U, A, BX):
                mid, halo = mid * there, halo * there
            if k == U:
                held[w + 1, 0:8] = mid
                held[w + 1, 8:16] = halo
            else:
                win[k - 1, w + 1, 0:8] = mid
                win[k - 1, w + 1, 8:16] = halo
    zero = jnp.zeros((16, nz), F32)
    held[0] = zero
    held[17] = zero
    win[BX - 1, 0] = zero

    for w in range(16):
        av, bxv, byv, bzv = win[A - 1, w + 1], win[BX - 1, w + 1], win[BY - 1, w + 1], win[BZ - 1, w + 1]
        low_x = win[BX - 1, w]
        total = av + ((bxv + low_x) + (byv + pltpu.roll(byv, 1, 0)) + (bzv + below_z(bzv)))
        inside = av > 0.0
        inverse = jnp.where(inside, 1.0 / jnp.where(inside, total, 1.0), 0.0)
        set_weights(weights, w, inverse, win[F - 1, w + 1], bxv, low_x, byv, bzv)
        diag[w] = total[0:8]
    smooth(weights, held, 0)
    for i in range(4):
        total = None
        for j in range(2):
            w = 4 + 2 * i + j
            new, here = relaxed(weights, held, w)
            out[w - 4] = here[0:8]
            res = diag[w] * (new[0:8] - here[0:8])
            total = res if total is None else total + res
        put(rows, 8 * i, total)
    both, _ = halves(nz)
    p1[0] = exact_dot(every_other(rows, 0, 16, nz) + every_other(rows, 1, 16, nz), both) * 0.125
    for k in range(4):
        p1[1 + k] = c1[k]


def middle_body(count, left, here, right, c2, out, p2, win, weights, held, rows):
    nz = here.shape[3]
    first = iota((8, nz), 0) < 4
    lower, upper = beside(count)[:2]
    zero = jnp.zeros((16, nz), F32)
    win[2, 0] = zero
    colours = coloured((16, nz))
    for b, (source, there) in enumerate(((left, lower), (here, None), (right, upper))):
        for k in range(5):
            for half in range(2):
                at = slice(8 * half, 8 * half + 8)
                above, mid, below = source[0, k, at], source[1, k, at], source[2, k, at]
                if k == 1 and there is not None:
                    below, mid, above = below * there, mid * there, above * there
                w = 4 * b + 2 * half + 1
                win[k, w, 0:8] = jnp.where(first, mid, pltpu.roll(above, 4, 0))
                win[k, w, 8:16] = jnp.where(first, 0.0, pltpu.roll(below, 4, 0))
                win[k, w + 1, 0:8] = jnp.where(first, pltpu.roll(mid, 4, 0), above)
                win[k, w + 1, 8:16] = jnp.where(first, 0.0, below)
    for w in range(12):
        total = win[1, w + 1]
        inside = total > 0.0
        inverse = jnp.where(inside, 0.25 / jnp.where(inside, total, 1.0), 0.0)
        set_weights(weights, w, inverse, 4.0 * win[0, w + 1], win[2, w + 1], win[2, w], win[3, w + 1], win[4, w + 1])
        held[w + 1] = jnp.where(colours[w % 2], weights[0, w], 0.0)
    held[0] = zero
    held[13] = zero
    smooth(weights, held, 1)
    for i in range(2):
        total = None
        for j in range(2):
            w = 4 + 2 * i + j
            new, now = relaxed(weights, held, w)
            out[w - 4] = now[0:4]
            res = win[1, w + 1, 0:8] * (new[0:8] - now[0:8])
            total = res if total is None else total + res
        put(rows, 8 * i, total)
    both, _ = halves(nz)
    coarse = exact_dot(every_other(rows, 0, 8, nz) + every_other(rows, 1, 8, nz), both) * 0.125
    p2[0:2] = coarse[0:2]
    p2[2:4] = coarse[4:6]
    p2[4:20] = c2[...]


def coarse_level_body(count, left, mid, right, down, up, out, win, weights, held):
    win[...] = jnp.zeros(win.shape, F32)
    near = beside(count)
    for k in range(5):
        factor = near if k == 1 else [1.0] * 4
        win[k, 1, 3:5] = left[3, 4 * k + 2 : 4 * k + 4] * factor[2]
        win[k, 8, 3:5] = right[3, 4 * k : 4 * k + 2] * factor[3]
        for i in range(2):
            at = 4 * k + 2 * i
            win[k, 4 + i, 0:1] = down[at + 1 : at + 2]
            win[k, 4 + i, 7:8] = up[at : at + 1]
            for b, (source, there) in enumerate(((left, factor[0]), (mid, 1.0), (right, factor[1]))):
                for j in range(3):
                    win[k, 2 + 2 * b + i, 1 + 2 * j : 3 + 2 * j] = source[2 - j, at : at + 2] * there
    held[0] = jnp.zeros(held.shape[1:], F32)
    held[9] = jnp.zeros(held.shape[1:], F32)
    colours = coloured(held.shape[1:])
    for w in range(8):
        total = win[1, w + 1]
        inside = total > 0.0
        inverse = jnp.where(inside, 0.0625 / jnp.where(inside, total, 1.0), 0.0)
        set_weights(weights, w, inverse, 16.0 * win[0, w + 1], win[2, w + 1], win[2, w], win[3, w + 1], win[4, w + 1])
        held[w + 1] = jnp.where(colours[w % 2], weights[0, w], 0.0)
    smooth(weights, held, 1)
    for i in range(2):
        out[i] = held[4 + i, 3:5]


def along_y(block, by):
    count = lax.axis_size("gy")
    return lax.ppermute(block, "gy", [(i, i + by) for i in range(count) if 0 <= i + by < count])


def round_x(block, by):
    count = lax.axis_size("gx")
    return lax.ppermute(block, "gx", [(i, (i + by) % count) for i in range(count)])


def shape(*dims):
    return jax.ShapeDtypeStruct(dims, F32)


def shards(solution, right_side, alpha, beta_x, beta_y, beta_z):
    args = (solution, right_side, alpha, beta_x, beta_y, beta_z)
    nz = solution.shape[2]
    count = lax.axis_size("gx")
    sent = shape(24, 8, nz)
    own, yh, yl, xl, xh = call(
        pack_body,
        (shape(48, 8, nz),) + (sent,) * 4,
        tuple(pltpu.with_memory_space_constraint(x, pltpu.HBM) for x in args),
        [pltpu.VMEM(x.shape, x.dtype) for x in args] + [pltpu.SemaphoreType.DMA((6,))],
        space=pltpu.HBM,
    )
    yhr, ylr = along_y(yh, 1), along_y(yl, -1)
    xlr, xhr = round_x(xl, -1), round_x(xh, 1)
    xcl, xch = call(corner_body, (shape(len(CORNER), 8, nz),) * 2, (yhr, ylr))
    xclr, xchr = round_x(xcl, -1), round_x(xch, 1)
    c1, c2 = call(
        functools.partial(coarse_body, count),
        (shape(4, 16, nz // 2), shape(16, nz // 4)),
        (own, xhr, yhr),
        [
            pltpu.VMEM((nz // 128, 32, 128), F32),
            pltpu.VMEM((8, nz), F32),
            pltpu.VMEM((4, 24, nz // 2), F32),
            pltpu.VMEM((32, nz // 2), F32),
        ],
    )
    fine, p1 = call(
        functools.partial(fine_body, count),
        (shape(8, 8, nz), shape(5, 16, nz // 2)),
        (own, xlr, xhr, yhr, ylr, xclr, xchr, c1),
        [
            pltpu.VMEM((5, 17, 16, nz), F32),
            pltpu.VMEM((7, 16, 16, nz), F32),
            pltpu.VMEM((18, 16, nz), F32),
            pltpu.VMEM((16, 8, nz), F32),
            pltpu.VMEM((nz // 128, 32, 128), F32),
        ],
        flops=20_000_000,
        nbytes=20_000_000,
    )
    above, below = along_y(p1, -1), along_y(p1, 1)
    here = jnp.stack([above, p1, below])
    left, right = round_x(here, 1), round_x(here, -1)
    middle, p2 = call(
        functools.partial(middle_body, count),
        (shape(4, 4, nz // 2), shape(20, nz // 4)),
        (left, here, right, c2),
        [
            pltpu.VMEM((5, 13, 16, nz // 2), F32),
            pltpu.VMEM((7, 12, 16, nz // 2), F32),
            pltpu.VMEM((14, 16, nz // 2), F32),
            pltpu.VMEM((nz // 256, 16, 128), F32),
        ],
    )
    before, after = round_x(p2, 1), round_x(p2, -1)
    above, below = along_y(p2, -1), along_y(p2, 1)
    down, up = along_y(p2, 2), along_y(p2, -2)
    left = round_x(jnp.stack([above, p2, below, before]), 1)
    right = round_x(jnp.stack([above, p2, below, after]), -1)
    coarse = call(
        functools.partial(coarse_level_body, count),
        shape(2, 2, nz // 4),
        (left, jnp.stack([above, p2, below]), right, down, up),
        [
            pltpu.VMEM((5, 9, 8, nz // 4), F32),
            pltpu.VMEM((7, 8, 8, nz // 4), F32),
            pltpu.VMEM((10, 8, nz // 4), F32),
        ],
    )
    return (fine, middle, coarse)


def solution(mesh):
    placed = P("gx", "gy", None)
    return jax.shard_map(
        shards,
        mesh=mesh,
        in_specs=(placed,) * 6,
        out_specs=(placed,) * 3,
        check_vma=False,
    )
```

```python
import functools

import jax
import jax.numpy as jnp
from jax import lax
from jax.experimental import pallas as pl
from jax.experimental.pallas import tpu as pltpu
from jax.sharding import PartitionSpec as P

F32 = jnp.float32
BF16 = jnp.bfloat16

U, F, A, BX, BY, BZ = range(6)
PAIRS = ((U, F), (A, BY), (BX, BZ))
H = 4


def iota(shape, dim):
    return lax.broadcasted_iota(jnp.int32, shape, dim)


def call(body, outs, args, scratch=(), flops=1_000_000, nbytes=2_000_000, space=pltpu.VMEM, grant=48 << 10):
    vmem = pl.BlockSpec(memory_space=pltpu.VMEM)
    return pl.pallas_call(
        body,
        out_shape=outs,
        in_specs=[pl.BlockSpec(memory_space=space)] * len(args),
        out_specs=jax.tree.map(lambda _: vmem, outs),
        scratch_shapes=list(scratch),
        compiler_params=pltpu.CompilerParams(vmem_limit_bytes=grant << 10),
        cost_estimate=pl.CostEstimate(flops=flops, bytes_accessed=nbytes, transcendentals=0),
    )(*args)


def pair_low(first, second):
    return jnp.where(iota(first.shape, 0) < 4, first, pltpu.roll(second, 4, 0))


def pair_high(first, second):
    return jnp.where(iota(first.shape, 0) >= 4, first, pltpu.roll(second, 4, 0))


def pack_body(u, f, a, bx, by, bz, own, yh, yl, xl, xh, uv, fv, av, bxv, byv, bzv, sems):
    fields = (uv, fv, av, bxv, byv, bzv)
    copies = [pltpu.make_async_copy(src, dst, sems.at[k]) for k, (src, dst) in enumerate(zip((u, f, a, bx, by, bz), fields))]
    for copy in copies:
        copy.start()
    for copy in copies:
        copy.wait()
    cut = bxv[3].astype(F32)
    for k, ref in enumerate(fields):
        for j in range(H):
            low, high = ref[j].astype(F32), ref[4 + j].astype(F32)
            own[k * 8 + j] = low
            own[k * 8 + 4 + j] = high
            if j == 3:
                if k == F:
                    low = low + cut * uv[4]
                elif k == A:
                    low = low + cut
                elif k == BX:
                    low = jnp.zeros_like(low)
            if j == 0:
                if k == F:
                    high = high + cut * uv[3]
                elif k == A:
                    high = high + cut
            xl[k * H + j] = low
            xh[k * H + j] = high
    row = iota(u.shape[1:], 0)
    for p in range(u.shape[0]):
        v = [own[k * 8 + p] for k in range(6)]
        face = v[BY]
        low = list(v)
        low[F] = v[F] + jnp.where(row == 3, face * pltpu.roll(v[U], 7, 0), 0.0)
        low[A] = v[A] + jnp.where(row == 3, face, 0.0)
        low[BY] = jnp.where(row == 3, 0.0, face)
        high = list(v)
        below = pltpu.roll(face, 1, 0)
        high[F] = v[F] + jnp.where(row == 4, below * pltpu.roll(v[U], 1, 0), 0.0)
        high[A] = v[A] + jnp.where(row == 4, below, 0.0)
        for n, (i, j) in enumerate(PAIRS):
            yl[n * 8 + p] = pair_low(low[i], low[j])
            yh[n * 8 + p] = pair_high(high[i], high[j])


def beside(count):
    at = lax.axis_index("gx")
    return [jnp.where(at >= d, 1.0, 0.0) if s < 0 else jnp.where(at < count - d, 1.0, 0.0) for d in (1, 2) for s in (-1, 1)]


CORNER = (
    [(1, (k,)) for k in range(6)]
    + [(2, (U,)), (2, (BY,)), (2, (BX,)), (2, (F, A)), (2, (BZ,))]
    + [(3, (U, BY)), (3, (F, A)), (3, (BX, BZ)), (4, (U, BY)), (4, (BX,))]
)


def nearest(shape):
    row = iota(shape, 0)
    return (row < 2) | (row >= 6)


def halo_rows(k, p, ylr, yhr):
    n, side = next((n, pair.index(k)) for n, pair in enumerate(PAIRS) if k in pair)
    above, below = ylr[n * 8 + p], yhr[n * 8 + p]
    first = iota(above.shape, 0) < 4
    if side:
        return pltpu.roll(jnp.where(first, below, above), 4, 0)
    return jnp.where(first, above, below)


def corner_body(yhr, ylr, xcl, xch):
    near = nearest(ylr.shape[1:])
    for out, plane in ((xcl, lambda d: d - 1), (xch, lambda d: 8 - d)):
        for t, (d, fields) in enumerate(CORNER):
            tile = halo_rows(fields[0], plane(d), ylr, yhr)
            if len(fields) == 2:
                tile = jnp.where(near, tile, pltpu.roll(halo_rows(fields[1], plane(d), ylr, yhr), 4, 0))
            out[t] = tile


def corner_rows(k, d, tiles):
    for t, (distance, fields) in enumerate(CORNER):
        if distance == d and k in fields:
            tile = tiles[t]
            if len(fields) == 1:
                return tile
            if fields[1] == k:
                tile = pltpu.roll(tile, 4, 0)
            return jnp.where(nearest(tile.shape), tile, 0.0)
    return jnp.zeros(tiles.shape[1:], F32)


def halves(n):
    row, col = iota((n, n // 2), 0), iota((n, n // 2), 1)
    both = jnp.where(row // 2 == col, 1.0, 0.0).astype(BF16)
    odd = jnp.where(row == 2 * col + 1, 1.0, 0.0).astype(BF16)
    return both, odd


def exact_dot(x, m):
    n = x.shape[0]
    one = x.astype(BF16)
    rest = x - one.astype(F32)
    two = rest.astype(BF16)
    three = (rest - two.astype(F32)).astype(BF16)
    y = jnp.dot(
        jnp.concatenate([one.astype(F32), two.astype(F32), three.astype(F32)], axis=0).astype(BF16),
        m,
        preferred_element_type=F32,
    )
    return (y[2 * n :] + y[n : 2 * n]) + y[:n]


def put(ref, at, x):
    for g in range(x.shape[1] // 128):
        ref[g, at : at + x.shape[0]] = x[:, 128 * g : 128 * g + 128]


def every_other(ref, first, n, width):
    return jnp.concatenate([ref[g, pl.ds(first, n, 2)] for g in range(width // 128)], axis=1)


def below_z(face):
    return jnp.where(iota(face.shape, face.ndim - 1) == 0, 0.0, pltpu.roll(face, 1, face.ndim - 1))


def coarse_body(count, own, xhr, yhr, c1, c2, rows, edge, fine, small):
    nz = own.shape[2]
    both, odd = halves(nz)
    both2, odd2 = halves(nz // 2)

    def even_odd(n):
        return every_other(rows, 0, n, nz), every_other(rows, 1, n, nz)

    def pairs(k):
        for i in range(4):
            put(rows, 8 * i, own[k * 8 + 2 * i] + own[k * 8 + 2 * i + 1])
        return even_odd(16)

    e, o = pairs(A)
    a_in = e + o
    e, o = pairs(BZ)
    bz_in = e + o
    e, o = pairs(BY)
    by_in = o
    for i in range(4):
        put(rows, 8 * i, own[BX * 8 + 2 * i + 1])
    e, o = even_odd(16)
    bx_in = e + o
    put(rows, 0, xhr[BX * H + 3] * beside(count)[0])
    e, o = even_odd(4)
    edge[0:4] = e + o
    for i in range(4):
        edge[4 + i : 5 + i] = yhr[8 + 2 * i, 3:4] + yhr[8 + 2 * i + 1, 3:4]
    out = exact_dot(jnp.concatenate([a_in, bx_in, by_in, edge[...]], axis=0), both)
    a1, bx1, by1, edges = out[0:16] * 0.125, out[16:32] * 0.25, out[32:48] * 0.25, out[48:56] * 0.25
    bz1 = exact_dot(bz_in, odd) * 0.25
    c1[1] = bx1
    c1[2] = by1
    c1[3] = bz1
    fine[0, 0:8] = edges
    fine[1, 0:4] = edges[0:4]
    fine[1, 4:20] = bx1
    lower_x = fine[1, 0:16]
    fine[2, 1:17] = by1
    lower_y = fine[2, 0:16]
    for i in range(4):
        fine[3, 4 * i : 4 * i + 4] = jnp.broadcast_to(fine[0, 4 + i : 5 + i], (4, nz // 2))
    lower_y = jnp.where(iota(lower_y.shape, 0) % 4 == 0, fine[3, 0:16], lower_y)
    c1[0] = a1 + 0.25 * ((bx1 + lower_x) + (by1 + lower_y) + (bz1 + below_z(bz1)))

    def split(x):
        put(rows, 0, x)
        n = x.shape[0] // 2
        return every_other(rows, 0, n, nz // 2), every_other(rows, 1, n, nz // 2)

    def layers(t):
        small[0:8] = t
        top = small[0:2] + small[2:4]
        bottom = small[4:6] + small[6:8]
        return top, bottom

    e, o = split(a1)
    a_t = layers(e + o)
    e, o = split(bz1)
    bz_t = layers(e + o)
    e, o = split(by1)
    by_t = layers(o)
    e, o = split(bx1)
    small[0:8] = e + o
    bx_t = (small[2:4], small[6:8])
    e, o = split(edges)
    small[0:4] = e + o
    small[8:10] = a_t[0]
    small[10:12] = a_t[1]
    small[12:14] = by_t[0]
    small[14:16] = by_t[1]
    small[16:18] = bx_t[0]
    small[18:20] = bx_t[1]
    small[20:24] = small[0:4]
    small[24:26] = bz_t[0]
    small[26:28] = bz_t[1]
    small[28:32] = small[0:4]
    out = exact_dot(small[8:24], both2)
    out_z = exact_dot(small[24:32], odd2)[0:4] * 0.25
    a2, by2, bx2, edges = out[0:4] * 0.125, out[4:8] * 0.25, out[8:12] * 0.25, out[12:16] * 0.25
    w = nz // 4
    c2[4:8] = bx2
    c2[8:12] = by2
    c2[12:16] = out_z
    small[0:2, 0:w] = edges[0:2]
    small[2:6, 0:w] = bx2
    lower_x = small[0:4, 0:w]
    small[8:12, 0:w] = by2
    small[16:20, 0:w] = edges
    small[24:25, 0:w] = small[18:19, 0:w]
    small[25:26, 0:w] = small[8:9, 0:w]
    small[26:27, 0:w] = small[19:20, 0:w]
    small[27:28, 0:w] = small[10:11, 0:w]
    lower_y = small[24:28, 0:w]
    c2[0:4] = a2 + 0.0625 * ((bx2 + lower_x) + (by2 + lower_y) + (out_z + below_z(out_z)))


def set_weights(weights, w, inverse, source, up_x, low_x, up_y, up_z):
    lane = iota(inverse.shape, 1)
    nz = inverse.shape[1]
    weights[0, w] = source * inverse
    weights[1, w] = up_x * inverse
    weights[2, w] = low_x * inverse
    weights[3, w] = up_y * inverse
    weights[4, w] = pltpu.roll(up_y, 1, 0) * inverse
    weights[5, w] = jnp.where(lane == nz - 1, 0.0, up_z) * inverse
    weights[6, w] = jnp.where(lane == 0, 0.0, pltpu.roll(up_z, 1, 1)) * inverse


def relaxed(weights, held, w):
    here = held[w + 1]
    ny, nz = here.shape
    x = weights[1, w] * held[w + 2] + weights[2, w] * held[w]
    y = weights[3, w] * pltpu.roll(here, ny - 1, 0) + weights[4, w] * pltpu.roll(here, 1, 0)
    z = weights[5, w] * pltpu.roll(here, nz - 1, 1) + weights[6, w] * pltpu.roll(here, 1, 1)
    return ((weights[0, w] + x) + (y + z)), here


def coloured(shape):
    parity = (iota(shape, 0) + iota(shape, 1)) % 2
    return [parity == 0, parity == 1]


def smooth(weights, held, first):
    count = weights.shape[1]
    colours = coloured((weights.shape[2], weights.shape[3]))
    for step in range(first, 4):
        for w in range(step, count - step):
            new, here = relaxed(weights, held, w)
            held[w + 1] = jnp.where(colours[(w + step) % 2], new, here)


def fine_body(count, own, xlr, xhr, yhr, ylr, xclr, xchr, c1, out, p1, win, weights, held, diag, rows):
    nz = own.shape[2]
    lower, upper = beside(count)[:2]

    for w in range(16):
        for k in range(6):
            if w < 4:
                mid, halo, there = xhr[k * H + w], corner_rows(k, 4 - w, xchr), lower
            elif w < 12:
                mid, halo, there = own[k * 8 + w - 4], halo_rows(k, w - 4, ylr, yhr), None
            else:
                mid, halo, there = xlr[k * H + w - 12], corner_rows(k, w - 11, xclr), upper
            if there is not None and k in (U, A, BX):
                mid, halo = mid * there, halo * there
            if k == U:
                held[w + 1, 0:8] = mid
                held[w + 1, 8:16] = halo
            else:
                win[k - 1, w + 1, 0:8] = mid
                win[k - 1, w + 1, 8:16] = halo
    zero = jnp.zeros((16, nz), F32)
    held[0] = zero
    held[17] = zero
    win[BX - 1, 0] = zero

    for w in range(16):
        av, bxv, byv, bzv = win[A - 1, w + 1], win[BX - 1, w + 1], win[BY - 1, w + 1], win[BZ - 1, w + 1]
        low_x = win[BX - 1, w]
        total = av + ((bxv + low_x) + (byv + pltpu.roll(byv, 1, 0)) + (bzv + below_z(bzv)))
        inside = av > 0.0
        inverse = jnp.where(inside, 1.0 / jnp.where(inside, total, 1.0), 0.0)
        set_weights(weights, w, inverse, win[F - 1, w + 1], bxv, low_x, byv, bzv)
        diag[w] = total[0:8]
    smooth(weights, held, 0)
    for i in range(4):
        total = None
        for j in range(2):
            w = 4 + 2 * i + j
            new, here = relaxed(weights, held, w)
            out[w - 4] = here[0:8]
            res = diag[w] * (new[0:8] - here[0:8])
            total = res if total is None else total + res
        put(rows, 8 * i, total)
    both, _ = halves(nz)
    p1[0] = exact_dot(every_other(rows, 0, 16, nz) + every_other(rows, 1, 16, nz), both) * 0.125
    for k in range(4):
        p1[1 + k] = c1[k]


def middle_body(count, left, here, right, c2, out, p2, win, weights, held, rows):
    nz = here.shape[3]
    first = iota((8, nz), 0) < 4
    lower, upper = beside(count)[:2]
    zero = jnp.zeros((16, nz), F32)
    win[2, 0] = zero
    colours = coloured((16, nz))
    for b, (source, there) in enumerate(((left, lower), (here, None), (right, upper))):
        for k in range(5):
            for half in range(2):
                at = slice(8 * half, 8 * half + 8)
                above, mid, below = source[0, k, at], source[1, k, at], source[2, k, at]
                if k == 1 and there is not None:
                    below, mid, above = below * there, mid * there, above * there
                w = 4 * b + 2 * half + 1
                win[k, w, 0:8] = jnp.where(first, mid, pltpu.roll(above, 4, 0))
                win[k, w, 8:16] = jnp.where(first, 0.0, pltpu.roll(below, 4, 0))
                win[k, w + 1, 0:8] = jnp.where(first, pltpu.roll(mid, 4, 0), above)
                win[k, w + 1, 8:16] = jnp.where(first, 0.0, below)
    for w in range(12):
        total = win[1, w + 1]
        inside = total > 0.0
        inverse = jnp.where(inside, 0.25 / jnp.where(inside, total, 1.0), 0.0)
        set_weights(weights, w, inverse, 4.0 * win[0, w + 1], win[2, w + 1], win[2, w], win[3, w + 1], win[4, w + 1])
        held[w + 1] = jnp.where(colours[w % 2], weights[0, w], 0.0)
    held[0] = zero
    held[13] = zero
    smooth(weights, held, 1)
    for i in range(2):
        total = None
        for j in range(2):
            w = 4 + 2 * i + j
            new, now = relaxed(weights, held, w)
            out[w - 4] = now[0:4]
            res = win[1, w + 1, 0:8] * (new[0:8] - now[0:8])
            total = res if total is None else total + res
        put(rows, 8 * i, total)
    both, _ = halves(nz)
    coarse = exact_dot(every_other(rows, 0, 8, nz) + every_other(rows, 1, 8, nz), both) * 0.125
    p2[0:2] = coarse[0:2]
    p2[2:4] = coarse[4:6]
    p2[4:20] = c2[...]


def coarse_level_body(count, left, mid, right, down, up, out, win, weights, held):
    win[...] = jnp.zeros(win.shape, F32)
    near = beside(count)
    for k in range(5):
        factor = near if k == 1 else [1.0] * 4
        win[k, 1, 3:5] = left[3, 4 * k + 2 : 4 * k + 4] * factor[2]
        win[k, 8, 3:5] = right[3, 4 * k : 4 * k + 2] * factor[3]
        for i in range(2):
            at = 4 * k + 2 * i
            win[k, 4 + i, 0:1] = down[at + 1 : at + 2]
            win[k, 4 + i, 7:8] = up[at : at + 1]
            for b, (source, there) in enumerate(((left, factor[0]), (mid, 1.0), (right, factor[1]))):
                for j in range(3):
                    win[k, 2 + 2 * b + i, 1 + 2 * j : 3 + 2 * j] = source[j, at : at + 2] * there
    held[0] = jnp.zeros(held.shape[1:], F32)
    held[9] = jnp.zeros(held.shape[1:], F32)
    colours = coloured(held.shape[1:])
    for w in range(8):
        total = win[1, w + 1]
        inside = total > 0.0
        inverse = jnp.where(inside, 0.0625 / jnp.where(inside, total, 1.0), 0.0)
        set_weights(weights, w, inverse, 16.0 * win[0, w + 1], win[2, w + 1], win[2, w], win[3, w + 1], win[4, w + 1])
        held[w + 1] = jnp.where(colours[w % 2], weights[0, w], 0.0)
    smooth(weights, held, 1)
    for i in range(2):
        out[i] = held[4 + i, 3:5]


def along_y(block, by):
    count = lax.axis_size("gy")
    return lax.ppermute(block, "gy", [(i, i + by) for i in range(count) if 0 <= i + by < count])


def round_x(block, by):
    count = lax.axis_size("gx")
    return lax.ppermute(block, "gx", [(i, (i + by) % count) for i in range(count)])


def shape(*dims):
    return jax.ShapeDtypeStruct(dims, F32)


def shards(solution, right_side, alpha, beta_x, beta_y, beta_z):
    args = (solution, right_side, alpha, beta_x, beta_y, beta_z)
    nz = solution.shape[2]
    count = lax.axis_size("gx")
    sent = shape(24, 8, nz)
    own, yh, yl, xl, xh = call(
        pack_body,
        (shape(48, 8, nz),) + (sent,) * 4,
        tuple(pltpu.with_memory_space_constraint(x, pltpu.HBM) for x in args),
        [pltpu.VMEM(x.shape, x.dtype) for x in args] + [pltpu.SemaphoreType.DMA((6,))],
        space=pltpu.HBM,
    )
    yhr, ylr = along_y(yh, 1), along_y(yl, -1)
    xlr, xhr = round_x(xl, -1), round_x(xh, 1)
    xcl, xch = call(corner_body, (shape(len(CORNER), 8, nz),) * 2, (yhr, ylr))
    xclr, xchr = round_x(xcl, -1), round_x(xch, 1)
    c1, c2 = call(
        functools.partial(coarse_body, count),
        (shape(4, 16, nz // 2), shape(16, nz // 4)),
        (own, xhr, yhr),
        [
            pltpu.VMEM((nz // 128, 32, 128), F32),
            pltpu.VMEM((8, nz), F32),
            pltpu.VMEM((4, 24, nz // 2), F32),
            pltpu.VMEM((32, nz // 2), F32),
        ],
    )
    fine, p1 = call(
        functools.partial(fine_body, count),
        (shape(8, 8, nz), shape(5, 16, nz // 2)),
        (own, xlr, xhr, yhr, ylr, xclr, xchr, c1),
        [
            pltpu.VMEM((5, 17, 16, nz), F32),
            pltpu.VMEM((7, 16, 16, nz), F32),
            pltpu.VMEM((18, 16, nz), F32),
            pltpu.VMEM((16, 8, nz), F32),
            pltpu.VMEM((nz // 128, 32, 128), F32),
        ],
        flops=20_000_000,
        nbytes=20_000_000,
    )
    above, below = along_y(p1, -1), along_y(p1, 1)
    here = jnp.stack([above, p1, below])
    left, right = round_x(here, 1), round_x(here, -1)
    middle, p2 = call(
        functools.partial(middle_body, count),
        (shape(4, 4, nz // 2), shape(20, nz // 4)),
        (left, here, right, c2),
        [
            pltpu.VMEM((5, 13, 16, nz // 2), F32),
            pltpu.VMEM((7, 12, 16, nz // 2), F32),
            pltpu.VMEM((14, 16, nz // 2), F32),
            pltpu.VMEM((nz // 256, 16, 128), F32),
        ],
    )
    before, after = round_x(p2, 1), round_x(p2, -1)
    above, below = along_y(p2, -1), along_y(p2, 1)
    down, up = along_y(p2, 2), along_y(p2, -2)
    left = round_x(jnp.stack([below, p2, above, before]), 1)
    right = round_x(jnp.stack([below, p2, above, after]), -1)
    coarse = call(
        functools.partial(coarse_level_body, count),
        shape(2, 2, nz // 4),
        (left, jnp.stack([below, p2, above]), right, down, up),
        [
            pltpu.VMEM((5, 9, 8, nz // 4), F32),
            pltpu.VMEM((7, 8, 8, nz // 4), F32),
            pltpu.VMEM((10, 8, nz // 4), F32),
        ],
    )
    return (fine, middle, coarse)


def solution(mesh):
    placed = P("gx", "gy", None)
    return jax.shard_map(
        shards,
        mesh=mesh,
        in_specs=(placed,) * 6,
        out_specs=(placed,) * 3,
        check_vma=False,
    )
```

```python
import functools

import jax
import jax.numpy as jnp
from jax import lax
from jax.experimental import pallas as pl
from jax.experimental.pallas import tpu as pltpu
from jax.sharding import PartitionSpec as P

F32 = jnp.float32
BF16 = jnp.bfloat16

U, F, A, BX, BY, BZ = range(6)
PAIRS = ((U, F), (A, BY), (BX, BZ))
H = 4


def iota(shape, dim):
    return lax.broadcasted_iota(jnp.int32, shape, dim)


def call(body, outs, args, scratch=(), flops=1_000_000, nbytes=2_000_000, space=pltpu.VMEM, grant=48 << 10):
    vmem = pl.BlockSpec(memory_space=pltpu.VMEM)
    return pl.pallas_call(
        body,
        out_shape=outs,
        in_specs=[pl.BlockSpec(memory_space=space)] * len(args),
        out_specs=jax.tree.map(lambda _: vmem, outs),
        scratch_shapes=list(scratch),
        compiler_params=pltpu.CompilerParams(vmem_limit_bytes=grant << 10),
        cost_estimate=pl.CostEstimate(flops=flops, bytes_accessed=nbytes, transcendentals=0),
    )(*args)


def pair_low(first, second):
    return jnp.where(iota(first.shape, 0) < 4, first, pltpu.roll(second, 4, 0))


def pair_high(first, second):
    return jnp.where(iota(first.shape, 0) >= 4, first, pltpu.roll(second, 4, 0))


def pack_body(u, f, a, bx, by, bz, own, yh, yl, xl, xh, uv, fv, av, bxv, byv, bzv, sems):
    fields = (uv, fv, av, bxv, byv, bzv)
    copies = [pltpu.make_async_copy(src, dst, sems.at[k]) for k, (src, dst) in enumerate(zip((u, f, a, bx, by, bz), fields))]
    for copy in copies:
        copy.start()
    for copy in copies:
        copy.wait()
    cut = bxv[3].astype(F32)
    for k, ref in enumerate(fields):
        for j in range(H):
            low, high = ref[j].astype(F32), ref[4 + j].astype(F32)
            own[k * 8 + j] = low
            own[k * 8 + 4 + j] = high
            if j == 3:
                if k == F:
                    low = low + cut * uv[4]
                elif k == A:
                    low = low + cut
                elif k == BX:
                    low = jnp.zeros_like(low)
            if j == 0:
                if k == F:
                    high = high + cut * uv[3]
                elif k == A:
                    high = high + cut
            xl[k * H + j] = low
            xh[k * H + j] = high
    row = iota(u.shape[1:], 0)
    for p in range(u.shape[0]):
        v = [own[k * 8 + p] for k in range(6)]
        face = v[BY]
        low = list(v)
        low[F] = v[F] + jnp.where(row == 3, face * pltpu.roll(v[U], 7, 0), 0.0)
        low[A] = v[A] + jnp.where(row == 3, face, 0.0)
        low[BY] = jnp.where(row == 3, 0.0, face)
        high = list(v)
        below = pltpu.roll(face, 1, 0)
        high[F] = v[F] + jnp.where(row == 4, below * pltpu.roll(v[U], 1, 0), 0.0)
        high[A] = v[A] + jnp.where(row == 4, below, 0.0)
        for n, (i, j) in enumerate(PAIRS):
            yl[n * 8 + p] = pair_low(low[i], low[j])
            yh[n * 8 + p] = pair_high(high[i], high[j])


def beside(count):
    at = lax.axis_index("gx")
    return [jnp.where(at >= d, 1.0, 0.0) if s < 0 else jnp.where(at < count - d, 1.0, 0.0) for d in (1, 2) for s in (-1, 1)]


CORNER = (
    [(1, (k,)) for k in range(6)]
    + [(2, (U,)), (2, (BY,)), (2, (BX,)), (2, (F, A)), (2, (BZ,))]
    + [(3, (U, BY)), (3, (F, A)), (3, (BX, BZ)), (4, (U, BY)), (4, (BX,))]
)


def nearest(shape):
    row = iota(shape, 0)
    return (row < 2) | (row >= 6)


def halo_rows(k, p, ylr, yhr):
    n, side = next((n, pair.index(k)) for n, pair in enumerate(PAIRS) if k in pair)
    above, below = ylr[n * 8 + p], yhr[n * 8 + p]
    first = iota(above.shape, 0) < 4
    if side:
        return pltpu.roll(jnp.where(first, below, above), 4, 0)
    return jnp.where(first, above, below)


def corner_body(yhr, ylr, xcl, xch):
    near = nearest(ylr.shape[1:])
    for out, plane in ((xcl, lambda d: d - 1), (xch, lambda d: 8 - d)):
        for t, (d, fields) in enumerate(CORNER):
            tile = halo_rows(fields[0], plane(d), ylr, yhr)
            if len(fields) == 2:
                tile = jnp.where(near, tile, pltpu.roll(halo_rows(fields[1], plane(d), ylr, yhr), 4, 0))
            out[t] = tile


def corner_rows(k, d, tiles):
    for t, (distance, fields) in enumerate(CORNER):
        if distance == d and k in fields:
            tile = tiles[t]
            if len(fields) == 1:
                return tile
            if fields[1] == k:
                tile = pltpu.roll(tile, 4, 0)
            return jnp.where(nearest(tile.shape), tile, 0.0)
    return jnp.zeros(tiles.shape[1:], F32)


def halves(n):
    row, col = iota((n, n // 2), 0), iota((n, n // 2), 1)
    both = jnp.where(row // 2 == col, 1.0, 0.0).astype(BF16)
    odd = jnp.where(row == 2 * col + 1, 1.0, 0.0).astype(BF16)
    return both, odd


def exact_dot(x, m):
    n = x.shape[0]
    one = x.astype(BF16)
    rest = x - one.astype(F32)
    two = rest.astype(BF16)
    three = (rest - two.astype(F32)).astype(BF16)
    y = jnp.dot(
        jnp.concatenate([one.astype(F32), two.astype(F32), three.astype(F32)], axis=0).astype(BF16),
        m,
        preferred_element_type=F32,
    )
    return (y[2 * n :] + y[n : 2 * n]) + y[:n]


def put(ref, at, x):
    for g in range(x.shape[1] // 128):
        ref[g, at : at + x.shape[0]] = x[:, 128 * g : 128 * g + 128]


def every_other(ref, first, n, width):
    return jnp.concatenate([ref[g, pl.ds(first, n, 2)] for g in range(width // 128)], axis=1)


def below_z(face):
    return jnp.where(iota(face.shape, face.ndim - 1) == 0, 0.0, pltpu.roll(face, 1, face.ndim - 1))


def coarse_body(count, own, xhr, yhr, c1, c2, rows, edge, fine, small):
    nz = own.shape[2]
    both, odd = halves(nz)
    both2, odd2 = halves(nz // 2)

    def even_odd(n):
        return every_other(rows, 0, n, nz), every_other(rows, 1, n, nz)

    def pairs(k):
        for i in range(4):
            put(rows, 8 * i, own[k * 8 + 2 * i] + own[k * 8 + 2 * i + 1])
        return even_odd(16)

    e, o = pairs(A)
    a_in = e + o
    e, o = pairs(BZ)
    bz_in = e + o
    e, o = pairs(BY)
    by_in = o
    for i in range(4):
        put(rows, 8 * i, own[BX * 8 + 2 * i + 1])
    e, o = even_odd(16)
    bx_in = e + o
    put(rows, 0, xhr[BX * H + 3] * beside(count)[0])
    e, o = even_odd(4)
    edge[0:4] = e + o
    for i in range(4):
        edge[4 + i : 5 + i] = yhr[8 + 2 * i, 3:4] + yhr[8 + 2 * i + 1, 3:4]
    out = exact_dot(jnp.concatenate([a_in, bx_in, by_in, edge[...]], axis=0), both)
    a1, bx1, by1, edges = out[0:16] * 0.125, out[16:32] * 0.25, out[32:48] * 0.25, out[48:56] * 0.25
    bz1 = exact_dot(bz_in, odd) * 0.25
    c1[1] = bx1
    c1[2] = by1
    c1[3] = bz1
    fine[0, 0:8] = edges
    fine[1, 0:4] = edges[0:4]
    fine[1, 4:20] = bx1
    lower_x = fine[1, 0:16]
    fine[2, 1:17] = by1
    lower_y = fine[2, 0:16]
    for i in range(4):
        fine[3, 4 * i : 4 * i + 4] = jnp.broadcast_to(fine[0, 4 + i : 5 + i], (4, nz // 2))
    lower_y = jnp.where(iota(lower_y.shape, 0) % 4 == 0, fine[3, 0:16], lower_y)
    c1[0] = a1 + 0.25 * ((bx1 + lower_x) + (by1 + lower_y) + (bz1 + below_z(bz1)))

    def split(x):
        put(rows, 0, x)
        n = x.shape[0] // 2
        return every_other(rows, 0, n, nz // 2), every_other(rows, 1, n, nz // 2)

    def layers(t):
        small[0:8] = t
        top = small[0:2] + small[2:4]
        bottom = small[4:6] + small[6:8]
        return top, bottom

    e, o = split(a1)
    a_t = layers(e + o)
    e, o = split(bz1)
    bz_t = layers(e + o)
    e, o = split(by1)
    by_t = layers(o)
    e, o = split(bx1)
    small[0:8] = e + o
    bx_t = (small[2:4], small[6:8])
    e, o = split(edges)
    small[0:4] = e + o
    small[8:10] = a_t[0]
    small[10:12] = a_t[1]
    small[12:14] = by_t[0]
    small[14:16] = by_t[1]
    small[16:18] = bx_t[0]
    small[18:20] = bx_t[1]
    small[20:24] = small[0:4]
    small[24:26] = bz_t[0]
    small[26:28] = bz_t[1]
    small[28:32] = small[0:4]
    out = exact_dot(small[8:24], both2)
    out_z = exact_dot(small[24:32], odd2)[0:4] * 0.25
    a2, by2, bx2, edges = out[0:4] * 0.125, out[4:8] * 0.25, out[8:12] * 0.25, out[12:16] * 0.25
    w = nz // 4
    c2[4:8] = bx2
    c2[8:12] = by2
    c2[12:16] = out_z
    small[0:2, 0:w] = edges[0:2]
    small[2:6, 0:w] = bx2
    lower_x = small[0:4, 0:w]
    small[8:12, 0:w] = by2
    small[16:20, 0:w] = edges
    small[24:25, 0:w] = small[18:19, 0:w]
    small[25:26, 0:w] = small[8:9, 0:w]
    small[26:27, 0:w] = small[19:20, 0:w]
    small[27:28, 0:w] = small[10:11, 0:w]
    lower_y = small[24:28, 0:w]
    c2[0:4] = a2 + 0.0625 * ((bx2 + lower_x) + (by2 + lower_y) + (out_z + below_z(out_z)))


def set_weights(weights, w, inverse, source, up_x, low_x, up_y, up_z):
    lane = iota(inverse.shape, 1)
    nz = inverse.shape[1]
    weights[0, w] = source * inverse
    weights[1, w] = up_x * inverse
    weights[2, w] = low_x * inverse
    weights[3, w] = up_y * inverse
    weights[4, w] = pltpu.roll(up_y, 1, 0) * inverse
    weights[5, w] = jnp.where(lane == nz - 1, 0.0, up_z) * inverse
    weights[6, w] = jnp.where(lane == 0, 0.0, pltpu.roll(up_z, 1, 1)) * inverse


def relaxed(weights, held, w):
    here = held[w + 1]
    ny, nz = here.shape
    x = weights[1, w] * held[w + 2] + weights[2, w] * held[w]
    y = weights[3, w] * pltpu.roll(here, ny - 1, 0) + weights[4, w] * pltpu.roll(here, 1, 0)
    z = weights[5, w] * pltpu.roll(here, nz - 1, 1) + weights[6, w] * pltpu.roll(here, 1, 1)
    return ((weights[0, w] + x) + (y + z)), here


def coloured(shape):
    parity = (iota(shape, 0) + iota(shape, 1)) % 2
    return [parity == 0, parity == 1]


def smooth(weights, held, first):
    count = weights.shape[1]
    colours = coloured((weights.shape[2], weights.shape[3]))
    for step in range(first, 4):
        for w in range(step, count - step):
            new, here = relaxed(weights, held, w)
            held[w + 1] = jnp.where(colours[(w + step) % 2], new, here)


def fine_body(count, own, xlr, xhr, yhr, ylr, xclr, xchr, c1, out, p1, win, weights, held, diag, rows):
    nz = own.shape[2]
    lower, upper = beside(count)[:2]

    for w in range(16):
        for k in range(6):
            if w < 4:
                mid, halo, there = xhr[k * H + w], corner_rows(k, 4 - w, xchr), lower
            elif w < 12:
                mid, halo, there = own[k * 8 + w - 4], halo_rows(k, w - 4, ylr, yhr), None
            else:
                mid, halo, there = xlr[k * H + w - 12], corner_rows(k, w - 11, xclr), upper
            if there is not None and k in (U, A, BX):
                mid, halo = mid * there, halo * there
            if k == U:
                held[w + 1, 0:8] = mid
                held[w + 1, 8:16] = halo
            else:
                win[k - 1, w + 1, 0:8] = mid
                win[k - 1, w + 1, 8:16] = halo
    zero = jnp.zeros((16, nz), F32)
    held[0] = zero
    held[17] = zero
    win[BX - 1, 0] = zero

    for w in range(16):
        av, bxv, byv, bzv = win[A - 1, w + 1], win[BX - 1, w + 1], win[BY - 1, w + 1], win[BZ - 1, w + 1]
        low_x = win[BX - 1, w]
        total = av + ((bxv + low_x) + (byv + pltpu.roll(byv, 1, 0)) + (bzv + below_z(bzv)))
        inside = av > 0.0
        inverse = jnp.where(inside, 1.0 / jnp.where(inside, total, 1.0), 0.0)
        set_weights(weights, w, inverse, win[F - 1, w + 1], bxv, low_x, byv, bzv)
        diag[w] = total[0:8]
    smooth(weights, held, 0)
    for i in range(4):
        total = None
        for j in range(2):
            w = 4 + 2 * i + j
            new, here = relaxed(weights, held, w)
            out[w - 4] = here[0:8]
            res = diag[w] * (new[0:8] - here[0:8])
            total = res if total is None else total + res
        put(rows, 8 * i, total)
    both, _ = halves(nz)
    p1[0] = exact_dot(every_other(rows, 0, 16, nz) + every_other(rows, 1, 16, nz), both) * 0.125
    for k in range(4):
        p1[1 + k] = c1[k]


def middle_body(count, left, here, right, c2, out, p2, win, weights, held, rows):
    nz = here.shape[3]
    first = iota((8, nz), 0) < 4
    lower, upper = beside(count)[:2]
    zero = jnp.zeros((16, nz), F32)
    win[2, 0] = zero
    colours = coloured((16, nz))
    for b, (source, there) in enumerate(((left, lower), (here, None), (right, upper))):
        for k in range(5):
            for half in range(2):
                at = slice(8 * half, 8 * half + 8)
                above, mid, below = source[0, k, at], source[1, k, at], source[2, k, at]
                if k == 1 and there is not None:
                    below, mid, above = below * there, mid * there, above * there
                w = 4 * b + 2 * half + 1
                win[k, w, 0:8] = jnp.where(first, mid, pltpu.roll(above, 4, 0))
                win[k, w, 8:16] = jnp.where(first, 0.0, pltpu.roll(below, 4, 0))
                win[k, w + 1, 0:8] = jnp.where(first, pltpu.roll(mid, 4, 0), above)
                win[k, w + 1, 8:16] = jnp.where(first, 0.0, below)
    for w in range(12):
        total = win[1, w + 1]
        inside = total > 0.0
        inverse = jnp.where(inside, 0.25 / jnp.where(inside, total, 1.0), 0.0)
        set_weights(weights, w, inverse, 4.0 * win[0, w + 1], win[2, w + 1], win[2, w], win[3, w + 1], win[4, w + 1])
        held[w + 1] = jnp.where(colours[w % 2], weights[0, w], 0.0)
    held[0] = zero
    held[13] = zero
    smooth(weights, held, 1)
    for i in range(2):
        total = None
        for j in range(2):
            w = 4 + 2 * i + j
            new, now = relaxed(weights, held, w)
            out[w - 4] = now[0:4]
            res = win[1, w + 1, 0:8] * (new[0:8] - now[0:8])
            total = res if total is None else total + res
        put(rows, 8 * i, total)
    both, _ = halves(nz)
    coarse = exact_dot(every_other(rows, 0, 8, nz) + every_other(rows, 1, 8, nz), both) * 0.125
    p2[0:2] = coarse[0:2]
    p2[2:4] = coarse[4:6]
    p2[4:20] = c2[...]


def coarse_level_body(count, left, mid, right, down, up, out, win, weights, held):
    win[...] = jnp.zeros(win.shape, F32)
    near = beside(count)
    for k in range(5):
        factor = near if k == 1 else [1.0] * 4
        win[k, 1, 3:5] = left[3, 4 * k + 2 : 4 * k + 4] * factor[2]
        win[k, 8, 3:5] = right[3, 4 * k : 4 * k + 2] * factor[3]
        for i in range(2):
            at = 4 * k + 2 * i
            win[k, 4 + i, 0:1] = down[at + 1 : at + 2]
            win[k, 4 + i, 7:8] = up[at : at + 1]
            for b, (source, there) in enumerate(((left, factor[0]), (mid, 1.0), (right, factor[1]))):
                for j in range(3):
                    win[k, 2 + 2 * b + i, 1 + 2 * j : 3 + 2 * j] = source[j, at : at + 2] * there
    held[0] = jnp.zeros(held.shape[1:], F32)
    held[9] = jnp.zeros(held.shape[1:], F32)
    colours = coloured(held.shape[1:])
    for w in range(8):
        total = win[1, w + 1]
        inside = total > 0.0
        inverse = jnp.where(inside, 0.0625 / jnp.where(inside, total, 1.0), 0.0)
        set_weights(weights, w, inverse, 16.0 * win[0, w + 1], win[2, w + 1], win[2, w], win[3, w + 1], win[4, w + 1])
        held[w + 1] = jnp.where(colours[w % 2], weights[0, w], 0.0)
    smooth(weights, held, 1)
    for i in range(2):
        out[i] = held[4 + i, 3:5]


def along_y(block, by):
    count = lax.axis_size("gy")
    return lax.ppermute(block, "gy", [(i, i + by) for i in range(count) if 0 <= i + by < count])


def swapped(block, odd):
    count = lax.axis_size("gy")
    firsts = range(int(odd), count - 1, 2)
    return lax.ppermute(block, "gy", [(i, i + 1) for i in firsts] + [(i + 1, i) for i in firsts])


def both_sides(block):
    one, other = swapped(block, False), swapped(block, True)
    first = lax.axis_index("gy") % 2 == 0
    return jnp.where(first, other, one), jnp.where(first, one, other)


def round_x(block, by):
    count = lax.axis_size("gx")
    return lax.ppermute(block, "gx", [(i, (i + by) % count) for i in range(count)])


def shape(*dims):
    return jax.ShapeDtypeStruct(dims, F32)


def shards(solution, right_side, alpha, beta_x, beta_y, beta_z):
    args = (solution, right_side, alpha, beta_x, beta_y, beta_z)
    nz = solution.shape[2]
    count = lax.axis_size("gx")
    sent = shape(24, 8, nz)
    own, yh, yl, xl, xh = call(
        pack_body,
        (shape(48, 8, nz),) + (sent,) * 4,
        tuple(pltpu.with_memory_space_constraint(x, pltpu.HBM) for x in args),
        [pltpu.VMEM(x.shape, x.dtype) for x in args] + [pltpu.SemaphoreType.DMA((6,))],
        space=pltpu.HBM,
    )
    yhr, ylr = along_y(yh, 1), along_y(yl, -1)
    xlr, xhr = round_x(xl, -1), round_x(xh, 1)
    xcl, xch = call(corner_body, (shape(len(CORNER), 8, nz),) * 2, (yhr, ylr))
    xclr, xchr = round_x(xcl, -1), round_x(xch, 1)
    c1, c2 = call(
        functools.partial(coarse_body, count),
        (shape(4, 16, nz // 2), shape(16, nz // 4)),
        (own, xhr, yhr),
        [
            pltpu.VMEM((nz // 128, 32, 128), F32),
            pltpu.VMEM((8, nz), F32),
            pltpu.VMEM((4, 24, nz // 2), F32),
            pltpu.VMEM((32, nz // 2), F32),
        ],
    )
    fine, p1 = call(
        functools.partial(fine_body, count),
        (shape(8, 8, nz), shape(5, 16, nz // 2)),
        (own, xlr, xhr, yhr, ylr, xclr, xchr, c1),
        [
            pltpu.VMEM((5, 17, 16, nz), F32),
            pltpu.VMEM((7, 16, 16, nz), F32),
            pltpu.VMEM((18, 16, nz), F32),
            pltpu.VMEM((16, 8, nz), F32),
            pltpu.VMEM((nz // 128, 32, 128), F32),
        ],
        flops=20_000_000,
        nbytes=20_000_000,
    )
    below, above = both_sides(p1)
    here = jnp.stack([above, p1, below])
    left, right = round_x(here, 1), round_x(here, -1)
    middle, p2 = call(
        functools.partial(middle_body, count),
        (shape(4, 4, nz // 2), shape(20, nz // 4)),
        (left, here, right, c2),
        [
            pltpu.VMEM((5, 13, 16, nz // 2), F32),
            pltpu.VMEM((7, 12, 16, nz // 2), F32),
            pltpu.VMEM((14, 16, nz // 2), F32),
            pltpu.VMEM((nz // 256, 16, 128), F32),
        ],
    )
    before, after = round_x(p2, 1), round_x(p2, -1)
    below, above = both_sides(p2)
    down, up = along_y(p2, 2), along_y(p2, -2)
    left = round_x(jnp.stack([below, p2, above, before]), 1)
    right = round_x(jnp.stack([below, p2, above, after]), -1)
    coarse = call(
        functools.partial(coarse_level_body, count),
        shape(2, 2, nz // 4),
        (left, jnp.stack([below, p2, above]), right, down, up),
        [
            pltpu.VMEM((5, 9, 8, nz // 4), F32),
            pltpu.VMEM((7, 8, 8, nz // 4), F32),
            pltpu.VMEM((10, 8, nz // 4), F32),
        ],
    )
    return (fine, middle, coarse)


def solution(mesh):
    placed = P("gx", "gy", None)
    return jax.shard_map(
        shards,
        mesh=mesh,
        in_specs=(placed,) * 6,
        out_specs=(placed,) * 3,
        check_vma=False,
    )
```

```python
import functools

import jax
import jax.numpy as jnp
from jax import lax
from jax.experimental import pallas as pl
from jax.experimental.pallas import tpu as pltpu
from jax.sharding import PartitionSpec as P

F32 = jnp.float32
BF16 = jnp.bfloat16

U, F, A, BX, BY, BZ = range(6)
PAIRS = ((U, F), (A, BY), (BX, BZ))
H = 4


def iota(shape, dim):
    return lax.broadcasted_iota(jnp.int32, shape, dim)


def call(body, outs, args, scratch=(), flops=1_000_000, nbytes=2_000_000, space=pltpu.VMEM, grant=48 << 10):
    vmem = pl.BlockSpec(memory_space=pltpu.VMEM)
    return pl.pallas_call(
        body,
        out_shape=outs,
        in_specs=[pl.BlockSpec(memory_space=space)] * len(args),
        out_specs=jax.tree.map(lambda _: vmem, outs),
        scratch_shapes=list(scratch),
        compiler_params=pltpu.CompilerParams(vmem_limit_bytes=grant << 10),
        cost_estimate=pl.CostEstimate(flops=flops, bytes_accessed=nbytes, transcendentals=0),
    )(*args)


def pair_low(first, second):
    return jnp.where(iota(first.shape, 0) < 4, first, pltpu.roll(second, 4, 0))


def pair_high(first, second):
    return jnp.where(iota(first.shape, 0) >= 4, first, pltpu.roll(second, 4, 0))


def pack_body(u, f, a, bx, by, bz, own, yh, yl, xl, xh, uv, fv, av, bxv, byv, bzv, sems):
    fields = (uv, fv, av, bxv, byv, bzv)
    copies = [pltpu.make_async_copy(src, dst, sems.at[k]) for k, (src, dst) in enumerate(zip((u, f, a, bx, by, bz), fields))]
    for copy in copies:
        copy.start()
    for copy in copies:
        copy.wait()
    cut = bxv[3].astype(F32)
    for k, ref in enumerate(fields):
        for j in range(H):
            low, high = ref[j].astype(F32), ref[4 + j].astype(F32)
            own[k * 8 + j] = low
            own[k * 8 + 4 + j] = high
            if j == 3:
                if k == F:
                    low = low + cut * uv[4]
                elif k == A:
                    low = low + cut
                elif k == BX:
                    low = jnp.zeros_like(low)
            if j == 0:
                if k == F:
                    high = high + cut * uv[3]
                elif k == A:
                    high = high + cut
            xl[k * H + j] = low
            xh[k * H + j] = high
    row = iota(u.shape[1:], 0)
    for p in range(u.shape[0]):
        v = [own[k * 8 + p] for k in range(6)]
        face = v[BY]
        low = list(v)
        low[F] = v[F] + jnp.where(row == 3, face * pltpu.roll(v[U], 7, 0), 0.0)
        low[A] = v[A] + jnp.where(row == 3, face, 0.0)
        low[BY] = jnp.where(row == 3, 0.0, face)
        high = list(v)
        below = pltpu.roll(face, 1, 0)
        high[F] = v[F] + jnp.where(row == 4, below * pltpu.roll(v[U], 1, 0), 0.0)
        high[A] = v[A] + jnp.where(row == 4, below, 0.0)
        for n, (i, j) in enumerate(PAIRS):
            yl[n * 8 + p] = pair_low(low[i], low[j])
            yh[n * 8 + p] = pair_high(high[i], high[j])


def beside(count):
    at = lax.axis_index("gx")
    return [jnp.where(at >= d, 1.0, 0.0) if s < 0 else jnp.where(at < count - d, 1.0, 0.0) for d in (1, 2) for s in (-1, 1)]


CORNER = (
    [(1, (k,)) for k in range(6)]
    + [(2, (U,)), (2, (BY,)), (2, (BX,)), (2, (F, A)), (2, (BZ,))]
    + [(3, (U, BY)), (3, (F, A)), (3, (BX, BZ)), (4, (U, BY)), (4, (BX,))]
)


def nearest(shape):
    row = iota(shape, 0)
    return (row < 2) | (row >= 6)


def halo_rows(k, p, ylr, yhr):
    n, side = next((n, pair.index(k)) for n, pair in enumerate(PAIRS) if k in pair)
    above, below = ylr[n * 8 + p], yhr[n * 8 + p]
    first = iota(above.shape, 0) < 4
    if side:
        return pltpu.roll(jnp.where(first, below, above), 4, 0)
    return jnp.where(first, above, below)


def corner_body(yhr, ylr, xcl, xch):
    near = nearest(ylr.shape[1:])
    for out, plane in ((xcl, lambda d: d - 1), (xch, lambda d: 8 - d)):
        for t, (d, fields) in enumerate(CORNER):
            tile = halo_rows(fields[0], plane(d), ylr, yhr)
            if len(fields) == 2:
                tile = jnp.where(near, tile, pltpu.roll(halo_rows(fields[1], plane(d), ylr, yhr), 4, 0))
            out[t] = tile


def corner_rows(k, d, tiles):
    for t, (distance, fields) in enumerate(CORNER):
        if distance == d and k in fields:
            tile = tiles[t]
            if len(fields) == 1:
                return tile
            if fields[1] == k:
                tile = pltpu.roll(tile, 4, 0)
            return jnp.where(nearest(tile.shape), tile, 0.0)
    return jnp.zeros(tiles.shape[1:], F32)


def halves(n):
    row, col = iota((n, n // 2), 0), iota((n, n // 2), 1)
    both = jnp.where(row // 2 == col, 1.0, 0.0).astype(BF16)
    odd = jnp.where(row == 2 * col + 1, 1.0, 0.0).astype(BF16)
    return both, odd


def exact_dot(x, m):
    n = x.shape[0]
    one = x.astype(BF16)
    rest = x - one.astype(F32)
    two = rest.astype(BF16)
    three = (rest - two.astype(F32)).astype(BF16)
    y = jnp.dot(
        jnp.concatenate([one.astype(F32), two.astype(F32), three.astype(F32)], axis=0).astype(BF16),
        m,
        preferred_element_type=F32,
    )
    return (y[2 * n :] + y[n : 2 * n]) + y[:n]


def put(ref, at, x):
    for g in range(x.shape[1] // 128):
        ref[g, at : at + x.shape[0]] = x[:, 128 * g : 128 * g + 128]


def every_other(ref, first, n, width):
    return jnp.concatenate([ref[g, pl.ds(first, n, 2)] for g in range(width // 128)], axis=1)


def below_z(face):
    return jnp.where(iota(face.shape, face.ndim - 1) == 0, 0.0, pltpu.roll(face, 1, face.ndim - 1))


def coarse_body(count, own, xhr, yhr, c1, c2, rows, edge, fine, small):
    nz = own.shape[2]
    both, odd = halves(nz)
    both2, odd2 = halves(nz // 2)

    def even_odd(n):
        return every_other(rows, 0, n, nz), every_other(rows, 1, n, nz)

    def pairs(k):
        for i in range(4):
            put(rows, 8 * i, own[k * 8 + 2 * i] + own[k * 8 + 2 * i + 1])
        return even_odd(16)

    e, o = pairs(A)
    a_in = e + o
    e, o = pairs(BZ)
    bz_in = e + o
    e, o = pairs(BY)
    by_in = o
    for i in range(4):
        put(rows, 8 * i, own[BX * 8 + 2 * i + 1])
    e, o = even_odd(16)
    bx_in = e + o
    put(rows, 0, xhr[BX * H + 3] * beside(count)[0])
    e, o = even_odd(4)
    edge[0:4] = e + o
    for i in range(4):
        edge[4 + i : 5 + i] = yhr[8 + 2 * i, 3:4] + yhr[8 + 2 * i + 1, 3:4]
    out = exact_dot(jnp.concatenate([a_in, bx_in, by_in, edge[...]], axis=0), both)
    a1, bx1, by1, edges = out[0:16] * 0.125, out[16:32] * 0.25, out[32:48] * 0.25, out[48:56] * 0.25
    bz1 = exact_dot(bz_in, odd) * 0.25
    c1[1] = bx1
    c1[2] = by1
    c1[3] = bz1
    fine[0, 0:8] = edges
    fine[1, 0:4] = edges[0:4]
    fine[1, 4:20] = bx1
    lower_x = fine[1, 0:16]
    fine[2, 1:17] = by1
    lower_y = fine[2, 0:16]
    for i in range(4):
        fine[3, 4 * i : 4 * i + 4] = jnp.broadcast_to(fine[0, 4 + i : 5 + i], (4, nz // 2))
    lower_y = jnp.where(iota(lower_y.shape, 0) % 4 == 0, fine[3, 0:16], lower_y)
    c1[0] = a1 + 0.25 * ((bx1 + lower_x) + (by1 + lower_y) + (bz1 + below_z(bz1)))

    def split(x):
        put(rows, 0, x)
        n = x.shape[0] // 2
        return every_other(rows, 0, n, nz // 2), every_other(rows, 1, n, nz // 2)

    def layers(t):
        small[0:8] = t
        top = small[0:2] + small[2:4]
        bottom = small[4:6] + small[6:8]
        return top, bottom

    e, o = split(a1)
    a_t = layers(e + o)
    e, o = split(bz1)
    bz_t = layers(e + o)
    e, o = split(by1)
    by_t = layers(o)
    e, o = split(bx1)
    small[0:8] = e + o
    bx_t = (small[2:4], small[6:8])
    e, o = split(edges)
    small[0:4] = e + o
    small[8:10] = a_t[0]
    small[10:12] = a_t[1]
    small[12:14] = by_t[0]
    small[14:16] = by_t[1]
    small[16:18] = bx_t[0]
    small[18:20] = bx_t[1]
    small[20:24] = small[0:4]
    small[24:26] = bz_t[0]
    small[26:28] = bz_t[1]
    small[28:32] = small[0:4]
    out = exact_dot(small[8:24], both2)
    out_z = exact_dot(small[24:32], odd2)[0:4] * 0.25
    a2, by2, bx2, edges = out[0:4] * 0.125, out[4:8] * 0.25, out[8:12] * 0.25, out[12:16] * 0.25
    w = nz // 4
    c2[4:8] = bx2
    c2[8:12] = by2
    c2[12:16] = out_z
    small[0:2, 0:w] = edges[0:2]
    small[2:6, 0:w] = bx2
    lower_x = small[0:4, 0:w]
    small[8:12, 0:w] = by2
    small[16:20, 0:w] = edges
    small[24:25, 0:w] = small[18:19, 0:w]
    small[25:26, 0:w] = small[8:9, 0:w]
    small[26:27, 0:w] = small[19:20, 0:w]
    small[27:28, 0:w] = small[10:11, 0:w]
    lower_y = small[24:28, 0:w]
    c2[0:4] = a2 + 0.0625 * ((bx2 + lower_x) + (by2 + lower_y) + (out_z + below_z(out_z)))


def set_weights(weights, w, inverse, source, up_x, low_x, up_y, up_z):
    lane = iota(inverse.shape, 1)
    nz = inverse.shape[1]
    weights[0, w] = source * inverse
    weights[1, w] = up_x * inverse
    weights[2, w] = low_x * inverse
    weights[3, w] = up_y * inverse
    weights[4, w] = pltpu.roll(up_y, 1, 0) * inverse
    weights[5, w] = jnp.where(lane == nz - 1, 0.0, up_z) * inverse
    weights[6, w] = jnp.where(lane == 0, 0.0, pltpu.roll(up_z, 1, 1)) * inverse


def relaxed(weights, held, w):
    here = held[w + 1]
    ny, nz = here.shape
    x = weights[1, w] * held[w + 2] + weights[2, w] * held[w]
    y = weights[3, w] * pltpu.roll(here, ny - 1, 0) + weights[4, w] * pltpu.roll(here, 1, 0)
    z = weights[5, w] * pltpu.roll(here, nz - 1, 1) + weights[6, w] * pltpu.roll(here, 1, 1)
    return ((weights[0, w] + x) + (y + z)), here


def coloured(shape):
    parity = (iota(shape, 0) + iota(shape, 1)) % 2
    return [parity == 0, parity == 1]


def smooth(weights, held, first):
    count = weights.shape[1]
    colours = coloured((weights.shape[2], weights.shape[3]))
    for step in range(first, 4):
        for w in range(step, count - step):
            new, here = relaxed(weights, held, w)
            held[w + 1] = jnp.where(colours[(w + step) % 2], new, here)


def fine_body(count, own, xlr, xhr, yhr, ylr, xclr, xchr, c1, out, p1, win, weights, held, diag, rows):
    nz = own.shape[2]
    lower, upper = beside(count)[:2]

    for w in range(16):
        for k in range(6):
            if w < 4:
                mid, halo, there = xhr[k * H + w], corner_rows(k, 4 - w, xchr), lower
            elif w < 12:
                mid, halo, there = own[k * 8 + w - 4], halo_rows(k, w - 4, ylr, yhr), None
            else:
                mid, halo, there = xlr[k * H + w - 12], corner_rows(k, w - 11, xclr), upper
            if there is not None and k in (U, A, BX):
                mid, halo = mid * there, halo * there
            if k == U:
                held[w + 1, 0:8] = mid
                held[w + 1, 8:16] = halo
            else:
                win[k - 1, w + 1, 0:8] = mid
                win[k - 1, w + 1, 8:16] = halo
    zero = jnp.zeros((16, nz), F32)
    held[0] = zero
    held[17] = zero
    win[BX - 1, 0] = zero

    for w in range(16):
        av, bxv, byv, bzv = win[A - 1, w + 1], win[BX - 1, w + 1], win[BY - 1, w + 1], win[BZ - 1, w + 1]
        low_x = win[BX - 1, w]
        total = av + ((bxv + low_x) + (byv + pltpu.roll(byv, 1, 0)) + (bzv + below_z(bzv)))
        inside = av > 0.0
        inverse = jnp.where(inside, 1.0 / jnp.where(inside, total, 1.0), 0.0)
        set_weights(weights, w, inverse, win[F - 1, w + 1], bxv, low_x, byv, bzv)
        diag[w] = total[0:8]
    smooth(weights, held, 0)
    for i in range(4):
        total = None
        for j in range(2):
            w = 4 + 2 * i + j
            new, here = relaxed(weights, held, w)
            out[w - 4] = here[0:8]
            res = diag[w] * (new[0:8] - here[0:8])
            total = res if total is None else total + res
        put(rows, 8 * i, total)
    both, _ = halves(nz)
    p1[0] = exact_dot(every_other(rows, 0, 16, nz) + every_other(rows, 1, 16, nz), both) * 0.125
    for k in range(4):
        p1[1 + k] = c1[k]


def middle_body(count, left, here, right, c2, out, p2, win, weights, held, rows):
    nz = here.shape[3]
    first = iota((8, nz), 0) < 4
    lower, upper = beside(count)[:2]
    zero = jnp.zeros((16, nz), F32)
    win[2, 0] = zero
    colours = coloured((16, nz))
    for b, (source, there) in enumerate(((left, lower), (here, None), (right, upper))):
        for k in range(5):
            for half in range(2):
                at = slice(8 * half, 8 * half + 8)
                above, mid, below = source[0, k, at], source[1, k, at], source[2, k, at]
                if k == 1 and there is not None:
                    below, mid, above = below * there, mid * there, above * there
                w = 4 * b + 2 * half + 1
                win[k, w, 0:8] = jnp.where(first, mid, pltpu.roll(above, 4, 0))
                win[k, w, 8:16] = jnp.where(first, 0.0, pltpu.roll(below, 4, 0))
                win[k, w + 1, 0:8] = jnp.where(first, pltpu.roll(mid, 4, 0), above)
                win[k, w + 1, 8:16] = jnp.where(first, 0.0, below)
    for w in range(12):
        total = win[1, w + 1]
        inside = total > 0.0
        inverse = jnp.where(inside, 0.25 / jnp.where(inside, total, 1.0), 0.0)
        set_weights(weights, w, inverse, 4.0 * win[0, w + 1], win[2, w + 1], win[2, w], win[3, w + 1], win[4, w + 1])
        held[w + 1] = jnp.where(colours[w % 2], weights[0, w], 0.0)
    held[0] = zero
    held[13] = zero
    smooth(weights, held, 1)
    for i in range(2):
        total = None
        for j in range(2):
            w = 4 + 2 * i + j
            new, now = relaxed(weights, held, w)
            out[w - 4] = now[0:4]
            res = win[1, w + 1, 0:8] * (new[0:8] - now[0:8])
            total = res if total is None else total + res
        put(rows, 8 * i, total)
    both, _ = halves(nz)
    coarse = exact_dot(every_other(rows, 0, 8, nz) + every_other(rows, 1, 8, nz), both) * 0.125
    p2[0:2] = coarse[0:2]
    p2[2:4] = coarse[4:6]
    p2[4:20] = c2[...]


def coarse_level_body(count, left, mid, right, other, last, out, win, weights, held):
    win[...] = jnp.zeros(win.shape, F32)
    near = beside(count)
    even = jnp.where(lax.axis_index("gy") % 2 == 0, 1.0, 0.0)
    odd = 1.0 - even
    for k in range(5):
        factor = near if k == 1 else [1.0] * 4
        win[k, 1, 3:5] = left[3, 4 * k + 2 : 4 * k + 4] * factor[2]
        win[k, 8, 3:5] = right[3, 4 * k : 4 * k + 2] * factor[3]
        for i in range(2):
            at = 4 * k + 2 * i
            far, passed = other[1, at : at + 2], last[at : at + 2]
            win[k, 4 + i, 0:1] = (far * even + passed * odd)[1:2]
            win[k, 4 + i, 7:8] = (passed * even + far * odd)[0:1]
            for b, (source, there) in enumerate(((left, factor[0]), (mid, 1.0), (right, factor[1]))):
                for j in range(3):
                    win[k, 2 + 2 * b + i, 1 + 2 * j : 3 + 2 * j] = source[j, at : at + 2] * there
    held[0] = jnp.zeros(held.shape[1:], F32)
    held[9] = jnp.zeros(held.shape[1:], F32)
    colours = coloured(held.shape[1:])
    for w in range(8):
        total = win[1, w + 1]
        inside = total > 0.0
        inverse = jnp.where(inside, 0.0625 / jnp.where(inside, total, 1.0), 0.0)
        set_weights(weights, w, inverse, 16.0 * win[0, w + 1], win[2, w + 1], win[2, w], win[3, w + 1], win[4, w + 1])
        held[w + 1] = jnp.where(colours[w % 2], weights[0, w], 0.0)
    smooth(weights, held, 1)
    for i in range(2):
        out[i] = held[4 + i, 3:5]


def along_y(block, by):
    count = lax.axis_size("gy")
    return lax.ppermute(block, "gy", [(i, i + by) for i in range(count) if 0 <= i + by < count])


def swapped(block, odd):
    count = lax.axis_size("gy")
    firsts = range(int(odd), count - 1, 2)
    return lax.ppermute(block, "gy", [(i, i + 1) for i in firsts] + [(i + 1, i) for i in firsts])


def both_sides(block):
    one, other = swapped(block, False), swapped(block, True)
    first = lax.axis_index("gy") % 2 == 0
    return jnp.where(first, other, one), jnp.where(first, one, other)


def round_x(block, by):
    count = lax.axis_size("gx")
    return lax.ppermute(block, "gx", [(i, (i + by) % count) for i in range(count)])


def shape(*dims):
    return jax.ShapeDtypeStruct(dims, F32)


def shards(solution, right_side, alpha, beta_x, beta_y, beta_z):
    args = (solution, right_side, alpha, beta_x, beta_y, beta_z)
    nz = solution.shape[2]
    count = lax.axis_size("gx")
    sent = shape(24, 8, nz)
    own, yh, yl, xl, xh = call(
        pack_body,
        (shape(48, 8, nz),) + (sent,) * 4,
        tuple(pltpu.with_memory_space_constraint(x, pltpu.HBM) for x in args),
        [pltpu.VMEM(x.shape, x.dtype) for x in args] + [pltpu.SemaphoreType.DMA((6,))],
        space=pltpu.HBM,
    )
    yhr, ylr = along_y(yh, 1), along_y(yl, -1)
    xlr, xhr = round_x(xl, -1), round_x(xh, 1)
    xcl, xch = call(corner_body, (shape(len(CORNER), 8, nz),) * 2, (yhr, ylr))
    xclr, xchr = round_x(xcl, -1), round_x(xch, 1)
    c1, c2 = call(
        functools.partial(coarse_body, count),
        (shape(4, 16, nz // 2), shape(16, nz // 4)),
        (own, xhr, yhr),
        [
            pltpu.VMEM((nz // 128, 32, 128), F32),
            pltpu.VMEM((8, nz), F32),
            pltpu.VMEM((4, 24, nz // 2), F32),
            pltpu.VMEM((32, nz // 2), F32),
        ],
    )
    fine, p1 = call(
        functools.partial(fine_body, count),
        (shape(8, 8, nz), shape(5, 16, nz // 2)),
        (own, xlr, xhr, yhr, ylr, xclr, xchr, c1),
        [
            pltpu.VMEM((5, 17, 16, nz), F32),
            pltpu.VMEM((7, 16, 16, nz), F32),
            pltpu.VMEM((18, 16, nz), F32),
            pltpu.VMEM((16, 8, nz), F32),
            pltpu.VMEM((nz // 128, 32, 128), F32),
        ],
        flops=20_000_000,
        nbytes=20_000_000,
    )
    below, above = both_sides(p1)
    here = jnp.stack([above, p1, below])
    left, right = round_x(here, 1), round_x(here, -1)
    middle, p2 = call(
        functools.partial(middle_body, count),
        (shape(4, 4, nz // 2), shape(20, nz // 4)),
        (left, here, right, c2),
        [
            pltpu.VMEM((5, 13, 16, nz // 2), F32),
            pltpu.VMEM((7, 12, 16, nz // 2), F32),
            pltpu.VMEM((14, 16, nz // 2), F32),
            pltpu.VMEM((nz // 256, 16, 128), F32),
        ],
    )
    one = swapped(p2, False)
    before, after = round_x(p2, 1), round_x(p2, -1)
    one, before, after = lax.optimization_barrier((one, before, after))
    other = swapped(jnp.stack([p2, one]), True)
    last = swapped(other[0], False)
    first = lax.axis_index("gy") % 2 == 0
    below, above = jnp.where(first, other[0], one), jnp.where(first, one, other[0])
    left = round_x(jnp.stack([below, p2, above, before]), 1)
    right = round_x(jnp.stack([below, p2, above, after]), -1)
    coarse = call(
        functools.partial(coarse_level_body, count),
        shape(2, 2, nz // 4),
        (left, jnp.stack([below, p2, above]), right, other, last),
        [
            pltpu.VMEM((5, 9, 8, nz // 4), F32),
            pltpu.VMEM((7, 8, 8, nz // 4), F32),
            pltpu.VMEM((10, 8, nz // 4), F32),
        ],
    )
    return (fine, middle, coarse)


def solution(mesh):
    placed = P("gx", "gy", None)
    return jax.shard_map(
        shards,
        mesh=mesh,
        in_specs=(placed,) * 6,
        out_specs=(placed,) * 3,
        check_vma=False,
    )
```

```python
import functools

import jax
import jax.numpy as jnp
from jax import lax
from jax.experimental import pallas as pl
from jax.experimental.pallas import tpu as pltpu
from jax.sharding import PartitionSpec as P

F32 = jnp.float32
BF16 = jnp.bfloat16

U, F, A, BX, BY, BZ = range(6)
PAIRS = ((U, F), (A, BY), (BX, BZ))
H = 4


def iota(shape, dim):
    return lax.broadcasted_iota(jnp.int32, shape, dim)


def call(body, outs, args, scratch=(), flops=1_000_000, nbytes=2_000_000, space=pltpu.VMEM, grant=48 << 10):
    vmem = pl.BlockSpec(memory_space=pltpu.VMEM)
    return pl.pallas_call(
        body,
        out_shape=outs,
        in_specs=[pl.BlockSpec(memory_space=space)] * len(args),
        out_specs=jax.tree.map(lambda _: vmem, outs),
        scratch_shapes=list(scratch),
        compiler_params=pltpu.CompilerParams(vmem_limit_bytes=grant << 10),
        cost_estimate=pl.CostEstimate(flops=flops, bytes_accessed=nbytes, transcendentals=0),
    )(*args)


def pair_low(first, second):
    return jnp.where(iota(first.shape, 0) < 4, first, pltpu.roll(second, 4, 0))


def pair_high(first, second):
    return jnp.where(iota(first.shape, 0) >= 4, first, pltpu.roll(second, 4, 0))


def pack_body(u, f, a, bx, by, bz, own, yh, yl, xl, xh, uv, fv, av, bxv, byv, bzv, sems):
    fields = (uv, fv, av, bxv, byv, bzv)
    copies = [pltpu.make_async_copy(src, dst, sems.at[k]) for k, (src, dst) in enumerate(zip((u, f, a, bx, by, bz), fields))]
    for copy in copies:
        copy.start()
    for copy in copies:
        copy.wait()
    cut = bxv[3].astype(F32)
    for k, ref in enumerate(fields):
        for j in range(H):
            low, high = ref[j].astype(F32), ref[4 + j].astype(F32)
            own[k * 8 + j] = low
            own[k * 8 + 4 + j] = high
            if j == 3:
                if k == F:
                    low = low + cut * uv[4]
                elif k == A:
                    low = low + cut
                elif k == BX:
                    low = jnp.zeros_like(low)
            if j == 0:
                if k == F:
                    high = high + cut * uv[3]
                elif k == A:
                    high = high + cut
            xl[k * H + j] = low
            xh[k * H + j] = high
    row = iota(u.shape[1:], 0)
    for p in range(u.shape[0]):
        v = [own[k * 8 + p] for k in range(6)]
        face = v[BY]
        low = list(v)
        low[F] = v[F] + jnp.where(row == 3, face * pltpu.roll(v[U], 7, 0), 0.0)
        low[A] = v[A] + jnp.where(row == 3, face, 0.0)
        low[BY] = jnp.where(row == 3, 0.0, face)
        high = list(v)
        below = pltpu.roll(face, 1, 0)
        high[F] = v[F] + jnp.where(row == 4, below * pltpu.roll(v[U], 1, 0), 0.0)
        high[A] = v[A] + jnp.where(row == 4, below, 0.0)
        for n, (i, j) in enumerate(PAIRS):
            yl[n * 8 + p] = pair_low(low[i], low[j])
            yh[n * 8 + p] = pair_high(high[i], high[j])


def beside(count):
    at = lax.axis_index("gx")
    return [jnp.where(at >= d, 1.0, 0.0) if s < 0 else jnp.where(at < count - d, 1.0, 0.0) for d in (1, 2) for s in (-1, 1)]


CORNER = (
    [(1, (k,)) for k in range(6)]
    + [(2, (U,)), (2, (BY,)), (2, (BX,)), (2, (F, A)), (2, (BZ,))]
    + [(3, (U, BY)), (3, (F, A)), (3, (BX, BZ)), (4, (U, BY)), (4, (BX,))]
)


def nearest(shape):
    row = iota(shape, 0)
    return (row < 2) | (row >= 6)


def halo_rows(k, p, ylr, yhr):
    n, side = next((n, pair.index(k)) for n, pair in enumerate(PAIRS) if k in pair)
    above, below = ylr[n * 8 + p], yhr[n * 8 + p]
    first = iota(above.shape, 0) < 4
    if side:
        return pltpu.roll(jnp.where(first, below, above), 4, 0)
    return jnp.where(first, above, below)


def corner_body(yhr, ylr, xcl, xch):
    near = nearest(ylr.shape[1:])
    for out, plane in ((xcl, lambda d: d - 1), (xch, lambda d: 8 - d)):
        for t, (d, fields) in enumerate(CORNER):
            tile = halo_rows(fields[0], plane(d), ylr, yhr)
            if len(fields) == 2:
                tile = jnp.where(near, tile, pltpu.roll(halo_rows(fields[1], plane(d), ylr, yhr), 4, 0))
            out[t] = tile


def corner_rows(k, d, tiles):
    for t, (distance, fields) in enumerate(CORNER):
        if distance == d and k in fields:
            tile = tiles[t]
            if len(fields) == 1:
                return tile
            if fields[1] == k:
                tile = pltpu.roll(tile, 4, 0)
            return jnp.where(nearest(tile.shape), tile, 0.0)
    return jnp.zeros(tiles.shape[1:], F32)


def halves(n):
    row, col = iota((n, n // 2), 0), iota((n, n // 2), 1)
    both = jnp.where(row // 2 == col, 1.0, 0.0).astype(BF16)
    odd = jnp.where(row == 2 * col + 1, 1.0, 0.0).astype(BF16)
    return both, odd


def exact_dot(x, m):
    n = x.shape[0]
    one = x.astype(BF16)
    rest = x - one.astype(F32)
    two = rest.astype(BF16)
    three = (rest - two.astype(F32)).astype(BF16)
    y = jnp.dot(
        jnp.concatenate([one.astype(F32), two.astype(F32), three.astype(F32)], axis=0).astype(BF16),
        m,
        preferred_element_type=F32,
    )
    return (y[2 * n :] + y[n : 2 * n]) + y[:n]


def put(ref, at, x):
    for g in range(x.shape[1] // 128):
        ref[g, at : at + x.shape[0]] = x[:, 128 * g : 128 * g + 128]


def every_other(ref, first, n, width):
    return jnp.concatenate([ref[g, pl.ds(first, n, 2)] for g in range(width // 128)], axis=1)


def below_z(face):
    return jnp.where(iota(face.shape, face.ndim - 1) == 0, 0.0, pltpu.roll(face, 1, face.ndim - 1))


def coarse_body(count, own, xhr, yhr, c1, c2, rows, edge, fine, small):
    nz = own.shape[2]
    both, odd = halves(nz)
    both2, odd2 = halves(nz // 2)

    def even_odd(n):
        return every_other(rows, 0, n, nz), every_other(rows, 1, n, nz)

    def pairs(k):
        for i in range(4):
            put(rows, 8 * i, own[k * 8 + 2 * i] + own[k * 8 + 2 * i + 1])
        return even_odd(16)

    e, o = pairs(A)
    a_in = e + o
    e, o = pairs(BZ)
    bz_in = e + o
    e, o = pairs(BY)
    by_in = o
    for i in range(4):
        put(rows, 8 * i, own[BX * 8 + 2 * i + 1])
    e, o = even_odd(16)
    bx_in = e + o
    put(rows, 0, xhr[BX * H + 3] * beside(count)[0])
    e, o = even_odd(4)
    edge[0:4] = e + o
    for i in range(4):
        edge[4 + i : 5 + i] = yhr[8 + 2 * i, 3:4] + yhr[8 + 2 * i + 1, 3:4]
    out = exact_dot(jnp.concatenate([a_in, bx_in, by_in, edge[...]], axis=0), both)
    a1, bx1, by1, edges = out[0:16] * 0.125, out[16:32] * 0.25, out[32:48] * 0.25, out[48:56] * 0.25
    bz1 = exact_dot(bz_in, odd) * 0.25
    c1[1] = bx1
    c1[2] = by1
    c1[3] = bz1
    fine[0, 0:8] = edges
    fine[1, 0:4] = edges[0:4]
    fine[1, 4:20] = bx1
    lower_x = fine[1, 0:16]
    fine[2, 1:17] = by1
    lower_y = fine[2, 0:16]
    for i in range(4):
        fine[3, 4 * i : 4 * i + 4] = jnp.broadcast_to(fine[0, 4 + i : 5 + i], (4, nz // 2))
    lower_y = jnp.where(iota(lower_y.shape, 0) % 4 == 0, fine[3, 0:16], lower_y)
    c1[0] = a1 + 0.25 * ((bx1 + lower_x) + (by1 + lower_y) + (bz1 + below_z(bz1)))

    def split(x):
        put(rows, 0, x)
        n = x.shape[0] // 2
        return every_other(rows, 0, n, nz // 2), every_other(rows, 1, n, nz // 2)

    def layers(t):
        small[0:8] = t
        top = small[0:2] + small[2:4]
        bottom = small[4:6] + small[6:8]
        return top, bottom

    e, o = split(a1)
    a_t = layers(e + o)
    e, o = split(bz1)
    bz_t = layers(e + o)
    e, o = split(by1)
    by_t = layers(o)
    e, o = split(bx1)
    small[0:8] = e + o
    bx_t = (small[2:4], small[6:8])
    e, o = split(edges)
    small[0:4] = e + o
    small[8:10] = a_t[0]
    small[10:12] = a_t[1]
    small[12:14] = by_t[0]
    small[14:16] = by_t[1]
    small[16:18] = bx_t[0]
    small[18:20] = bx_t[1]
    small[20:24] = small[0:4]
    small[24:26] = bz_t[0]
    small[26:28] = bz_t[1]
    small[28:32] = small[0:4]
    out = exact_dot(small[8:24], both2)
    out_z = exact_dot(small[24:32], odd2)[0:4] * 0.25
    a2, by2, bx2, edges = out[0:4] * 0.125, out[4:8] * 0.25, out[8:12] * 0.25, out[12:16] * 0.25
    w = nz // 4
    c2[4:8] = bx2
    c2[8:12] = by2
    c2[12:16] = out_z
    small[0:2, 0:w] = edges[0:2]
    small[2:6, 0:w] = bx2
    lower_x = small[0:4, 0:w]
    small[8:12, 0:w] = by2
    small[16:20, 0:w] = edges
    small[24:25, 0:w] = small[18:19, 0:w]
    small[25:26, 0:w] = small[8:9, 0:w]
    small[26:27, 0:w] = small[19:20, 0:w]
    small[27:28, 0:w] = small[10:11, 0:w]
    lower_y = small[24:28, 0:w]
    c2[0:4] = a2 + 0.0625 * ((bx2 + lower_x) + (by2 + lower_y) + (out_z + below_z(out_z)))


def set_weights(weights, w, inverse, source, up_x, low_x, up_y, up_z):
    lane = iota(inverse.shape, 1)
    nz = inverse.shape[1]
    weights[0, w] = source * inverse
    weights[1, w] = up_x * inverse
    weights[2, w] = low_x * inverse
    weights[3, w] = up_y * inverse
    weights[4, w] = pltpu.roll(up_y, 1, 0) * inverse
    weights[5, w] = jnp.where(lane == nz - 1, 0.0, up_z) * inverse
    weights[6, w] = jnp.where(lane == 0, 0.0, pltpu.roll(up_z, 1, 1)) * inverse


def relaxed(weights, held, w):
    here = held[w + 1]
    ny, nz = here.shape
    x = weights[1, w] * held[w + 2] + weights[2, w] * held[w]
    y = weights[3, w] * pltpu.roll(here, ny - 1, 0) + weights[4, w] * pltpu.roll(here, 1, 0)
    z = weights[5, w] * pltpu.roll(here, nz - 1, 1) + weights[6, w] * pltpu.roll(here, 1, 1)
    return ((weights[0, w] + x) + (y + z)), here


def coloured(shape):
    parity = (iota(shape, 0) + iota(shape, 1)) % 2
    return [parity == 0, parity == 1]


def smooth(weights, held, first):
    count = weights.shape[1]
    colours = coloured((weights.shape[2], weights.shape[3]))
    for step in range(first, 4):
        for w in range(step, count - step):
            new, here = relaxed(weights, held, w)
            held[w + 1] = jnp.where(colours[(w + step) % 2], new, here)


def fine_body(count, own, xlr, xhr, yhr, ylr, xclr, xchr, c1, out, p1, win, weights, held, diag, rows):
    nz = own.shape[2]
    lower, upper = beside(count)[:2]

    for w in range(16):
        for k in range(6):
            if w < 4:
                mid, halo, there = xhr[k * H + w], corner_rows(k, 4 - w, xchr), lower
            elif w < 12:
                mid, halo, there = own[k * 8 + w - 4], halo_rows(k, w - 4, ylr, yhr), None
            else:
                mid, halo, there = xlr[k * H + w - 12], corner_rows(k, w - 11, xclr), upper
            if there is not None and k in (U, A, BX):
                mid, halo = mid * there, halo * there
            if k == U:
                held[w + 1, 0:8] = mid
                held[w + 1, 8:16] = halo
            else:
                win[k - 1, w + 1, 0:8] = mid
                win[k - 1, w + 1, 8:16] = halo
    zero = jnp.zeros((16, nz), F32)
    held[0] = zero
    held[17] = zero
    win[BX - 1, 0] = zero

    for w in range(16):
        av, bxv, byv, bzv = win[A - 1, w + 1], win[BX - 1, w + 1], win[BY - 1, w + 1], win[BZ - 1, w + 1]
        low_x = win[BX - 1, w]
        total = av + ((bxv + low_x) + (byv + pltpu.roll(byv, 1, 0)) + (bzv + below_z(bzv)))
        inside = av > 0.0
        inverse = jnp.where(inside, 1.0 / jnp.where(inside, total, 1.0), 0.0)
        set_weights(weights, w, inverse, win[F - 1, w + 1], bxv, low_x, byv, bzv)
        diag[w] = total[0:8]
    smooth(weights, held, 0)
    for i in range(4):
        total = None
        for j in range(2):
            w = 4 + 2 * i + j
            new, here = relaxed(weights, held, w)
            out[w - 4] = here[0:8]
            res = diag[w] * (new[0:8] - here[0:8])
            total = res if total is None else total + res
        put(rows, 8 * i, total)
    both, _ = halves(nz)
    p1[0] = exact_dot(every_other(rows, 0, 16, nz) + every_other(rows, 1, 16, nz), both) * 0.125
    for k in range(4):
        p1[1 + k] = c1[k]


def middle_body(count, left, here, right, c2, out, p2, win, weights, held, rows):
    nz = here.shape[3]
    first = iota((8, nz), 0) < 4
    lower, upper = beside(count)[:2]
    zero = jnp.zeros((16, nz), F32)
    win[2, 0] = zero
    colours = coloured((16, nz))
    for b, (source, there) in enumerate(((left, lower), (here, None), (right, upper))):
        for k in range(5):
            for half in range(2):
                at = slice(8 * half, 8 * half + 8)
                above, mid, below = source[0, k, at], source[1, k, at], source[2, k, at]
                if k == 1 and there is not None:
                    below, mid, above = below * there, mid * there, above * there
                w = 4 * b + 2 * half + 1
                win[k, w, 0:8] = jnp.where(first, mid, pltpu.roll(above, 4, 0))
                win[k, w, 8:16] = jnp.where(first, 0.0, pltpu.roll(below, 4, 0))
                win[k, w + 1, 0:8] = jnp.where(first, pltpu.roll(mid, 4, 0), above)
                win[k, w + 1, 8:16] = jnp.where(first, 0.0, below)
    for w in range(12):
        total = win[1, w + 1]
        inside = total > 0.0
        inverse = jnp.where(inside, 0.25 / jnp.where(inside, total, 1.0), 0.0)
        set_weights(weights, w, inverse, 4.0 * win[0, w + 1], win[2, w + 1], win[2, w], win[3, w + 1], win[4, w + 1])
        held[w + 1] = jnp.where(colours[w % 2], weights[0, w], 0.0)
    held[0] = zero
    held[13] = zero
    smooth(weights, held, 1)
    for i in range(2):
        total = None
        for j in range(2):
            w = 4 + 2 * i + j
            new, now = relaxed(weights, held, w)
            out[w - 4] = now[0:4]
            res = win[1, w + 1, 0:8] * (new[0:8] - now[0:8])
            total = res if total is None else total + res
        put(rows, 8 * i, total)
    both, _ = halves(nz)
    coarse = exact_dot(every_other(rows, 0, 8, nz) + every_other(rows, 1, 8, nz), both) * 0.125
    p2[0:2] = coarse[0:2]
    p2[2:4] = coarse[4:6]
    p2[4:20] = c2[...]


def coarse_level_body(count, last, left, mid, right, other, out, win, weights, held):
    win[...] = jnp.zeros(win.shape, F32)
    near = beside(count)
    even = jnp.where(lax.axis_index("gy") % 2 == 0, 1.0, 0.0)
    odd = 1.0 - even
    for k in range(5):
        factor = near if k == 1 else [1.0] * 4
        win[k, 1, 3:5] = left[3, 4 * k + 2 : 4 * k + 4] * factor[2]
        win[k, 8, 3:5] = right[3, 4 * k : 4 * k + 2] * factor[3]
        for i in range(2):
            at = 4 * k + 2 * i
            far, passed = other[1, at : at + 2], last[at : at + 2]
            win[k, 4 + i, 0:1] = (far * even + passed * odd)[1:2]
            win[k, 4 + i, 7:8] = (passed * even + far * odd)[0:1]
            for b, (source, there) in enumerate(((left, factor[0]), (mid, 1.0), (right, factor[1]))):
                for j in range(3):
                    win[k, 2 + 2 * b + i, 1 + 2 * j : 3 + 2 * j] = source[j, at : at + 2] * there
    held[0] = jnp.zeros(held.shape[1:], F32)
    held[9] = jnp.zeros(held.shape[1:], F32)
    colours = coloured(held.shape[1:])
    for w in range(8):
        total = win[1, w + 1]
        inside = total > 0.0
        inverse = jnp.where(inside, 0.0625 / jnp.where(inside, total, 1.0), 0.0)
        set_weights(weights, w, inverse, 16.0 * win[0, w + 1], win[2, w + 1], win[2, w], win[3, w + 1], win[4, w + 1])
        held[w + 1] = jnp.where(colours[w % 2], weights[0, w], 0.0)
    smooth(weights, held, 1)
    for i in range(2):
        out[i] = held[4 + i, 3:5]


def along_y(block, by):
    count = lax.axis_size("gy")
    return lax.ppermute(block, "gy", [(i, i + by) for i in range(count) if 0 <= i + by < count])


def swapped(block, odd):
    count = lax.axis_size("gy")
    firsts = range(int(odd), count - 1, 2)
    return lax.ppermute(block, "gy", [(i, i + 1) for i in firsts] + [(i + 1, i) for i in firsts])


def both_sides(block):
    one, other = swapped(block, False), swapped(block, True)
    first = lax.axis_index("gy") % 2 == 0
    return jnp.where(first, other, one), jnp.where(first, one, other)


def round_x(block, by):
    count = lax.axis_size("gx")
    return lax.ppermute(block, "gx", [(i, (i + by) % count) for i in range(count)])


def shape(*dims):
    return jax.ShapeDtypeStruct(dims, F32)


def shards(solution, right_side, alpha, beta_x, beta_y, beta_z):
    args = (solution, right_side, alpha, beta_x, beta_y, beta_z)
    nz = solution.shape[2]
    count = lax.axis_size("gx")
    sent = shape(24, 8, nz)
    own, yh, yl, xl, xh = call(
        pack_body,
        (shape(48, 8, nz),) + (sent,) * 4,
        tuple(pltpu.with_memory_space_constraint(x, pltpu.HBM) for x in args),
        [pltpu.VMEM(x.shape, x.dtype) for x in args] + [pltpu.SemaphoreType.DMA((6,))],
        space=pltpu.HBM,
    )
    yhr, ylr = along_y(yh, 1), along_y(yl, -1)
    xlr, xhr = round_x(xl, -1), round_x(xh, 1)
    xcl, xch = call(corner_body, (shape(len(CORNER), 8, nz),) * 2, (yhr, ylr))
    xclr, xchr = round_x(xcl, -1), round_x(xch, 1)
    c1, c2 = call(
        functools.partial(coarse_body, count),
        (shape(4, 16, nz // 2), shape(16, nz // 4)),
        (own, xhr, yhr),
        [
            pltpu.VMEM((nz // 128, 32, 128), F32),
            pltpu.VMEM((8, nz), F32),
            pltpu.VMEM((4, 24, nz // 2), F32),
            pltpu.VMEM((32, nz // 2), F32),
        ],
    )
    fine, p1 = call(
        functools.partial(fine_body, count),
        (shape(8, 8, nz), shape(5, 16, nz // 2)),
        (own, xlr, xhr, yhr, ylr, xclr, xchr, c1),
        [
            pltpu.VMEM((5, 17, 16, nz), F32),
            pltpu.VMEM((7, 16, 16, nz), F32),
            pltpu.VMEM((18, 16, nz), F32),
            pltpu.VMEM((16, 8, nz), F32),
            pltpu.VMEM((nz // 128, 32, 128), F32),
        ],
        flops=20_000_000,
        nbytes=20_000_000,
    )
    below, above = both_sides(p1)
    here = jnp.stack([above, p1, below])
    left, right = round_x(here, 1), round_x(here, -1)
    middle, p2 = call(
        functools.partial(middle_body, count),
        (shape(4, 4, nz // 2), shape(20, nz // 4)),
        (left, here, right, c2),
        [
            pltpu.VMEM((5, 13, 16, nz // 2), F32),
            pltpu.VMEM((7, 12, 16, nz // 2), F32),
            pltpu.VMEM((14, 16, nz // 2), F32),
            pltpu.VMEM((nz // 256, 16, 128), F32),
        ],
    )
    one = swapped(p2, False)
    before, after = round_x(p2, 1), round_x(p2, -1)
    one, before, after = lax.optimization_barrier((one, before, after))
    other = swapped(jnp.stack([p2, one]), True)
    last = swapped(other[0], False)
    first = lax.axis_index("gy") % 2 == 0
    below, above = jnp.where(first, other[0], one), jnp.where(first, one, other[0])
    left = round_x(jnp.stack([below, p2, above, before]), 1)
    right = round_x(jnp.stack([below, p2, above, after]), -1)
    coarse = call(
        functools.partial(coarse_level_body, count),
        shape(2, 2, nz // 4),
        (last, left, jnp.stack([below, p2, above]), right, other),
        [
            pltpu.VMEM((5, 9, 8, nz // 4), F32),
            pltpu.VMEM((7, 8, 8, nz // 4), F32),
            pltpu.VMEM((10, 8, nz // 4), F32),
        ],
    )
    return (fine, middle, coarse)


def solution(mesh):
    placed = P("gx", "gy", None)
    return jax.shard_map(
        shards,
        mesh=mesh,
        in_specs=(placed,) * 6,
        out_specs=(placed,) * 3,
        check_vma=False,
    )
```
